32 devices in a mesh: dp: 4 (over y, x), row: 8 (over z, core).
Axes of the slice: x: 2, y: 2, z: 4, core: 2. Of those that a mesh axis runs over, the one named last changes fastest.
Arguments:
- frames: bfloat16 [16, 64, 64, 256], P('dp', 'row'), may hold values from -6 to 6
- tokens: bfloat16 [32, 1024, 768], P(('dp', 'row')), may hold values from -6 to 6
- segment_ids: int32 [32, 1024], P(('dp', 'row')), may hold values from 0 to 3, never falling along the last dimension, each value on 1 to 512 neighbouring positions
- clip_frame: int32 [32, 4], P(('dp', 'row')), may hold values from 0 to 3
- filter_weight: bfloat16 [9, 256, 256], replicated, may hold values from -0.125 to 0.125
- filter_bias: float32 [256], replicated, may hold values from -0.5 to 0.5
- context_gain: float32 [256], replicated, may hold values from 0.5 to 1.5
- context_shift: float32 [256], replicated, may hold values from -0.25 to 0.25
- cross_query: bfloat16 [768, 768], replicated, may hold values from -0.21875 to 0.21875
- cross_key: bfloat16 [256, 768], replicated, may hold values from -1.5 to 1.5
- cross_value: bfloat16 [256, 768], replicated, may hold values from -1.5 to 1.5
- cross_output: bfloat16 [768, 768], replicated, may hold values from -0.875 to 0.875
- first_gain: float32 [768], replicated, may hold values from 0.5 to 1.5
- first_shift: float32 [768], replicated, may hold values from -0.625 to 0.625
- self_project: bfloat16 [768, 2304], replicated, may hold values from -0.3125 to 0.3125
- self_output: bfloat16 [768, 768], replicated, may hold values from -0.875 to 0.875
- second_gain: float32 [768], replicated, may hold values from 0.5 to 1.5
- second_shift: float32 [768], replicated, may hold values from -1.75 to 1.75
- up_weight: bfloat16 [768, 3072], replicated, may hold values from -0.21875 to 0.21875
- up_bias: float32 [3072], replicated, may hold values from -3 to 3
- down_weight: bfloat16 [3072, 768], replicated, may hold values from -0.109375 to 0.109375
- cotangent: bfloat16 [32, 1024, 768], P(('dp', 'row')), may hold values from -6 to 6
Outputs:
- middle: float32 [32, 1024, 768], P(('dp', 'row'))
- output: float32 [32, 1024, 768], P(('dp', 'row'))
- tokens_grad: float32 [32, 1024, 768], P(('dp', 'row'))
- frames_grad: float32 [16, 64, 64, 256], P('dp', 'row')
- filter_weight_grad: float32 [9, 256, 256], P(None, None, 'row')
- filter_bias_grad: float32 [256], P('row')
- context_gain_grad: float32 [256], P('row')
- context_shift_grad: float32 [256], P('row')
- cross_query_grad: float32 [768, 768], P(None, 'row')
- cross_key_grad: float32 [256, 768], P(None, 'row')
- cross_value_grad: float32 [256, 768], P(None, 'row')
- cross_output_grad: float32 [768, 768], P(None, 'row')
- first_gain_grad: float32 [768], P('row')
- first_shift_grad: float32 [768], P('row')
- self_project_grad: float32 [768, 2304], P(None, 'row')
- self_output_grad: float32 [768, 768], P(None, 'row')
- second_gain_grad: float32 [768], P('row')
- second_shift_grad: float32 [768], P('row')
- up_weight_grad: float32 [768, 3072], P(None, 'row')
- up_bias_grad: float32 [3072], P('row')
- down_weight_grad: float32 [3072, 768], P(None, 'row')
The draws below stay inside these ranges and needn't reach their ends.
Inputs may be any that keep to these rules, and one draw needn't show every extreme that they name: `segment_ids`: ids never fall along a row; each of the 4 clips of a row holds 1 to 512 tokens, and one clip of every row holds exactly 512. Clip c of token row r reads context frame (r // 8) * 4 + clip_frame[r, c].
All inputs are finite; a program needn't handle non-finite values.
Results may differ from the reference program's by a relative error of at most 0.03.
Values may be sent and summed in bfloat16 or wider, within the bound.
A program may use at most 384 MiB of HBM per device.

```python
import math
import jax
import jax.numpy as jnp
import numpy as np
from jax import lax

D = 768
H = 12
HD = 64
FF = 3072
C = 256
IMG = 64
POOL = 4
CLIPS = 4
SEQ = 1024
FR_DP = 4
KEYS = 256
FRAMES = 16
ROWS = 32
ROWS_GROUP = 8
N_DP = 4


def plant(values, key, least, largest):
    spot = [jax.random.randint(jax.random.fold_in(key, axis), (), 0, length) for axis, length in enumerate(values.shape)]
    widest = values.shape.index(max(values.shape))
    beside = spot[:widest] + [(spot[widest] + 1) % values.shape[widest]] + spot[widest + 1:]
    return values.at[tuple(spot)].set(least).at[tuple(beside)].set(largest)


def level_of(key, shape, cuts, low, largest):
    def one(position, shards_of):
        draws = jax.random.uniform(jax.random.fold_in(jax.random.fold_in(key, 6), position), (shards_of,), jnp.float32, low / len(cuts), largest / len(cuts))
        return jnp.repeat(jnp.exp(draws), shape[position] // shards_of).reshape((-1,) + (1,) * (len(shape) - position - 1))

    loudness = one(*cuts[0])
    for cut in cuts[1:]:
        loudness = loudness * one(*cut)
    return loudness


def split_up(count, total, most, slope):
    loads = [(1 << 20) // math.isqrt(rank ** slope) + 1 for rank in range(2, count + 1)]
    spare, counts = total - most - (count - 1), [1] * (count - 1)
    while spare > 0:
        candidates = [i for i in range(count - 1) if counts[i] < most]
        whole, remaining = sum([loads[i] for i in candidates]), spare
        for i in candidates:
            extra = min(most - counts[i], max(1, remaining * loads[i] // whole), spare)
            counts[i] = counts[i] + extra
            spare = spare - extra
    return np.array([most] + counts)


def ragged_sizes(stream_key, amount, total, bound, skew):
    if amount == 2:
        one = jax.random.randint(stream_key, (), max(1, total - bound), min(bound, total - 1) + 1)
        return jnp.stack([one, total - one])
    lengths = jnp.asarray(split_up(amount, total, bound, skew), jnp.int32)
    pairs = (amount - 1) // 2
    giver, receiver = lengths[1:1 + 2 * pairs:2], lengths[2:2 + 2 * pairs:2]
    slack = jnp.minimum(giver - 1, bound - receiver)
    passed = jax.random.randint(jax.random.fold_in(stream_key, 1), (pairs,), 0, 1 << 20) % (slack + 1)
    lengths = lengths.at[1:1 + 2 * pairs:2].set(giver - passed).at[2:2 + 2 * pairs:2].set(receiver + passed)
    return lengths[jax.random.permutation(jax.random.fold_in(stream_key, 2), amount)]


def bell_draw(key, shape, scale, reach, split=(), kind=jnp.bfloat16):
    level = level_of(key, shape, split, -0.22, 0.18) if split else 1.0
    result = jax.random.normal(key, shape, jnp.float32) * scale * level
    return jnp.minimum(jnp.maximum(result, -reach), reach).astype(kind)


def setup_inputs(seed: int = 0) -> dict:
    streams_of = jax.random.split(jax.random.key(seed), 23)
    return {
        "frames": bell_draw(streams_of[0], (FRAMES, IMG, IMG, C), 1.0, 6.0, ((0, 4), (1, 8))),
        "tokens": bell_draw(streams_of[1], (ROWS, SEQ, D), 1.0, 6.0, ((0, 32),)),
        "segment_ids": jax.vmap(lambda own: jnp.searchsorted(jnp.cumsum(ragged_sizes(own, CLIPS, SEQ, SEQ // 2, 2)), jnp.arange(SEQ), side="right"))(jax.random.split(streams_of[2], ROWS)).reshape((ROWS, SEQ)).astype(jnp.int32),
        "clip_frame": plant(jax.random.randint(streams_of[3], (ROWS, CLIPS), 0, FR_DP), jax.random.fold_in(streams_of[3], 1), 0, FR_DP - 1).astype(jnp.int32),
        "filter_weight": bell_draw(streams_of[4], (9, C, C), (9 * C) ** -0.5, 0.125),
        "filter_bias": bell_draw(streams_of[5], (C,), 0.08, 0.5, (), jnp.float32),
        "context_gain": jnp.clip(1.0 + 0.1 * jax.random.normal(streams_of[6], (C,), jnp.float32), 0.5, 1.5),
        "context_shift": bell_draw(streams_of[7], (C,), 0.04, 0.25, (), jnp.float32),
        "cross_query": bell_draw(streams_of[8], (D, D), D ** -0.5, 0.21875),
        "cross_key": bell_draw(streams_of[9], (C, D), (C // 16) ** -0.5, 1.5),
        "cross_value": bell_draw(streams_of[10], (C, D), (C // 16) ** -0.5, 1.5),
        "cross_output": bell_draw(streams_of[11], (D, D), (D // 16) ** -0.5, 0.875),
        "first_gain": jnp.clip(1.0 + 0.1 * jax.random.normal(streams_of[12], (D,), jnp.float32), 0.5, 1.5),
        "first_shift": bell_draw(streams_of[13], (D,), 0.1, 0.625, (), jnp.float32),
        "self_project": bell_draw(streams_of[14], (D, 3 * D), (D // 2) ** -0.5, 0.3125),
        "self_output": bell_draw(streams_of[15], (D, D), (D // 16) ** -0.5, 0.875),
        "second_gain": jnp.clip(1.0 + 0.1 * jax.random.normal(streams_of[16], (D,), jnp.float32), 0.5, 1.5),
        "second_shift": bell_draw(streams_of[17], (D,), 0.3, 1.75, (), jnp.float32),
        "up_weight": bell_draw(streams_of[18], (D, FF), D ** -0.5, 0.21875),
        "up_bias": bell_draw(streams_of[19], (FF,), 0.5, 3.0, (), jnp.float32),
        "down_weight": bell_draw(streams_of[20], (FF, D), FF ** -0.5, 0.109375),
        "cotangent": bell_draw(streams_of[21], (ROWS, SEQ, D), 1.0, 6.0, ((0, 32),)),
    }


@jax.custom_vjp
def low(v):
    return lax.optimization_barrier(v.astype(jnp.bfloat16)).astype(jnp.float32)

@jax.custom_vjp
def low_back(v):
    return v

def low_keep(v):
    return (low(v), None)

def low_pass(kept, grad):
    return (grad,)

def back_keep(v):
    return (v, None)

def back_low(kept, grad):
    return (low(grad),)
low.defvjp(low_keep, low_pass)
low_back.defvjp(back_keep, back_low)
epsilon = 1e-05
negative = -1e+30

def exact_dot(left, right):
    return jnp.dot(left, right, precision=lax.Precision.HIGHEST, preferred_element_type=jnp.float32)

def layer_norm(values, gain, shift):
    average = lax.optimization_barrier(jnp.mean(values, -1, keepdims=True))
    centred = values - average
    variance = lax.optimization_barrier(jnp.mean(centred * centred, -1, keepdims=True))
    return centred * lax.rsqrt(variance + epsilon) * gain + shift

def convolve(frames, filter_weight, filter_bias):
    padded = jnp.pad(frames, ((0, 0), (1, 1), (1, 1), (0, 0)))
    summed = filter_bias
    for kernel_tap in range(9):
        row_shift = kernel_tap // 3
        col_shift = kernel_tap % 3
        window = padded[:, row_shift:row_shift + IMG, col_shift:col_shift + IMG, :]
        summed = summed + jnp.einsum('fyxc,cd->fyxd', window, filter_weight[kernel_tap], precision=lax.Precision.HIGHEST)
    return summed

def attention(queries, key_rows, value_rows, allowed):
    score_scale = 1.0 / math.sqrt(HD)
    query_heads = queries.reshape(queries.shape[0], H, HD)
    key_heads = key_rows.reshape(key_rows.shape[0], H, HD)
    value_heads = value_rows.reshape(value_rows.shape[0], H, HD)
    scores = low_back(jnp.einsum('qhd,khd->hqk', query_heads, key_heads, precision=lax.Precision.HIGHEST) * score_scale)
    scores = jnp.where(allowed[None], scores, negative)
    highest = lax.optimization_barrier(jnp.max(scores, -1, keepdims=True))
    weights_exp = jnp.exp(scores - highest)
    softmax_probs = low(weights_exp / lax.optimization_barrier(jnp.sum(weights_exp, -1, keepdims=True)))
    attended = jnp.einsum('hqk,khd->qhd', softmax_probs, value_heads, precision=lax.Precision.HIGHEST)
    return low(low_back(attended.reshape(queries.shape[0], D)))

def context_features(frames, filter_weight, filter_bias, context_gain, context_shift, cross_key, cross_value):
    pre_act = low_back(convolve(frames, filter_weight, filter_bias))
    normed = layer_norm(jax.nn.gelu(pre_act), context_gain, context_shift)
    pooled = lax.optimization_barrier(jnp.mean(normed.reshape(FRAMES, IMG // POOL, POOL, IMG // POOL, POOL, C), axis=(2, 4)))
    pooled = low(pooled.reshape(FRAMES, KEYS, C))
    key_rows = low(jnp.einsum('fkc,cd->fkd', pooled, cross_key, precision=lax.Precision.HIGHEST))
    value_rows = low(jnp.einsum('fkc,cd->fkd', pooled, cross_value, precision=lax.Precision.HIGHEST))
    return (key_rows, value_rows)

def row_forward(row_tokens, row_segments, row_clips, keys_group, values_group, weights):
    cross_query, cross_output, first_gain, first_shift, self_project, self_output, second_gain, second_shift, up_weight, up_bias, down_weight = weights
    clip_range = jnp.arange(CLIPS, dtype=jnp.int32)
    frame_ids = lax.optimization_barrier(jnp.sum(jnp.where(row_segments[:, None] == clip_range[None, :], row_clips[None, :], 0), axis=1)).astype(jnp.int32)
    key_frames = jnp.arange(FR_DP * KEYS, dtype=jnp.int32) // KEYS
    queries = low(low_back(exact_dot(row_tokens, cross_query)))
    attended = attention(queries, keys_group, values_group, frame_ids[:, None] == key_frames[None, :])
    middle = row_tokens + low_back(exact_dot(attended, cross_output))
    first_normed = low(layer_norm(middle, first_gain, first_shift))
    packed = low(low_back(exact_dot(first_normed, self_project)))
    positions = jnp.arange(SEQ, dtype=jnp.int32)
    allowed = (positions[:, None] >= positions[None, :]) & (row_segments[:, None] == row_segments[None, :])
    attended = attention(packed[:, :D], packed[:, D:2 * D], packed[:, 2 * D:], allowed)
    second_mid = middle + low_back(exact_dot(attended, self_output))
    second_normed = low(layer_norm(second_mid, second_gain, second_shift))
    hidden_pre = low_back(exact_dot(second_normed, up_weight) + up_bias)
    hidden = low(jax.nn.gelu(hidden_pre))
    output = second_mid + exact_dot(hidden, down_weight)
    return (middle, output)

def forward(frames, tokens, front_weights, block_weights, segment_ids, clip_frame):
    key_rows, value_rows = context_features(frames, *front_weights[:6])
    cross_query, cross_output = (front_weights[6], front_weights[7])
    weights = (cross_query, cross_output) + tuple(block_weights)
    keys_grouped = key_rows.reshape(N_DP, FR_DP * KEYS, D)
    values_grouped = value_rows.reshape(N_DP, FR_DP * KEYS, D)
    checked_row = jax.checkpoint(row_forward)

    def step(running, inputs):
        row_tokens, row_segments, row_clips, row_index = inputs
        group_index = row_index // ROWS_GROUP
        keys_group = lax.dynamic_index_in_dim(keys_grouped, group_index, 0, keepdims=False)
        values_group = lax.dynamic_index_in_dim(values_grouped, group_index, 0, keepdims=False)
        return (running, checked_row(row_tokens, row_segments, row_clips, keys_group, values_group, weights))
    row_numbers = jnp.arange(ROWS, dtype=jnp.int32)
    _, (middle, output) = lax.scan(step, jnp.zeros((), jnp.float32), (tokens, segment_ids, clip_frame, row_numbers))
    return (middle, output)

def reference(frames, tokens, segment_ids, clip_frame, filter_weight, filter_bias, context_gain, context_shift, cross_query, cross_key, cross_value, cross_output, first_gain, first_shift, self_project, self_output, second_gain, second_shift, up_weight, up_bias, down_weight, cotangent):
    front = (filter_weight, filter_bias, context_gain, context_shift, cross_key, cross_value, cross_query, cross_output)
    block = (first_gain, first_shift, self_project, self_output, second_gain, second_shift, up_weight, up_bias, down_weight)
    front = tuple((item.astype(jnp.float32) for item in front))
    block = tuple((item.astype(jnp.float32) for item in block))

    def wrapped(frames_in, tokens_in, front_in, block_in):
        return forward(frames_in, tokens_in, front_in, block_in, segment_ids, clip_frame)
    (middle, output), pullback = jax.vjp(wrapped, frames.astype(jnp.float32), tokens.astype(jnp.float32), front, block)
    frames_grad, tokens_grad, front_grad, block_grad = pullback((jnp.zeros_like(middle), cotangent.astype(jnp.float32)))
    return (middle, output, tokens_grad, frames_grad, front_grad[0], front_grad[1], front_grad[2], front_grad[3], front_grad[6], front_grad[4], front_grad[5], front_grad[7], block_grad[0], block_grad[1], block_grad[2], block_grad[3], block_grad[4], block_grad[5], block_grad[6], block_grad[7], block_grad[8])
```

```python
import functools
import math
import jax
import jax.numpy as jnp
from jax import lax
from jax.experimental import pallas as pl
from jax.experimental.pallas import tpu as pltpu
from jax.sharding import PartitionSpec as P

D = 768
HD = 64
PAIR = 128
BLOCK = 256
KEYS = 256
CLIPS = 4
FAR = 2.0**100
SCALE = 0.125
f32 = jnp.float32
bf16 = jnp.bfloat16
VMEM_ASK = 48 * 2**20


def lane_of(rows):
    return lax.broadcasted_iota(jnp.int32, (rows, PAIR), 1)


def dot_nt(left, right):
    return lax.dot_general(left, right, (((1,), (1,)), ((), ())), preferred_element_type=f32)


def dot_nn(left, right):
    return lax.dot_general(left, right, (((1,), (0,)), ((), ())), preferred_element_type=f32)


def three_terms(value):
    high = value.astype(bf16).astype(f32)
    rest = value - high
    middle = rest.astype(bf16).astype(f32)
    return high, middle, rest - middle


def tagged(extra, value, half):
    high, middle, low = three_terms(value)
    extra = jnp.where(half == 8, -high, extra)
    extra = jnp.where(half == 9, -middle, extra)
    return jnp.where(half == 10, -low, extra)


def segment_tags(segment_row):
    lane = jnp.arange(PAIR, dtype=jnp.int32) % HD
    wrong = (lane[None, :] < CLIPS) & (lane[None, :] != segment_row[:, None])
    return jnp.where(wrong, -FAR, 0.0).astype(bf16)


def key_tags(segment_row):
    lane = jnp.arange(PAIR, dtype=jnp.int32) % HD
    ones = (lane[None, :] == segment_row[:, None]) | ((lane[None, :] >= 8) & (lane[None, :] <= 10))
    return jnp.where(ones, 1.0, 0.0).astype(bf16)


def clip_key_tags(rows, clip):
    half = lane_of(rows) % HD
    return jnp.where((half == clip) | ((half >= 8) & (half <= 10)), 1.0, 0.0).astype(bf16)


def cross_forward_kernel(
    seg_ref, frame_ref, q_ref, pooled_ref, key_w_ref, value_w_ref, tag_ref, col_ref,
    out_ref, extra_ref, keys_s, values_s,
):
    keys_s[...] = dot_nn(pooled_ref[...], key_w_ref[...]).astype(bf16)
    values_s[...] = dot_nn(pooled_ref[...], value_w_ref[...]).astype(bf16)
    left = lane_of(BLOCK) < HD
    half = lane_of(BLOCK) % HD
    for block in range(q_ref.shape[0] // BLOCK):
        rows = pl.ds(block * BLOCK, BLOCK)
        query = (q_ref[rows, :].astype(f32) * SCALE).astype(bf16)
        tags = tag_ref[rows, :]
        query_a = jnp.where(left, query, tags)
        query_b = jnp.where(left, tags, query)

        def one_clip(clip, carry, rows=rows, query_a=query_a, query_b=query_b, tags=tags):
            own = pl.ds(pl.multiple_of(frame_ref[clip] * KEYS, KEYS), KEYS)
            key = keys_s[own, :]
            value = values_s[own, :]
            key_tag = clip_key_tags(KEYS, clip)
            one = jnp.ones_like(value)
            score_a = dot_nt(query_a, jnp.where(left, key, key_tag))
            score_b = dot_nt(query_b, jnp.where(left, key_tag, key))
            top_a = jnp.max(score_a, -1, keepdims=True)
            top_b = jnp.max(score_b, -1, keepdims=True)
            exp_a = jnp.exp(score_a - top_a).astype(bf16)
            exp_b = jnp.exp(score_b - top_b).astype(bf16)
            mix_a = dot_nn(exp_a, jnp.where(left, value, one))
            mix_b = dot_nn(exp_b, jnp.where(left, one, value))
            total = jnp.where(left, mix_b, mix_a)
            mixed = jnp.where(left, mix_a, mix_b) / pltpu.roll(total, HD, 1)
            log_sum = jnp.where(left, top_b, top_a) + jnp.log(total)
            extra = tagged(tags.astype(f32), log_sum, half)
            mine = col_ref[rows, :] == clip
            out_ref[rows, :] = jnp.where(mine, mixed, out_ref[rows, :].astype(f32)).astype(bf16)
            extra_ref[rows, :] = jnp.where(mine, extra, extra_ref[rows, :].astype(f32)).astype(bf16)
            return carry

        lax.fori_loop(seg_ref[block * BLOCK], seg_ref[block * BLOCK + BLOCK - 1] + 1, one_clip, 0)


def pair_spec(rows):
    return pl.BlockSpec((rows, PAIR), lambda p, *_: (0, p))


def whole_spec(shape):
    return pl.BlockSpec(shape, lambda p, *_: (0,) * len(shape))


def cross_forward(segments, frames, queries, pooled, key_w, value_w, tags):
    rows = queries.shape[0]
    return pl.pallas_call(
        cross_forward_kernel,
        out_shape=(
            jax.ShapeDtypeStruct((rows, D), bf16),
            jax.ShapeDtypeStruct((rows, D), bf16),
        ),
        grid_spec=pltpu.PrefetchScalarGridSpec(
            num_scalar_prefetch=2,
            grid=(D // PAIR,),
            in_specs=[
                pair_spec(rows),
                whole_spec(pooled.shape),
                pair_spec(key_w.shape[0]),
                pair_spec(key_w.shape[0]),
                whole_spec((rows, PAIR)),
                whole_spec((rows, 1)),
            ],
            out_specs=[pair_spec(rows), pair_spec(rows)],
            scratch_shapes=[
                pltpu.VMEM((pooled.shape[0], PAIR), bf16),
                pltpu.VMEM((pooled.shape[0], PAIR), bf16),
            ],
        ),
        compiler_params=pltpu.CompilerParams(vmem_limit_bytes=VMEM_ASK),
        cost_estimate=pl.CostEstimate(
            flops=12_000_000_000, bytes_accessed=8_000_000, transcendentals=4_000_000
        ),
        name="cross_forward",
    )(segments, frames, queries, pooled, key_w, value_w, tags, segments[:, None])


def self_forward_kernel(
    first_ref, q_ref, k_ref, v_ref, tag_ref, key_tag_ref,
    out_ref, extra_ref, mix_a_s, mix_b_s, top_s,
):
    left = lane_of(BLOCK) < HD
    half = lane_of(BLOCK) % HD
    row_at = lax.broadcasted_iota(jnp.int32, (BLOCK, BLOCK), 0)
    col_at = lax.broadcasted_iota(jnp.int32, (BLOCK, BLOCK), 1)
    for block in range(q_ref.shape[0] // BLOCK):
        rows = pl.ds(block * BLOCK, BLOCK)
        query = (q_ref[rows, :].astype(f32) * SCALE).astype(bf16)
        tags = tag_ref[rows, :]
        query_a = jnp.where(left, query, tags)
        query_b = jnp.where(left, tags, query)

        def scores(own, query_a=query_a, query_b=query_b):
            key = k_ref[own, :]
            value = v_ref[own, :]
            key_tag = key_tag_ref[own, :]
            one = jnp.ones_like(value)
            score_a = dot_nt(query_a, jnp.where(left, key, key_tag))
            score_b = dot_nt(query_b, jnp.where(left, key_tag, key))
            return score_a, score_b, jnp.where(left, value, one), jnp.where(left, one, value)

        score_a, score_b, value_a, value_b = scores(rows)
        score_a = jnp.where(row_at >= col_at, score_a, -FAR)
        score_b = jnp.where(row_at >= col_at, score_b, -FAR)
        top_a = jnp.max(score_a, -1, keepdims=True)
        top_b = jnp.max(score_b, -1, keepdims=True)
        mix_a_s[...] = dot_nn(jnp.exp(score_a - top_a).astype(bf16), value_a)
        mix_b_s[...] = dot_nn(jnp.exp(score_b - top_b).astype(bf16), value_b)
        top_s[...] = jnp.where(left, top_a, top_b)

        if block:

            def one_block(other, carry, scores=scores):
                own = pl.ds(pl.multiple_of(other * BLOCK, BLOCK), BLOCK)
                score_a, score_b, value_a, value_b = scores(own)
                old_a = top_s[:, 0:1]
                old_b = top_s[:, HD : HD + 1]
                top_a = jnp.maximum(old_a, jnp.max(score_a, -1, keepdims=True))
                top_b = jnp.maximum(old_b, jnp.max(score_b, -1, keepdims=True))
                mix_a_s[...] = mix_a_s[...] * jnp.exp(old_a - top_a) + dot_nn(
                    jnp.exp(score_a - top_a).astype(bf16), value_a
                )
                mix_b_s[...] = mix_b_s[...] * jnp.exp(old_b - top_b) + dot_nn(
                    jnp.exp(score_b - top_b).astype(bf16), value_b
                )
                top_s[...] = jnp.where(left, top_a, top_b)
                return carry

            lax.fori_loop(first_ref[block], block, one_block, 0)

        total = jnp.where(left, mix_b_s[...], mix_a_s[...])
        mixed = jnp.where(left, mix_a_s[...], mix_b_s[...]) / pltpu.roll(total, HD, 1)
        log_sum = pltpu.roll(top_s[...], HD, 1) + jnp.log(total)
        out_ref[rows, :] = mixed.astype(bf16)
        extra_ref[rows, :] = tagged(tags.astype(f32), log_sum, half).astype(bf16)


def self_forward(first_blocks, packed, tags, key_tag):
    rows = packed.shape[0]
    pairs = D // PAIR
    shifted = lambda by: pl.BlockSpec((rows, PAIR), lambda p, *_: (0, p + by))
    return pl.pallas_call(
        self_forward_kernel,
        out_shape=(
            jax.ShapeDtypeStruct((rows, D), bf16),
            jax.ShapeDtypeStruct((rows, D), bf16),
        ),
        grid_spec=pltpu.PrefetchScalarGridSpec(
            num_scalar_prefetch=1,
            grid=(pairs,),
            in_specs=[
                shifted(0), shifted(pairs), shifted(2 * pairs),
                whole_spec((rows, PAIR)), whole_spec((rows, PAIR)),
            ],
            out_specs=[pair_spec(rows), pair_spec(rows)],
            scratch_shapes=[pltpu.VMEM((BLOCK, PAIR), f32)] * 3,
        ),
        compiler_params=pltpu.CompilerParams(vmem_limit_bytes=VMEM_ASK),
        cost_estimate=pl.CostEstimate(
            flops=12_000_000_000, bytes_accessed=8_000_000, transcendentals=4_000_000
        ),
        name="self_forward",
    )(first_blocks, packed, packed, packed, tags, key_tag)


def grad_rows(mixed, grad, left, half):
    product = mixed.astype(f32) * grad.astype(f32)
    dot_a = jnp.sum(jnp.where(left, product, 0.0), -1, keepdims=True)
    dot_b = jnp.sum(jnp.where(left, 0.0, product), -1, keepdims=True)
    extra = tagged(jnp.zeros_like(product), jnp.where(left, dot_b, dot_a), half).astype(bf16)
    return jnp.where(left, grad, extra), jnp.where(left, extra, grad)


def back_products(query_a, query_b, grad_a, grad_b, key, value, key_tag, left, masked=None):
    key_a = jnp.where(left, key, key_tag)
    key_b = jnp.where(left, key_tag, key)
    score_a = dot_nt(query_a, key_a)
    score_b = dot_nt(query_b, key_b)
    if masked is not None:
        score_a = jnp.where(masked, score_a, -FAR)
        score_b = jnp.where(masked, score_b, -FAR)
    prob_a = jnp.exp(score_a)
    prob_b = jnp.exp(score_b)
    back_a = (prob_a * dot_nt(grad_a, jnp.where(left, value, key_tag))).astype(bf16)
    back_b = (prob_b * dot_nt(grad_b, jnp.where(left, key_tag, value))).astype(bf16)
    query_grad = jnp.where(left, dot_nn(back_a, key_a), dot_nn(back_b, key_b))
    return prob_a.astype(bf16), prob_b.astype(bf16), back_a, back_b, query_grad


def cross_backward_kernel(
    seg_ref, frame_ref, q_ref, pooled_ref, key_w_ref, value_w_ref, extra_ref, mixed_ref, grad_ref,
    dq_ref, dk_ref, dv_ref, keys_s, values_s, dk_s, dv_s, dq_s,
):
    keys_s[...] = dot_nn(pooled_ref[...], key_w_ref[...]).astype(bf16)
    values_s[...] = dot_nn(pooled_ref[...], value_w_ref[...]).astype(bf16)
    dk_s[...] = jnp.zeros_like(dk_s)
    dv_s[...] = jnp.zeros_like(dv_s)
    left = lane_of(BLOCK) < HD
    half = lane_of(BLOCK) % HD
    for block in range(q_ref.shape[0] // BLOCK):
        rows = pl.ds(block * BLOCK, BLOCK)
        query = (q_ref[rows, :].astype(f32) * SCALE).astype(bf16)
        extra = extra_ref[rows, :]
        grad = grad_ref[rows, :]
        query_a = jnp.where(left, query, extra)
        query_b = jnp.where(left, extra, query)
        grad_a, grad_b = grad_rows(mixed_ref[rows, :], grad, left, half)
        query_t = query.T
        grad_t = grad.T
        dq_s[...] = jnp.zeros_like(dq_s)

        def one_clip(clip, carry, query_a=query_a, query_b=query_b, grad_a=grad_a, grad_b=grad_b,
                     query_t=query_t, grad_t=grad_t):
            own = pl.ds(pl.multiple_of(frame_ref[clip] * KEYS, KEYS), KEYS)
            prob_a, prob_b, back_a, back_b, query_grad = back_products(
                query_a, query_b, grad_a, grad_b, keys_s[own, :], values_s[own, :],
                clip_key_tags(KEYS, clip), left,
            )
            dq_s[...] += query_grad
            dk_s[0:HD, own] += dot_nn(query_t[0:HD], back_a)
            dk_s[HD:PAIR, own] += dot_nn(query_t[HD:PAIR], back_b)
            dv_s[0:HD, own] += dot_nn(grad_t[0:HD], prob_a)
            dv_s[HD:PAIR, own] += dot_nn(grad_t[HD:PAIR], prob_b)
            return carry

        lax.fori_loop(seg_ref[block * BLOCK], seg_ref[block * BLOCK + BLOCK - 1] + 1, one_clip, 0)
        dq_ref[rows, :] = (dq_s[...] * SCALE).astype(bf16)
    dk_ref[...] = dk_s[...].astype(bf16)
    dv_ref[...] = dv_s[...].astype(bf16)


def cross_backward(segments, frames, queries, pooled, key_w, value_w, extra, mixed, grad):
    rows = queries.shape[0]
    keys = pooled.shape[0]
    upright = pl.BlockSpec((PAIR, keys), lambda p, *_: (p, 0))
    return pl.pallas_call(
        cross_backward_kernel,
        out_shape=(
            jax.ShapeDtypeStruct((rows, D), bf16),
            jax.ShapeDtypeStruct((D, keys), bf16),
            jax.ShapeDtypeStruct((D, keys), bf16),
        ),
        grid_spec=pltpu.PrefetchScalarGridSpec(
            num_scalar_prefetch=2,
            grid=(D // PAIR,),
            in_specs=[
                pair_spec(rows),
                whole_spec(pooled.shape),
                pair_spec(key_w.shape[0]),
                pair_spec(key_w.shape[0]),
                pair_spec(rows), pair_spec(rows), pair_spec(rows),
            ],
            out_specs=[pair_spec(rows), upright, upright],
            scratch_shapes=[
                pltpu.VMEM((keys, PAIR), bf16),
                pltpu.VMEM((keys, PAIR), bf16),
                pltpu.VMEM((PAIR, keys), f32),
                pltpu.VMEM((PAIR, keys), f32),
                pltpu.VMEM((BLOCK, PAIR), f32),
            ],
        ),
        compiler_params=pltpu.CompilerParams(vmem_limit_bytes=VMEM_ASK),
        cost_estimate=pl.CostEstimate(
            flops=24_000_000_000, bytes_accessed=16_000_000, transcendentals=4_000_000
        ),
        name="cross_backward",
    )(segments, frames, queries, pooled, key_w, value_w, extra, mixed, grad)


def self_backward_kernel(
    first_ref, q_ref, k_ref, v_ref, key_tag_ref, extra_ref, mixed_ref, grad_ref,
    dq_ref, dk_ref, dv_ref, dk_s, dv_s, dq_s,
):
    dk_s[...] = jnp.zeros_like(dk_s)
    dv_s[...] = jnp.zeros_like(dv_s)
    left = lane_of(BLOCK) < HD
    half = lane_of(BLOCK) % HD
    row_at = lax.broadcasted_iota(jnp.int32, (BLOCK, BLOCK), 0)
    col_at = lax.broadcasted_iota(jnp.int32, (BLOCK, BLOCK), 1)
    for block in range(q_ref.shape[0] // BLOCK):
        rows = pl.ds(block * BLOCK, BLOCK)
        query = (q_ref[rows, :].astype(f32) * SCALE).astype(bf16)
        extra = extra_ref[rows, :]
        grad = grad_ref[rows, :]
        query_a = jnp.where(left, query, extra)
        query_b = jnp.where(left, extra, query)
        grad_a, grad_b = grad_rows(mixed_ref[rows, :], grad, left, half)
        query_t = query.T
        grad_t = grad.T

        def one_block(own, masked=None, query_a=query_a, query_b=query_b, grad_a=grad_a,
                      grad_b=grad_b, query_t=query_t, grad_t=grad_t):
            prob_a, prob_b, back_a, back_b, query_grad = back_products(
                query_a, query_b, grad_a, grad_b, k_ref[own, :], v_ref[own, :],
                key_tag_ref[own, :], left, masked,
            )
            dk_s[0:HD, own] += dot_nn(query_t[0:HD], back_a)
            dk_s[HD:PAIR, own] += dot_nn(query_t[HD:PAIR], back_b)
            dv_s[0:HD, own] += dot_nn(grad_t[0:HD], prob_a)
            dv_s[HD:PAIR, own] += dot_nn(grad_t[HD:PAIR], prob_b)
            return query_grad

        dq_s[...] = one_block(rows, row_at >= col_at)
        if block:

            def step(other, carry, one_block=one_block):
                dq_s[...] += one_block(pl.ds(pl.multiple_of(other * BLOCK, BLOCK), BLOCK))
                return carry

            lax.fori_loop(first_ref[block], block, step, 0)
        dq_ref[rows, :] = (dq_s[...] * SCALE).astype(bf16)
    dk_ref[...] = dk_s[...].T.astype(bf16)
    dv_ref[...] = dv_s[...].T.astype(bf16)


def self_backward(first_blocks, packed, key_tag, extra, mixed, grad):
    rows = packed.shape[0]
    pairs = D // PAIR
    shifted = lambda by: pl.BlockSpec((rows, PAIR), lambda p, *_: (0, p + by))
    return pl.pallas_call(
        self_backward_kernel,
        out_shape=(jax.ShapeDtypeStruct((rows, D), bf16),) * 3,
        grid_spec=pltpu.PrefetchScalarGridSpec(
            num_scalar_prefetch=1,
            grid=(pairs,),
            in_specs=[
                shifted(0), shifted(pairs), shifted(2 * pairs), whole_spec((rows, PAIR)),
                pair_spec(rows), pair_spec(rows), pair_spec(rows),
            ],
            out_specs=[pair_spec(rows)] * 3,
            scratch_shapes=[
                pltpu.VMEM((PAIR, rows), f32),
                pltpu.VMEM((PAIR, rows), f32),
                pltpu.VMEM((BLOCK, PAIR), f32),
            ],
        ),
        compiler_params=pltpu.CompilerParams(vmem_limit_bytes=VMEM_ASK),
        cost_estimate=pl.CostEstimate(
            flops=24_000_000_000, bytes_accessed=16_000_000, transcendentals=4_000_000
        ),
        name="self_backward",
    )(first_blocks, packed, packed, packed, key_tag, extra, mixed, grad)


def first_block_table(segment_row):
    clips = jnp.arange(CLIPS, dtype=jnp.int32)
    starts = jnp.sum((segment_row[:, None] < clips[None, :]).astype(jnp.int32), 0)
    heads = segment_row[::BLOCK]
    first = jnp.sum(jnp.where(heads[:, None] == clips[None, :], starts[None, :], 0), 1)
    return (first // BLOCK).astype(jnp.int32)


epsilon = 1e-05
ROOT = math.sqrt(2.0 / math.pi)
CUBE = 0.044715
C = 256
IMG = 64
POOL = 4


TILE = 256


def dot_tn(left, right):
    return lax.dot_general(left, right, (((0,), (0,)), ((), ())), preferred_element_type=f32)


def normalized(values):
    average = jnp.mean(values, -1, keepdims=True)
    centred = values - average
    spread = lax.rsqrt(jnp.mean(centred * centred, -1, keepdims=True) + epsilon)
    return centred * spread, spread


def norm_back(unit, spread, gain, grad):
    scaled = grad * gain
    mean_scaled = jnp.mean(scaled, -1, keepdims=True)
    mean_along = jnp.mean(scaled * unit, -1, keepdims=True)
    lead = tuple(range(grad.ndim - 1))
    return (
        (scaled - mean_scaled - unit * mean_along) * spread,
        jnp.sum(grad * unit, lead),
        jnp.sum(grad, lead),
    )


def gelu_and_slope(value):
    square = value * value
    bent = jnp.tanh(value * (ROOT + (ROOT * CUBE) * square))
    half = 0.5 + 0.5 * bent
    slope = half + value * (0.5 - 0.5 * bent * bent) * (ROOT + (3.0 * ROOT * CUBE) * square)
    return value * half, slope


def tiles_of(count):
    return [pl.ds(at, TILE) for at in range(0, count, TILE)]


def feed_forward_kernel(
    middle_ref, mixed_ref, join_ref, gain_ref, shift_ref, up_ref, bias_ref, down_ref, grad_ref,
    out_ref, second_ref, low_ref, mixed_grad_ref, join_grad_ref, gain_grad_ref, shift_grad_ref,
    bias_grad_ref, chunk_ref,
    normed_s, grad_t_s, back_s, hidden_s, pre_grad_s, up_s, down_s, sems,
):
    step = pl.program_id(0)
    steps = pl.num_programs(0)
    rows = middle_ref.shape[0]
    shares, deep = chunk_ref.shape[0], chunk_ref.shape[1] // 2
    group, narrow = D // deep, D // shares

    @pl.when(step == 0)
    def _():
        for at in tiles_of(rows):
            total = middle_ref[at, :] + dot_nn(mixed_ref[at, :], join_ref[...])
            out_ref[at, :] = total
            second_ref[at, :] = total
            unit, _ = normalized(total)
            normed_s[at, :] = (unit * gain_ref[...] + shift_ref[...]).astype(bf16)
            back_s[at, :] = jnp.zeros((TILE, D), f32)
            grad_t_s[:, at] = grad_ref[at, :].T

    bias_grad = jnp.zeros((1, D), f32)
    for at in tiles_of(rows):
        hidden, slope = gelu_and_slope(dot_nn(normed_s[at, :], up_ref[...]) + bias_ref[...])
        hidden = hidden.astype(bf16)
        hidden_s[at, :] = hidden
        pre_grad = (dot_nt(grad_ref[at, :], down_ref[...]) * slope).astype(bf16)
        pre_grad_s[at, :] = pre_grad
        bias_grad += jnp.sum(pre_grad.astype(f32), 0, keepdims=True)
        out_ref[at, :] += dot_nn(hidden, down_ref[...])
        back_s[at, :] += dot_nt(pre_grad, up_ref[...])
    bias_grad_ref[...] = bias_grad
    up_s[step] = dot_tn(pre_grad_s[...], normed_s[...]).astype(bf16).reshape(group, deep, D)
    down_s[step] = dot_nn(grad_t_s[...], hidden_s[...]).astype(bf16).reshape(shares, narrow, D)

    def copies(at):
        return (
            pltpu.make_async_copy(
                up_s.at[at], chunk_ref.at[pl.ds(at * group, group), pl.ds(0, deep)], sems.at[0, at]
            ),
            pltpu.make_async_copy(
                down_s.at[at],
                chunk_ref.at[:, pl.ds(pl.multiple_of(deep + at * narrow, 16), narrow)],
                sems.at[1, at],
            ),
        )

    for copy in copies(step):
        copy.start()

    @pl.when(step == steps - 1)
    def _():
        gain_grad = jnp.zeros((1, D), f32)
        shift_grad = jnp.zeros((1, D), f32)
        for at in tiles_of(rows):
            unit, spread = normalized(second_ref[at, :])
            part, one, two = norm_back(unit, spread, gain_ref[...], back_s[at, :])
            gain_grad += one[None]
            shift_grad += two[None]
            total = grad_ref[at, :].astype(f32) + part
            second_ref[at, :] = total
            low = total.astype(bf16)
            low_ref[at, :] = low
            mixed_grad_ref[at, :] = dot_nt(low, join_ref[...]).astype(bf16)
        gain_grad_ref[...] = gain_grad
        shift_grad_ref[...] = shift_grad
        join_grad_ref[...] = dot_tn(low_ref[...], mixed_ref[...]).astype(bf16)
        for at in range(FF // D):
            for copy in copies(at):
                copy.wait()


FF = 3072


def still(shape):
    return pl.BlockSpec(shape, lambda *_: (0,) * len(shape), pipeline_mode=pl.Buffered(1))


def feed_forward(middle, mixed, join, gain, shift, up, bias, down, grad, shares):
    rows = middle.shape[0]
    steps = FF // D
    deep = FF // shares
    tall = still((rows, D))
    row = still((1, D))
    return pl.pallas_call(
        feed_forward_kernel,
        out_shape=(
            jax.ShapeDtypeStruct((rows, D), f32),
            jax.ShapeDtypeStruct((rows, D), f32),
            jax.ShapeDtypeStruct((rows, D), bf16),
            jax.ShapeDtypeStruct((rows, D), bf16),
            jax.ShapeDtypeStruct((D, D), bf16),
            jax.ShapeDtypeStruct((1, D), f32),
            jax.ShapeDtypeStruct((1, D), f32),
            jax.ShapeDtypeStruct((1, FF), f32),
            jax.ShapeDtypeStruct((shares, 2 * deep, D), bf16),
        ),
        grid_spec=pltpu.PrefetchScalarGridSpec(
            num_scalar_prefetch=0,
            grid=(steps,),
            in_specs=[
                tall, tall, still((D, D)), row, row,
                pl.BlockSpec((D, D), lambda j: (0, j)),
                pl.BlockSpec((1, D), lambda j: (0, j)),
                pl.BlockSpec((D, D), lambda j: (j, 0)),
                tall,
            ],
            out_specs=[
                tall, tall, tall, tall, still((D, D)), row, row,
                pl.BlockSpec((1, D), lambda j: (0, j)),
                pl.BlockSpec(memory_space=pl.ANY),
            ],
            scratch_shapes=[
                pltpu.VMEM((rows, D), bf16),
                pltpu.VMEM((D, rows), bf16),
                pltpu.VMEM((rows, D), f32),
                pltpu.VMEM((rows, D), bf16),
                pltpu.VMEM((rows, D), bf16),
                pltpu.VMEM((steps, D // deep, deep, D), bf16),
                pltpu.VMEM((steps, shares, D // shares, D), bf16),
                pltpu.SemaphoreType.DMA((2, steps)),
            ],
        ),
        compiler_params=pltpu.CompilerParams(vmem_limit_bytes=56 * 2**20),
        cost_estimate=pl.CostEstimate(
            flops=34_000_000_000, bytes_accessed=40_000_000, transcendentals=3_200_000
        ),
        name="feed_forward",
    )(middle, mixed, join, gain[None], shift[None], up, bias[None], down, grad)


def project_back_kernel(
    query_ref, key_ref, value_ref, project_ref, middle_ref, second_ref, gain_ref, shift_ref,
    join_ref, mixed_ref,
    middle_grad_ref, mixed_grad_ref, project_grad_ref, join_grad_ref, gain_grad_ref, shift_grad_ref,
    normed_s, low_s,
):
    rows = middle_ref.shape[0]
    gain_grad = jnp.zeros((1, D), f32)
    shift_grad = jnp.zeros((1, D), f32)
    for at in tiles_of(rows):
        back = dot_nt(query_ref[at, :], project_ref[:, 0:D])
        back += dot_nt(key_ref[at, :], project_ref[:, D : 2 * D])
        back += dot_nt(value_ref[at, :], project_ref[:, 2 * D : 3 * D])
        unit, spread = normalized(middle_ref[at, :])
        normed_s[at, :] = (unit * gain_ref[...] + shift_ref[...]).astype(bf16)
        part, one, two = norm_back(unit, spread, gain_ref[...], back)
        gain_grad += one[None]
        shift_grad += two[None]
        total = second_ref[at, :] + part
        middle_grad_ref[at, :] = total
        low = total.astype(bf16)
        low_s[at, :] = low
        mixed_grad_ref[at, :] = dot_nt(low, join_ref[...]).astype(bf16)
    gain_grad_ref[...] = gain_grad
    shift_grad_ref[...] = shift_grad
    project_grad_ref[0:D] = dot_tn(query_ref[...], normed_s[...]).astype(bf16)
    project_grad_ref[D : 2 * D] = dot_tn(key_ref[...], normed_s[...]).astype(bf16)
    project_grad_ref[2 * D : 3 * D] = dot_tn(value_ref[...], normed_s[...]).astype(bf16)
    join_grad_ref[...] = dot_tn(low_s[...], mixed_ref[...]).astype(bf16)


def project_back(query, key, value, project, middle, second, gain, shift, join, mixed):
    rows = middle.shape[0]
    return pl.pallas_call(
        project_back_kernel,
        out_shape=(
            jax.ShapeDtypeStruct((rows, D), f32),
            jax.ShapeDtypeStruct((rows, D), bf16),
            jax.ShapeDtypeStruct((3 * D, D), bf16),
            jax.ShapeDtypeStruct((D, D), bf16),
            jax.ShapeDtypeStruct((1, D), f32),
            jax.ShapeDtypeStruct((1, D), f32),
        ),
        in_specs=[pl.BlockSpec(memory_space=pltpu.VMEM)] * 10,
        out_specs=[pl.BlockSpec(memory_space=pltpu.VMEM)] * 6,
        scratch_shapes=[pltpu.VMEM((rows, D), bf16), pltpu.VMEM((rows, D), bf16)],
        compiler_params=pltpu.CompilerParams(vmem_limit_bytes=56 * 2**20),
        cost_estimate=pl.CostEstimate(
            flops=10_000_000_000, bytes_accessed=30_000_000, transcendentals=2_000
        ),
        name="project_back",
    )(query, key, value, project, middle, second, gain[None], shift[None], join, mixed)


MESH = pl.DeviceIdType.MESH


def bits_of(count):
    return count.bit_length() - 1


def plan_streams(rows, dp, orders):
    unit = 16 * dp
    units = rows // unit
    sizes = [units // len(orders) + (i < units % len(orders)) for i in range(len(orders))]
    plan, at = [], 0
    for order, size in zip(orders, sizes):
        if size:
            plan.append((at * unit, size * unit, order))
            at += size
    return plan


def stream_steps(count, kind_order, dp_bits, q_bits):
    dp_up = [("dp", b) for b in range(dp_bits)]
    dp_down = dp_up[::-1]
    q_steps = [("q", b) for b in range(q_bits)]
    return {
        "up": dp_up + q_steps,
        "down": dp_down + q_steps,
        "q_up": q_steps + dp_up,
        "q_down": q_steps + dp_down,
    }[kind_order]


def reduce_kernel(layout, dp, row, *refs):
    (partial_ref, summed_ref, out_ref), refs = refs[:3], refs[3:]
    accs, refs = refs[: len(layout)], refs[len(layout) :]
    n_recv = sum(len(item[3]) + (item[0] == 0) for item in layout)
    recvs, (send_sem, recv_sem, local_sem) = refs[:n_recv], refs[n_recv:]
    me_dp, me_row = lax.axis_index("dp"), lax.axis_index("row")
    core = lax.rem(me_row, 2)
    me_q = me_row // 2
    q_bits = bits_of(row // 2)

    def bit(value, b):
        return lax.rem(value // (2**b), 2)

    def partner(step):
        kind, b = step
        if kind == "core":
            return me_dp, me_row + 1 - 2 * core
        if kind == "dp":
            return me_dp + (2**b) * (1 - 2 * bit(me_dp, b)), me_row
        return me_dp, me_row + 2 * (2**b) * (1 - 2 * bit(me_q, b))

    steps_all = [("core", 0)] + [("dp", b) for b in range(bits_of(dp))]
    steps_all += [("q", b) for b in range(q_bits)]
    barrier = pltpu.get_barrier_semaphore()
    for step in steps_all:
        pl.semaphore_signal(barrier, inc=1, device_id=partner(step), device_id_type=MESH)
    pl.semaphore_wait(barrier, len(steps_all))

    counter = [0]

    def push(src, dst, step):
        at = counter[0]
        counter[0] += 1
        copy = pltpu.make_async_remote_copy(
            src_ref=src, dst_ref=dst, send_sem=send_sem.at[at], recv_sem=recv_sem.at[at],
            device_id=partner(step), device_id_type=MESH,
        )
        copy.start()
        return copy

    state = []
    free = list(recvs)
    started = []
    for at, (source, first, rows, steps) in enumerate(layout):
        acc = accs[at]
        rows_at = pl.ds(first, rows)
        if source == 0:
            every = (slice(None),) * q_bits
            landing = free.pop(0)
            local = pltpu.make_async_copy(
                partial_ref.at[every + (core, rows_at)], acc, local_sem.at[at]
            )
            copy = push(partial_ref.at[every + (1 - core, rows_at)], landing, ("core", 0))
            started.append(copy)
        else:
            landing, copy = None, None
            local = pltpu.make_async_copy(summed_ref.at[rows_at], acc, local_sem.at[at])
        local.start()
        state.append(dict(
            acc=acc, number=at, source=source, local=local, copy=copy,
            landing=landing, picked=[None] * (q_bits if source == 0 else 0), off=0, rows=rows,
            steps=list(steps), todo=list(steps),
        ))

    def index_of(item, off, rows):
        picks = tuple(slice(None) if p is None else p for p in item["picked"])
        return picks + (pl.ds(pl.multiple_of(off, 16), rows),)

    def add_landing(item):
        acc, landing = item["acc"], item["landing"]
        rows = item["rows"]
        picks = index_of(item, 0, 16)[:-1]
        lead = (slice(None),) * (len(landing.shape) - 2)

        def body(i, carry):
            own = picks + (pl.ds(pl.multiple_of(item["off"] + i * 16, 16), 16),)
            other = lead + (pl.ds(pl.multiple_of(i * 16, 16), 16),)
            acc[own] = (acc[own].astype(f32) + landing[other].astype(f32)).astype(bf16)
            return carry

        lax.fori_loop(0, rows // 16, body, 0)

    def send_next(item):
        kind, b = item["todo"].pop(0)
        landing = free.pop(0)
        if kind == "dp":
            half = item["rows"] // 2
            mine = bit(me_dp, b)
            src = item["acc"].at[index_of(item, item["off"] + (1 - mine) * half, half)]
            item["copy"] = push(src, landing, (kind, b))
            item["off"] = item["off"] + mine * half
            item["rows"] = half
        else:
            mine = bit(me_q, b)
            place = q_bits - 1 - b
            item["picked"][place] = 1 - mine
            src = item["acc"].at[index_of(item, item["off"], item["rows"])]
            item["copy"] = push(src, landing, (kind, b))
            item["picked"][place] = mine
        started.append(item["copy"])
        item["landing"] = landing

    for item in state:
        if item["source"] == 1:
            item["local"].wait()
            send_next(item)
    busy = [item for item in state if item["source"] == 0] + [
        item for item in state if item["source"] == 1
    ]
    gathering = []
    while busy:
        for item in list(busy):
            if item["local"] is not None and item["source"] == 0:
                item["local"].wait()
                item["local"] = None
            item["copy"].wait_recv()
            add_landing(item)
            if item["todo"]:
                send_next(item)
            else:
                busy = [other for other in busy if other is not item]
                base = item["base"] = layout_base(layout, item["number"])
                picks = index_of(item, item["off"], item["rows"])
                out_ref[pl.ds(pl.multiple_of(base + item["off"], 16), item["rows"]), :] = item["acc"][picks]
                item["back"] = [s for s in item["steps"] if s[0] == "dp"][::-1]
                gather_next(item, out_ref, push, bit, me_dp, started)
                gathering.append(item)
    while gathering:
        for item in list(gathering):
            item["copy"].wait_recv()
            kind, b = item["back"].pop(0)
            item["off"] = item["off"] - bit(me_dp, b) * item["rows"]
            item["rows"] *= 2
            if item["back"]:
                gather_next(item, out_ref, push, bit, me_dp, started)
            else:
                gathering = [other for other in gathering if other is not item]
    for copy in started:
        copy.wait_send()


def layout_base(layout, at):
    return sum(item[2] for item in layout[:at])


def gather_next(item, out_ref, push, bit, me_dp, started):
    at = pl.ds(pl.multiple_of(item["base"] + item["off"], 16), item["rows"])
    item["copy"] = push(out_ref.at[at], out_ref.at[at], item["back"][0])
    started.append(item["copy"])


def reduce_everything(partial, summed, dp, row, orders, summed_orders):
    q_bits, dp_bits = bits_of(row // 2), bits_of(dp)
    layout = [
        (0, first, rows, stream_steps(rows, order, dp_bits, q_bits))
        for first, rows, order in plan_streams(partial.shape[1], dp, orders)
    ] + [
        (1, first, rows, stream_steps(rows, order, dp_bits, 0))
        for first, rows, order in plan_streams(summed.shape[0], dp, summed_orders)
    ]
    accs, recvs = [], []
    for source, _, rows, steps in layout:
        lead = (2,) * (q_bits if source == 0 else 0)
        accs.append(pltpu.VMEM(lead + (rows, D), bf16))
    for source, _, rows, steps in layout:
        if source == 0:
            recvs.append((0, pltpu.VMEM((2,) * q_bits + (rows, D), bf16)))
    walk = [
        dict(rows=rows, lead=q_bits if source == 0 else 0, todo=list(steps), source=source)
        for source, _, rows, steps in layout
    ]

    def landing(item):
        kind, _ = item["todo"].pop(0)
        if kind == "dp":
            item["rows"] //= 2
        else:
            item["lead"] -= 1
        recvs.append((1, pltpu.VMEM((2,) * item["lead"] + (item["rows"], D), bf16)))

    for item in walk:
        if item["source"] == 1:
            landing(item)
    busy = [i for i in walk if i["source"] == 0] + [i for i in walk if i["source"] == 1]
    while busy:
        for item in list(busy):
            if item["todo"]:
                landing(item)
            else:
                busy.remove(item)
    recvs = [spec for _, spec in recvs]
    n_copies = len(recvs) + len(layout) * dp_bits
    rows_out = sum(item[2] for item in layout)
    view = (2,) * q_bits + (2,) + partial.shape[1:]
    return pl.pallas_call(
        functools.partial(reduce_kernel, layout, dp, row),
        out_shape=jax.ShapeDtypeStruct((rows_out, D), bf16),
        in_specs=[pl.BlockSpec(memory_space=pl.ANY)] * 2,
        out_specs=pl.BlockSpec(memory_space=pltpu.VMEM),
        scratch_shapes=accs + recvs + [
            pltpu.SemaphoreType.DMA((n_copies,)),
            pltpu.SemaphoreType.DMA((n_copies,)),
            pltpu.SemaphoreType.DMA((len(layout),)),
        ],
        compiler_params=pltpu.CompilerParams(
            collective_id=3, has_side_effects=True, vmem_limit_bytes=VMEM_ASK
        ),
        name="reduce_everything",
    )(partial.reshape(view), summed)


def row_of(lead, me_row):
    return lead + (me_row,)


def greet_row(row):
    me_dp, me_row = lax.axis_index("dp"), lax.axis_index("row")
    barrier = pltpu.get_barrier_semaphore()
    for ahead in range(1, row):
        pl.semaphore_signal(
            barrier, inc=1, device_id=(me_dp, lax.rem(me_row + ahead, row)), device_id_type=MESH
        )
    pl.semaphore_wait(barrier, row - 1)


def edge_copies(cells, above, below, send_sem, recv_sem, row):
    me_dp, me_row = lax.axis_index("dp"), lax.axis_index("row")
    here = cells.shape[1]
    onward = pltpu.make_async_remote_copy(
        src_ref=cells.at[:, here - 1], dst_ref=above, send_sem=send_sem.at[0],
        recv_sem=recv_sem.at[0], device_id=(me_dp, lax.rem(me_row + 1, row)), device_id_type=MESH,
    )
    back = pltpu.make_async_remote_copy(
        src_ref=cells.at[:, 0], dst_ref=below, send_sem=send_sem.at[1],
        recv_sem=recv_sem.at[1], device_id=(me_dp, lax.rem(me_row + row - 1, row)),
        device_id_type=MESH,
    )
    return onward, back


def start_edges(copies):
    for copy in copies:
        copy.start()


def end_edges(copies):
    for copy in copies:
        copy.wait_send()
        copy.wait_recv()


def put_wide(wide, frame, first, cells):
    column = lax.broadcasted_iota(jnp.int32, cells.shape, 0) % IMG
    cells = cells.astype(f32)
    count = cells.shape[0]
    left = jnp.where(column == 0, 0.0, pltpu.roll(cells, 1, 0))
    right = jnp.where(column == IMG - 1, 0.0, pltpu.roll(cells, count - 1, 0))
    at = pl.ds(first, count)
    wide[frame, at, 0:C] = left.astype(bf16)
    wide[frame, at, C : 2 * C] = cells.astype(bf16)
    wide[frame, at, 2 * C : 3 * C] = right.astype(bf16)


def put_edges(wide, above, below, here, row):
    me_row = lax.axis_index("row")
    keep_above = jnp.where(me_row > 0, 1.0, 0.0)
    keep_below = jnp.where(me_row < row - 1, 1.0, 0.0)
    for frame in range(wide.shape[0]):
        put_wide(wide, frame, 0, above[frame].astype(f32) * keep_above)
        put_wide(wide, frame, (here + 1) * IMG, below[frame].astype(f32) * keep_below)


def conv_forward_kernel(
    row, frames_ref, taps_ref, bias_ref, gain_ref, shift_ref,
    pre_ref, wide_ref, every_ref,
    above_s, below_s, pool_s, edge_send, edge_recv, send_sem, recv_sem,
):
    me_dp, me_row = lax.axis_index("dp"), lax.axis_index("row")
    core, me_q, places = lax.rem(me_row, 2), me_row // 2, row // 2
    count, here = frames_ref.shape[0], frames_ref.shape[1]
    greet_row(row)
    edges = edge_copies(frames_ref, above_s, below_s, edge_send, edge_recv, row)
    start_edges(edges)
    for frame in range(count):
        put_wide(wide_ref, frame, IMG, frames_ref[frame].reshape(here * IMG, C))
    end_edges(edges)
    put_edges(wide_ref, above_s, below_s, here, row)
    tile = POOL * IMG
    for frame in range(count):
        for part in range(here // POOL):
            first = part * tile
            pre = bias_ref[...] + dot_nn(wide_ref[frame, pl.ds(first, tile), :], taps_ref[0])
            pre += dot_nn(wide_ref[frame, pl.ds(first + IMG, tile), :], taps_ref[1])
            pre += dot_nn(wide_ref[frame, pl.ds(first + 2 * IMG, tile), :], taps_ref[2])
            pre_ref[frame, pl.ds(first, tile), :] = pre
            active, _ = gelu_and_slope(pre)
            unit, _ = normalized(active)
            normed = unit * gain_ref[...] + shift_ref[...]
            lines = normed.reshape(POOL, IMG, C)
            lines = lines[0] + lines[1] + lines[2] + lines[3]
            cells = IMG // POOL
            for side in range(C // PAIR):
                lanes = slice(side * PAIR, (side + 1) * PAIR)
                pool_s[side] = lines[:, lanes]
                total = pool_s[side, pl.ds(0, cells, stride=POOL), :]
                for at in range(1, POOL):
                    total += pool_s[side, pl.ds(at, cells, stride=POOL), :]
                every_ref[frame, me_row, pl.ds(part * cells, cells), lanes] = (
                    total * (1.0 / (POOL * POOL))
                ).astype(bf16)

    def push(source_row, to_row, at):
        copy = pltpu.make_async_remote_copy(
            src_ref=every_ref.at[:, source_row], dst_ref=every_ref.at[:, source_row],
            send_sem=send_sem.at[at], recv_sem=recv_sem.at[at], device_id=(me_dp, to_row),
            device_id_type=MESH,
        )
        copy.start()
        return copy

    other = me_row + 1 - 2 * core
    copies = [push(me_row, other, 0)]
    for ahead in range(1, places):
        copies.append(push(me_row, lax.rem(me_q + ahead, places) * 2 + core, ahead))
    for ahead in range(1, places):
        copies[ahead].wait_recv()
        came = lax.rem(me_q + places - ahead, places) * 2 + core
        copies.append(push(came, other, places - 1 + ahead))
    copies[0].wait_recv()
    for copy in copies[places:]:
        copy.wait_recv()
    for copy in copies:
        copy.wait_send()


def conv_forward(frames, taps, bias, gain, shift, row):
    count, here = frames.shape[0], frames.shape[1]
    keys = (here // POOL) * (IMG // POOL)
    return pl.pallas_call(
        functools.partial(conv_forward_kernel, row),
        out_shape=(
            jax.ShapeDtypeStruct((count, here * IMG, C), f32),
            jax.ShapeDtypeStruct((count, (here + 2) * IMG, 3 * C), bf16),
            jax.ShapeDtypeStruct((count, row, keys, C), bf16),
        ),
        in_specs=[pl.BlockSpec(memory_space=pltpu.VMEM)] * 5,
        out_specs=[pl.BlockSpec(memory_space=pltpu.VMEM)] * 3,
        scratch_shapes=[
            pltpu.VMEM((count, IMG, C), bf16),
            pltpu.VMEM((count, IMG, C), bf16),
            pltpu.VMEM((C // PAIR, IMG, PAIR), f32),
            pltpu.SemaphoreType.DMA((2,)),
            pltpu.SemaphoreType.DMA((2,)),
            pltpu.SemaphoreType.DMA((row,)),
            pltpu.SemaphoreType.DMA((row,)),
        ],
        compiler_params=pltpu.CompilerParams(
            collective_id=1, has_side_effects=True, vmem_limit_bytes=VMEM_ASK
        ),
        name="conv_forward",
    )(frames, taps.reshape(3, 3 * C, C), bias[None], gain[None], shift[None])


def conv_backward_kernel(
    row, keys_grad_ref, values_grad_ref, key_w_ref, value_w_ref, pre_ref, wide_ref, taps_ref,
    gain_ref,
    frames_grad_ref, filter_grad_ref, bias_grad_ref, gain_grad_ref, shift_grad_ref,
    part_s, landing_s, sum_s, arrive_s, spread_s, grad_s, grad_t_s, wide_s, above_s, below_s,
    edge_send, edge_recv, send_sem, recv_sem,
):
    me_dp, me_row = lax.axis_index("dp"), lax.axis_index("row")
    core, me_q, places = lax.rem(me_row, 2), me_row // 2, row // 2
    count, here = grad_s.shape[0], grad_s.shape[1]
    keys = part_s.shape[3]
    greet_row(row)
    part = lax.dot_general(
        keys_grad_ref[...], key_w_ref[...], (((0,), (1,)), ((), ())), preferred_element_type=f32
    )
    part += lax.dot_general(
        values_grad_ref[...], value_w_ref[...], (((0,), (1,)), ((), ())), preferred_element_type=f32
    )
    part_s[...] = part.astype(bf16).reshape(count, places, 2, keys, C)

    def push(src, dst, to_row, at):
        copy = pltpu.make_async_remote_copy(
            src_ref=src, dst_ref=dst, send_sem=send_sem.at[at], recv_sem=recv_sem.at[at],
            device_id=(me_dp, to_row), device_id_type=MESH,
        )
        copy.start()
        return copy

    copies = [push(part_s.at[:, :, 1 - core], landing_s, me_row + 1 - 2 * core, 0)]
    copies[0].wait_recv()
    sum_s[...] = (part_s[:, :, core].astype(f32) + landing_s[...].astype(f32)).astype(bf16)
    for ahead in range(1, places):
        to = lax.rem(me_q + ahead, places)
        copies.append(push(sum_s.at[:, to], arrive_s.at[ahead - 1], to * 2 + core, ahead))
    for copy in copies[1:]:
        copy.wait_recv()
    pooled = sum_s[:, me_q].astype(f32)
    for ahead in range(1, places):
        pooled += arrive_s[ahead - 1].astype(f32)
    pooled = pooled * (1.0 / (POOL * POOL))

    tile = POOL * IMG
    cells = IMG // POOL
    bias_grad = jnp.zeros((1, C), f32)
    gain_grad = jnp.zeros((1, C), f32)
    shift_grad = jnp.zeros((1, C), f32)
    for frame in range(count):
        for part in range(here // POOL):
            for side in range(C // PAIR):
                own = pooled[
                    frame, part * cells : (part + 1) * cells, side * PAIR : (side + 1) * PAIR
                ]
                for at in range(POOL):
                    spread_s[side, pl.ds(at, cells, stride=POOL), :] = own
            line = jnp.concatenate([spread_s[side] for side in range(C // PAIR)], 1)
            back = jnp.broadcast_to(line[None], (POOL, IMG, C)).reshape(tile, C)
            active, slope = gelu_and_slope(pre_ref[frame, pl.ds(part * tile, tile), :])
            unit, spread = normalized(active)
            grad, one, two = norm_back(unit, spread, gain_ref[...], back)
            gain_grad += one[None]
            shift_grad += two[None]
            grad = (slope * grad).astype(bf16)
            bias_grad += jnp.sum(grad.astype(f32), 0, keepdims=True)
            grad_s[frame, pl.ds(part * POOL, POOL)] = grad.reshape(POOL, IMG, C)
    bias_grad_ref[...] = bias_grad
    gain_grad_ref[...] = gain_grad
    shift_grad_ref[...] = shift_grad
    edges = edge_copies(grad_s, above_s, below_s, edge_send, edge_recv, row)
    start_edges(edges)
    for frame in range(count):
        cells_here = grad_s[frame].reshape(here * IMG, C)
        put_wide(wide_s, frame, IMG, cells_here)
        grad_t_s[frame] = cells_here.T
    for dy in range(3):
        total = None
        for frame in range(count):
            piece = dot_nn(grad_t_s[frame], wide_ref[frame, pl.ds(dy * IMG, here * IMG), :])
            total = piece if total is None else total + piece
        filter_grad_ref[dy] = total.astype(bf16)
    end_edges(edges)
    put_edges(wide_s, above_s, below_s, here, row)
    for frame in range(count):
        for part in range(here // POOL):
            total = None
            for tap in range(9):
                dy, dx = tap // 3, tap % 3
                window = wide_s[frame, pl.ds(part * tile + dy * IMG, tile), dx * C : (dx + 1) * C]
                piece = dot_nt(window, taps_ref[8 - tap])
                total = piece if total is None else total + piece
            frames_grad_ref[frame, pl.ds(part * tile, tile), :] = total
    for copy in copies:
        copy.wait_send()


def conv_backward(keys_grad_t, values_grad_t, key_w, value_w, pre, wide, taps, gain, row):
    count = pre.shape[0]
    here = pre.shape[1] // IMG
    keys = (here // POOL) * (IMG // POOL)
    return pl.pallas_call(
        functools.partial(conv_backward_kernel, row),
        out_shape=(
            jax.ShapeDtypeStruct(pre.shape, f32),
            jax.ShapeDtypeStruct((3, C, 3 * C), bf16),
            jax.ShapeDtypeStruct((1, C), f32),
            jax.ShapeDtypeStruct((1, C), f32),
            jax.ShapeDtypeStruct((1, C), f32),
        ),
        in_specs=[pl.BlockSpec(memory_space=pltpu.VMEM)] * 8,
        out_specs=[pl.BlockSpec(memory_space=pltpu.VMEM)] * 5,
        scratch_shapes=[
            pltpu.VMEM((count, row // 2, 2, keys, C), bf16),
            pltpu.VMEM((count, row // 2, keys, C), bf16),
            pltpu.VMEM((count, row // 2, keys, C), bf16),
            pltpu.VMEM((row // 2 - 1, count, keys, C), bf16),
            pltpu.VMEM((C // PAIR, IMG, PAIR), f32),
            pltpu.VMEM((count, here, IMG, C), bf16),
            pltpu.VMEM((count, C, here * IMG), bf16),
            pltpu.VMEM((count, (here + 2) * IMG, 3 * C), bf16),
            pltpu.VMEM((count, IMG, C), bf16),
            pltpu.VMEM((count, IMG, C), bf16),
            pltpu.SemaphoreType.DMA((2,)),
            pltpu.SemaphoreType.DMA((2,)),
            pltpu.SemaphoreType.DMA((row,)),
            pltpu.SemaphoreType.DMA((row,)),
        ],
        compiler_params=pltpu.CompilerParams(
            collective_id=2, has_side_effects=True, vmem_limit_bytes=VMEM_ASK
        ),
        name="conv_backward",
    )(keys_grad_t, values_grad_t, key_w, value_w, pre, wide, taps, gain[None])


def fast_dot(left, right):
    return jnp.dot(left, right, preferred_element_type=f32)


def shared_rows(matrix, count):
    return matrix.reshape(count, matrix.shape[0] // count, matrix.shape[1])


def on_device(
    frames, tokens, segment_ids, clip_frame, filter_weight, filter_bias, context_gain,
    context_shift, cross_query, cross_key, cross_value, cross_output, first_gain, first_shift,
    self_project, self_output, second_gain, second_shift, up_weight, up_bias, down_weight, cotangent,
):
    shares = lax.axis_size("row")
    x = tokens[0]
    segments = segment_ids[0]
    clip_frames = clip_frame[0]
    out_grad = cotangent[0]
    tags = segment_tags(segments)
    key_tag = key_tags(segments)
    first_blocks = first_block_table(segments)

    pre_act, wide, everyone = conv_forward(
        frames, filter_weight, filter_bias, context_gain, context_shift, shares
    )
    everyone = everyone.reshape(-1, C)
    cross_q = fast_dot(x, cross_query).astype(bf16)
    cross_mixed, cross_extra = cross_forward(
        segments, clip_frames, cross_q, everyone, cross_key, cross_value, tags
    )
    middle = x.astype(f32) + fast_dot(cross_mixed, cross_output)
    first_unit, first_spread = normalized(middle)
    first_normed = (first_unit * first_gain + first_shift).astype(bf16)
    packed = fast_dot(first_normed, self_project).astype(bf16)
    self_mixed, self_extra = self_forward(first_blocks, packed, tags, key_tag)
    (
        output, second_grad, second_low, self_mixed_grad, join_grad, second_gain_grad,
        second_shift_grad, up_bias_grad, chunk_a,
    ) = feed_forward(
        middle, self_mixed, self_output, second_gain, second_shift, up_weight, up_bias, down_weight,
        out_grad, shares,
    )
    share_a = lax.psum_scatter(chunk_a, "row", scatter_dimension=0, tiled=False)
    query_grad, key_grad, value_grad = self_backward(
        first_blocks, packed, key_tag, self_extra, self_mixed, self_mixed_grad
    )
    (
        middle_grad, cross_mixed_grad, project_grad, cross_join_grad, first_gain_grad,
        first_shift_grad,
    ) = project_back(
        query_grad, key_grad, value_grad, self_project, middle, second_grad, first_gain, first_shift,
        cross_output, cross_mixed,
    )
    cross_q_grad, keys_grad_t, values_grad_t = cross_backward(
        segments, clip_frames, cross_q, everyone, cross_key, cross_value, cross_extra, cross_mixed,
        cross_mixed_grad,
    )
    tokens_grad = middle_grad + dot_nt(cross_q_grad, cross_query)

    frames_grad, filter_grad, filter_bias_grad, context_gain_grad, context_shift_grad = conv_backward(
        keys_grad_t, values_grad_t, cross_key, cross_value, pre_act, wide, filter_weight,
        context_gain, shares,
    )
    filter_pieces = [shared_rows(filter_grad[dy], shares) for dy in range(3)]
    small = jnp.concatenate(
        [
            item.astype(bf16).reshape(shares, -1)
            for item in (
                first_gain_grad, first_shift_grad, second_gain_grad, second_shift_grad,
                up_bias_grad, filter_bias_grad, context_gain_grad, context_shift_grad,
            )
        ],
        1,
    )
    small = jnp.pad(small, ((0, 0), (0, 16 * D - small.shape[1]))).reshape(shares, 16, D)
    key_pieces = [
        jnp.pad(
            fast_dot(grad_t, everyone).astype(bf16).reshape(shares, D // shares, C),
            ((0, 0), (0, 0), (0, 0)),
        )
        for grad_t in (keys_grad_t, values_grad_t)
    ]
    key_pieces = jnp.concatenate(
        key_pieces + [jnp.zeros_like(key_pieces[0])], 2
    )
    chunk = [
        shared_rows(project_grad, shares),
        shared_rows(join_grad, shares),
        shared_rows(cross_join_grad, shares),
        shared_rows(dot_tn(cross_q_grad, x).astype(bf16), shares),
        key_pieces,
        *filter_pieces,
        small,
    ]
    used = sum(item.shape[1] for item in chunk)
    unit = 16 * lax.axis_size("dp")
    spare = -used % unit
    if spare:
        chunk.append(jnp.zeros((shares, spare, D), bf16))
    reduced = reduce_everything(
        jnp.concatenate(chunk, 1), share_a, lax.axis_size("dp"), shares,
        ("up", "down", "q_up") * 2 + ("up",), ("up", "down"),
    )
    share_b, share_c = reduced[: 4 * D // shares], reduced[4 * D // shares : used]
    share_a = reduced[used + spare :]

    wide_part, model_part, own_part = 3072 // shares, D // shares, C // shares
    up_grad = share_a[:wide_part].astype(f32).T
    down_grad = jnp.concatenate(
        [
            share_a[wide_part + part * model_part : wide_part + (part + 1) * model_part].T
            for part in range(4)
        ],
        0,
    ).astype(f32)
    project_grad = share_b[: 3 * model_part].astype(f32).T
    self_output_grad = share_b[3 * model_part :].astype(f32).T
    at = 0

    def take(count):
        nonlocal at
        at += count
        return share_c[at - count : at].astype(f32)

    cross_output_grad = take(model_part).T
    cross_query_grad = take(model_part).T
    both = take(model_part)
    cross_key_grad = both[:, :C].T
    cross_value_grad = both[:, C : 2 * C].T
    filter_grad = jnp.concatenate(
        [jnp.transpose(take(own_part).reshape(own_part, 3, C), (1, 2, 0)) for _ in range(3)], 0
    )
    flat = take(16).reshape(-1)
    sizes = [model_part] * 4 + [wide_part] + [own_part] * 3
    ends = [sum(sizes[: i + 1]) for i in range(len(sizes))]
    vectors = [flat[e - s : e] for e, s in zip(ends, sizes)]
    return (
        middle[None],
        output[None],
        tokens_grad[None],
        frames_grad.reshape(frames.shape),
        filter_grad,
        vectors[5],
        vectors[6],
        vectors[7],
        cross_query_grad,
        cross_key_grad,
        cross_value_grad,
        cross_output_grad,
        vectors[0],
        vectors[1],
        project_grad,
        self_output_grad,
        vectors[2],
        vectors[3],
        up_grad,
        vectors[4],
        down_grad,
    )


def solution(mesh):
    whole = P()
    by_row = P(("dp", "row"), None, None)
    in_specs = (
        P("dp", "row", None, None),
        by_row,
        P(("dp", "row"), None),
        P(("dp", "row"), None),
    ) + (whole,) * 17 + (by_row,)
    columns = P(None, "row")
    vector = P("row")
    out_specs = (
        by_row, by_row, by_row, P("dp", "row", None, None), P(None, None, "row"), vector, vector,
        vector, columns, columns, columns, columns, vector, vector, columns, columns, vector, vector,
        columns, vector, columns,
    )
    return jax.shard_map(
        on_device, mesh=mesh, in_specs=in_specs, out_specs=out_specs, check_vma=False
    )
```

```python
import functools
import math
import jax
import jax.numpy as jnp
from jax import lax
from jax.experimental import pallas as pl
from jax.experimental.pallas import tpu as pltpu
from jax.sharding import PartitionSpec as P

D = 768
HD = 64
PAIR = 128
BLOCK = 256
KEYS = 256
CLIPS = 4
FAR = 2.0**100
SCALE = 0.125
CROSS_GROUP = 6
FORWARD_GROUP = 3
BACKWARD_GROUP = 3
f32 = jnp.float32
bf16 = jnp.bfloat16
VMEM_ASK = 48 * 2**20


def lane_of(rows):
    return lax.broadcasted_iota(jnp.int32, (rows, PAIR), 1)


def dot_nt(left, right):
    return lax.dot_general(left, right, (((1,), (1,)), ((), ())), preferred_element_type=f32)


def dot_nn(left, right):
    return lax.dot_general(left, right, (((1,), (0,)), ((), ())), preferred_element_type=f32)


def tagged(extra, value, half):
    high = value.astype(bf16).astype(f32)
    rest = value - high
    middle = rest.astype(bf16).astype(f32)
    extra = jnp.where(half == 8, -high, extra)
    extra = jnp.where(half == 9, -middle, extra)
    return jnp.where(half == 10, middle - rest, extra)


def segment_tags(segment_row):
    lane = jnp.arange(PAIR, dtype=jnp.int32) % HD
    wrong = (lane[None, :] < CLIPS) & (lane[None, :] != segment_row[:, None])
    return jnp.where(wrong, -FAR, 0.0).astype(bf16)


def key_tags(segment_row):
    lane = jnp.arange(PAIR, dtype=jnp.int32) % HD
    ones = (lane[None, :] == segment_row[:, None]) | ((lane[None, :] >= 8) & (lane[None, :] <= 10))
    return jnp.where(ones, 1.0, 0.0).astype(bf16)


def ones_tags(rows):
    half = lane_of(rows) % HD
    return jnp.where((half >= 8) & (half <= 10), 1.0, 0.0)


def halves(value, filler):
    left = lane_of(value.shape[0]) < HD
    value = value.astype(f32)
    return jnp.where(left, value, filler).astype(bf16), jnp.where(left, filler, value).astype(bf16)


def put_halves(store, group, value, filler):
    for pair in range(group):
        for at in range(0, value.shape[0], BLOCK):
            rows = slice(at, at + BLOCK)
            fill = filler if filler.shape[0] == BLOCK else filler[rows, :]
            one, two = halves(value[rows, pair * PAIR : (pair + 1) * PAIR], fill)
            store[pair, 0, rows, :] = one
            store[pair, 1, rows, :] = two


def lanes_of(pair):
    return slice(pair * PAIR, (pair + 1) * PAIR)


def cross_forward_kernel(
    group, seg_ref, frame_ref, q_ref, pooled_ref, key_w_ref, value_w_ref, col_ref,
    out_ref, extra_ref, key_s, value_s,
):
    put_halves(key_s, group, dot_nn(pooled_ref[...], key_w_ref[...]), jnp.zeros((BLOCK, PAIR), f32))
    put_halves(value_s, group, dot_nn(pooled_ref[...], value_w_ref[...]), jnp.ones((BLOCK, PAIR), f32))
    left = lane_of(BLOCK) < HD
    half = lane_of(BLOCK) % HD
    for block in range(q_ref.shape[0] // BLOCK):
        rows = pl.ds(block * BLOCK, BLOCK)
        queries = [
            (q_ref[rows, lanes_of(pair)].astype(f32) * SCALE).astype(bf16) for pair in range(group)
        ]

        def one_clip(clip, carry, rows=rows, queries=queries):
            own = pl.ds(pl.multiple_of(frame_ref[clip] * KEYS, KEYS), KEYS)
            mine = col_ref[rows, :] == clip
            scores = [
                dot_nt(queries[pair], key_s[pair, side, own, :])
                for pair in range(group)
                for side in range(2)
            ]
            tops = [jnp.max(score, -1, keepdims=True) for score in scores]
            exps = [jnp.exp(score - top).astype(bf16) for score, top in zip(scores, tops)]
            mixes = [
                dot_nn(exps[2 * pair + side], value_s[pair, side, own, :])
                for pair in range(group)
                for side in range(2)
            ]
            for pair in range(group):
                mix_a, mix_b = mixes[2 * pair : 2 * pair + 2]
                top_a, top_b = tops[2 * pair : 2 * pair + 2]
                total = jnp.where(left, mix_b, mix_a)
                mixed = jnp.where(left, mix_a, mix_b) / pltpu.roll(total, HD, 1)
                log_sum = jnp.where(left, top_b, top_a) + jnp.log(total)
                extra = tagged(jnp.zeros((BLOCK, PAIR), f32), log_sum, half)
                at = (rows, lanes_of(pair))
                out_ref[at] = jnp.where(mine, mixed, out_ref[at].astype(f32)).astype(bf16)
                extra_ref[at] = jnp.where(mine, extra, extra_ref[at].astype(f32)).astype(bf16)
            return carry

        lax.fori_loop(seg_ref[block * BLOCK], seg_ref[block * BLOCK + BLOCK - 1] + 1, one_clip, 0)


def pair_spec(rows, group):
    return pl.BlockSpec((rows, PAIR * group), lambda p, *_: (0, p))


def whole_spec(shape):
    return pl.BlockSpec(shape, lambda p, *_: (0,) * len(shape), pipeline_mode=pl.Buffered(1))


def cross_forward(segments, frames, queries, pooled, key_w, value_w):
    rows = queries.shape[0]
    keys = pooled.shape[0]
    group = CROSS_GROUP
    return pl.pallas_call(
        functools.partial(cross_forward_kernel, group),
        out_shape=(
            jax.ShapeDtypeStruct((rows, D), bf16),
            jax.ShapeDtypeStruct((rows, D), bf16),
        ),
        grid_spec=pltpu.PrefetchScalarGridSpec(
            num_scalar_prefetch=2,
            grid=(D // PAIR // group,),
            in_specs=[
                pair_spec(rows, group),
                whole_spec(pooled.shape),
                pair_spec(key_w.shape[0], group),
                pair_spec(key_w.shape[0], group),
                whole_spec((rows, 1)),
            ],
            out_specs=[pair_spec(rows, group), pair_spec(rows, group)],
            scratch_shapes=[pltpu.VMEM((group, 2, keys, PAIR), bf16)] * 2,
        ),
        compiler_params=pltpu.CompilerParams(vmem_limit_bytes=VMEM_ASK),
        cost_estimate=pl.CostEstimate(
            flops=12_000_000_000, bytes_accessed=8_000_000, transcendentals=4_000_000
        ),
        name="cross_forward",
    )(segments, frames, queries, pooled, key_w, value_w, segments[:, None])


def self_forward_kernel(
    group, first_ref, q_ref, k_ref, v_ref, tag_ref, key_tag_ref,
    out_ref, extra_ref, mix_s, top_s, key_s, value_s,
):
    put_halves(key_s, group, k_ref[...], key_tag_ref[...].astype(f32))
    put_halves(value_s, group, v_ref[...], jnp.ones((BLOCK, PAIR), f32))
    left = lane_of(BLOCK) < HD
    half = lane_of(BLOCK) % HD
    row_at = lax.broadcasted_iota(jnp.int32, (BLOCK, BLOCK), 0)
    col_at = lax.broadcasted_iota(jnp.int32, (BLOCK, BLOCK), 1)
    every = [(pair, side) for pair in range(group) for side in range(2)]
    for block in range(q_ref.shape[0] // BLOCK):
        rows = pl.ds(block * BLOCK, BLOCK)
        tags = tag_ref[rows, :].astype(f32)
        queries = [
            halves(q_ref[rows, lanes_of(pair)].astype(f32) * SCALE, tags) for pair in range(group)
        ]
        scores = [dot_nt(queries[pair][side], key_s[pair, side, rows, :]) for pair, side in every]
        scores = [jnp.where(row_at >= col_at, score, -FAR) for score in scores]
        tops = [jnp.max(score, -1, keepdims=True) for score in scores]
        exps = [jnp.exp(score - top).astype(bf16) for score, top in zip(scores, tops)]
        for at, (pair, side) in enumerate(every):
            mix_s[at] = dot_nn(exps[at], value_s[pair, side, rows, :])
            top_s[at] = jnp.broadcast_to(tops[at], (BLOCK, PAIR))

        if block:

            def one_block(other, carry, queries=queries):
                own = pl.ds(pl.multiple_of(other * BLOCK, BLOCK), BLOCK)
                scores = [dot_nt(queries[pair][side], key_s[pair, side, own, :]) for pair, side in every]
                olds = [top_s[at] for at in range(len(every))]
                tops = [
                    jnp.maximum(old, jnp.max(score, -1, keepdims=True))
                    for old, score in zip(olds, scores)
                ]
                exps = [
                    jnp.exp(score - jnp.concatenate([top, top], 1)).astype(bf16)
                    for score, top in zip(scores, tops)
                ]
                for at, (pair, side) in enumerate(every):
                    mix_s[at] = mix_s[at] * jnp.exp(olds[at] - tops[at]) + dot_nn(
                        exps[at], value_s[pair, side, own, :]
                    )
                    top_s[at] = tops[at]
                return carry

            lax.fori_loop(first_ref[block], block, one_block, 0)

        for pair in range(group):
            mix_a, mix_b = mix_s[2 * pair], mix_s[2 * pair + 1]
            total = jnp.where(left, mix_b, mix_a)
            mixed = jnp.where(left, mix_a, mix_b) / pltpu.roll(total, HD, 1)
            log_sum = jnp.where(left, top_s[2 * pair + 1], top_s[2 * pair]) + jnp.log(total)
            out_ref[rows, lanes_of(pair)] = mixed.astype(bf16)
            extra_ref[rows, lanes_of(pair)] = tagged(tags, log_sum, half).astype(bf16)


def packed_spec(rows, group, third):
    return pl.BlockSpec((rows, PAIR * group), lambda p, *_: (0, p + third * (D // PAIR // group)))


def self_forward(first_blocks, packed, tags, key_tag):
    rows = packed.shape[0]
    group = FORWARD_GROUP
    return pl.pallas_call(
        functools.partial(self_forward_kernel, group),
        out_shape=(
            jax.ShapeDtypeStruct((rows, D), bf16),
            jax.ShapeDtypeStruct((rows, D), bf16),
        ),
        grid_spec=pltpu.PrefetchScalarGridSpec(
            num_scalar_prefetch=1,
            grid=(D // PAIR // group,),
            in_specs=[
                packed_spec(rows, group, 0), packed_spec(rows, group, 1), packed_spec(rows, group, 2),
                whole_spec((rows, PAIR)), whole_spec((rows, PAIR)),
            ],
            out_specs=[pair_spec(rows, group), pair_spec(rows, group)],
            scratch_shapes=[pltpu.VMEM((2 * group, BLOCK, PAIR), f32)] * 2
            + [pltpu.VMEM((group, 2, rows, PAIR), bf16)] * 2,
        ),
        compiler_params=pltpu.CompilerParams(vmem_limit_bytes=VMEM_ASK),
        cost_estimate=pl.CostEstimate(
            flops=12_000_000_000, bytes_accessed=8_000_000, transcendentals=4_000_000
        ),
        name="self_forward",
    )(first_blocks, packed, packed, packed, tags, key_tag)


def grad_rows(mixed, grad, left, half):
    product = mixed.astype(f32) * grad
    dot_a = jnp.sum(jnp.where(left, product, 0.0), -1, keepdims=True)
    dot_b = jnp.sum(jnp.where(left, 0.0, product), -1, keepdims=True)
    return halves(grad, tagged(jnp.zeros_like(product), jnp.where(left, dot_b, dot_a), half))


def back_step(group, own, queries, grads, turned, key_s, value_s, dq_s, dk_s, dv_s, left,
              masked=None, offset=None, fresh=False):
    every = [(pair, side) for pair in range(group) for side in range(2)]
    scores = [dot_nt(queries[pair][side], key_s[pair, side, own, :]) for pair, side in every]
    slopes = [dot_nt(grads[pair][side], value_s[pair, side, own, :]) for pair, side in every]
    if masked is not None:
        scores = [jnp.where(masked, score, -FAR) for score in scores]
    if offset is not None:
        scores = [score + offset for score in scores]
    probs = [jnp.exp(score) for score in scores]
    backs = [(prob * slope).astype(bf16) for prob, slope in zip(probs, slopes)]
    probs = [prob.astype(bf16) for prob in probs]
    for pair in range(group):
        back_a, back_b = backs[2 * pair : 2 * pair + 2]
        grad = jnp.where(
            left, dot_nn(back_a, key_s[pair, 0, own, :]), dot_nn(back_b, key_s[pair, 1, own, :])
        )
        if fresh:
            dq_s[pair] = grad
        else:
            dq_s[pair] += grad
        query_t, grad_t = turned[pair]
        for side in range(2):
            at = slice(side * HD, (side + 1) * HD)
            dk_s[pair, at, own] += dot_nn(query_t[at], backs[2 * pair + side])
            dv_s[pair, at, own] += dot_nn(grad_t[at], probs[2 * pair + side])


def back_operands(group, rows, q_ref, extra_ref, mixed_ref, grad_ref, left, half):
    queries, grads, turned = [], [], []
    for pair in range(group):
        at = (rows, lanes_of(pair))
        query = q_ref[at].astype(f32) * SCALE
        grad = grad_ref[at]
        queries.append(halves(query, extra_ref[at].astype(f32)))
        grads.append(grad_rows(mixed_ref[at], grad.astype(f32), left, half))
        turned.append((query.astype(bf16).T, grad.T))
    return queries, grads, turned


def cross_backward_kernel(
    group, seg_ref, frame_ref, q_ref, pooled_ref, key_w_ref, value_w_ref, extra_ref, mixed_ref,
    grad_ref, col_ref, dq_ref, dk_ref, dv_ref, key_s, value_s, dk_s, dv_s, dq_s,
):
    ones = ones_tags(BLOCK)
    put_halves(key_s, group, dot_nn(pooled_ref[...], key_w_ref[...]), ones)
    put_halves(value_s, group, dot_nn(pooled_ref[...], value_w_ref[...]), ones)
    dk_s[...] = jnp.zeros_like(dk_s)
    dv_s[...] = jnp.zeros_like(dv_s)
    left = lane_of(BLOCK) < HD
    half = lane_of(BLOCK) % HD
    for block in range(q_ref.shape[0] // BLOCK):
        rows = pl.ds(block * BLOCK, BLOCK)
        operands = back_operands(group, rows, q_ref, extra_ref, mixed_ref, grad_ref, left, half)
        dq_s[...] = jnp.zeros_like(dq_s)

        def one_clip(clip, carry, rows=rows, operands=operands):
            own = pl.ds(pl.multiple_of(frame_ref[clip] * KEYS, KEYS), KEYS)
            offset = jnp.where(col_ref[rows, :] == clip, 0.0, -FAR)
            back_step(group, own, *operands, key_s, value_s, dq_s, dk_s, dv_s, left, offset=offset)
            return carry

        lax.fori_loop(seg_ref[block * BLOCK], seg_ref[block * BLOCK + BLOCK - 1] + 1, one_clip, 0)
        for pair in range(group):
            dq_ref[rows, lanes_of(pair)] = (dq_s[pair] * SCALE).astype(bf16)
    for pair in range(group):
        dk_ref[lanes_of(pair), :] = dk_s[pair].astype(bf16)
        dv_ref[lanes_of(pair), :] = dv_s[pair].astype(bf16)


def cross_backward(segments, frames, queries, pooled, key_w, value_w, extra, mixed, grad):
    rows = queries.shape[0]
    keys = pooled.shape[0]
    group = BACKWARD_GROUP
    upright = pl.BlockSpec((PAIR * group, keys), lambda p, *_: (p, 0))
    own = pair_spec(rows, group)
    return pl.pallas_call(
        functools.partial(cross_backward_kernel, group),
        out_shape=(
            jax.ShapeDtypeStruct((rows, D), bf16),
            jax.ShapeDtypeStruct((D, keys), bf16),
            jax.ShapeDtypeStruct((D, keys), bf16),
        ),
        grid_spec=pltpu.PrefetchScalarGridSpec(
            num_scalar_prefetch=2,
            grid=(D // PAIR // group,),
            in_specs=[
                own,
                whole_spec(pooled.shape),
                pair_spec(key_w.shape[0], group),
                pair_spec(key_w.shape[0], group),
                own, own, own, whole_spec((rows, 1)),
            ],
            out_specs=[own, upright, upright],
            scratch_shapes=[pltpu.VMEM((group, 2, keys, PAIR), bf16)] * 2
            + [pltpu.VMEM((group, PAIR, keys), f32)] * 2
            + [pltpu.VMEM((group, BLOCK, PAIR), f32)],
        ),
        compiler_params=pltpu.CompilerParams(vmem_limit_bytes=VMEM_ASK),
        cost_estimate=pl.CostEstimate(
            flops=24_000_000_000, bytes_accessed=16_000_000, transcendentals=4_000_000
        ),
        name="cross_backward",
    )(segments, frames, queries, pooled, key_w, value_w, extra, mixed, grad, segments[:, None])


def self_backward_kernel(
    group, first_ref, q_ref, k_ref, v_ref, key_tag_ref, extra_ref, mixed_ref, grad_ref,
    dq_ref, dk_ref, dv_ref, key_s, value_s, dk_s, dv_s, dq_s,
):
    key_tag = key_tag_ref[...].astype(f32)
    put_halves(key_s, group, k_ref[...], key_tag)
    put_halves(value_s, group, v_ref[...], key_tag)
    dk_s[...] = jnp.zeros_like(dk_s)
    dv_s[...] = jnp.zeros_like(dv_s)
    left = lane_of(BLOCK) < HD
    half = lane_of(BLOCK) % HD
    row_at = lax.broadcasted_iota(jnp.int32, (BLOCK, BLOCK), 0)
    col_at = lax.broadcasted_iota(jnp.int32, (BLOCK, BLOCK), 1)
    for block in range(q_ref.shape[0] // BLOCK):
        rows = pl.ds(block * BLOCK, BLOCK)
        operands = back_operands(group, rows, q_ref, extra_ref, mixed_ref, grad_ref, left, half)
        back_step(
            group, rows, *operands, key_s, value_s, dq_s, dk_s, dv_s, left,
            masked=row_at >= col_at, fresh=True,
        )
        if block:

            def step(other, carry, operands=operands):
                own = pl.ds(pl.multiple_of(other * BLOCK, BLOCK), BLOCK)
                back_step(group, own, *operands, key_s, value_s, dq_s, dk_s, dv_s, left)
                return carry

            lax.fori_loop(first_ref[block], block, step, 0)
        for pair in range(group):
            dq_ref[rows, lanes_of(pair)] = (dq_s[pair] * SCALE).astype(bf16)
    for pair in range(group):
        dk_ref[:, lanes_of(pair)] = dk_s[pair].T.astype(bf16)
        dv_ref[:, lanes_of(pair)] = dv_s[pair].T.astype(bf16)


def self_backward(first_blocks, packed, key_tag, extra, mixed, grad):
    rows = packed.shape[0]
    group = BACKWARD_GROUP
    own = pair_spec(rows, group)
    return pl.pallas_call(
        functools.partial(self_backward_kernel, group),
        out_shape=(jax.ShapeDtypeStruct((rows, D), bf16),) * 3,
        grid_spec=pltpu.PrefetchScalarGridSpec(
            num_scalar_prefetch=1,
            grid=(D // PAIR // group,),
            in_specs=[
                packed_spec(rows, group, 0), packed_spec(rows, group, 1), packed_spec(rows, group, 2),
                whole_spec((rows, PAIR)),
                own, own, own,
            ],
            out_specs=[own] * 3,
            scratch_shapes=[pltpu.VMEM((group, 2, rows, PAIR), bf16)] * 2
            + [pltpu.VMEM((group, PAIR, rows), f32)] * 2
            + [pltpu.VMEM((group, BLOCK, PAIR), f32)],
        ),
        compiler_params=pltpu.CompilerParams(vmem_limit_bytes=VMEM_ASK),
        cost_estimate=pl.CostEstimate(
            flops=24_000_000_000, bytes_accessed=16_000_000, transcendentals=4_000_000
        ),
        name="self_backward",
    )(first_blocks, packed, packed, packed, key_tag, extra, mixed, grad)


def first_block_table(segment_row):
    clips = jnp.arange(CLIPS, dtype=jnp.int32)
    starts = jnp.sum((segment_row[:, None] < clips[None, :]).astype(jnp.int32), 0)
    heads = segment_row[::BLOCK]
    first = jnp.sum(jnp.where(heads[:, None] == clips[None, :], starts[None, :], 0), 1)
    return (first // BLOCK).astype(jnp.int32)


epsilon = 1e-05
ROOT = math.sqrt(2.0 / math.pi)
CUBE = 0.044715
C = 256
IMG = 64
POOL = 4


TILE = 256


def dot_tn(left, right):
    return lax.dot_general(left, right, (((0,), (0,)), ((), ())), preferred_element_type=f32)


def normalized(values):
    average = jnp.mean(values, -1, keepdims=True)
    centred = values - average
    spread = lax.rsqrt(jnp.mean(centred * centred, -1, keepdims=True) + epsilon)
    return centred * spread, spread


def norm_back(unit, spread, gain, grad):
    scaled = grad * gain
    mean_scaled = jnp.mean(scaled, -1, keepdims=True)
    mean_along = jnp.mean(scaled * unit, -1, keepdims=True)
    lead = tuple(range(grad.ndim - 1))
    return (
        (scaled - mean_scaled - unit * mean_along) * spread,
        jnp.sum(grad * unit, lead),
        jnp.sum(grad, lead),
    )


def gelu_and_slope(value):
    square = value * value
    bent = jnp.tanh(value * (ROOT + (ROOT * CUBE) * square))
    half = 0.5 + 0.5 * bent
    slope = half + value * (0.5 - 0.5 * bent * bent) * (ROOT + (3.0 * ROOT * CUBE) * square)
    return value * half, slope


def tiles_of(count):
    return [pl.ds(at, TILE) for at in range(0, count, TILE)]


def feed_forward_kernel(
    middle_ref, mixed_ref, join_ref, gain_ref, shift_ref, up_ref, bias_ref, down_ref, grad_ref,
    out_ref, second_ref, low_ref, mixed_grad_ref, join_grad_ref, gain_grad_ref, shift_grad_ref,
    bias_grad_ref, chunk_ref,
    normed_s, grad_t_s, back_s, hidden_s, pre_grad_s, up_s, down_s, sems,
):
    step = pl.program_id(0)
    steps = pl.num_programs(0)
    rows = middle_ref.shape[0]
    shares, deep = chunk_ref.shape[0], chunk_ref.shape[1] // 2
    group, narrow = D // deep, D // shares

    @pl.when(step == 0)
    def _():
        for at in tiles_of(rows):
            total = middle_ref[at, :] + dot_nn(mixed_ref[at, :], join_ref[...])
            out_ref[at, :] = total
            second_ref[at, :] = total
            unit, _ = normalized(total)
            normed_s[at, :] = (unit * gain_ref[...] + shift_ref[...]).astype(bf16)
            back_s[at, :] = jnp.zeros((TILE, D), f32)
            grad_t_s[:, at] = grad_ref[at, :].T

    bias_grad = jnp.zeros((1, D), f32)
    for at in tiles_of(rows):
        hidden, slope = gelu_and_slope(dot_nn(normed_s[at, :], up_ref[...]) + bias_ref[...])
        hidden = hidden.astype(bf16)
        hidden_s[at, :] = hidden
        pre_grad = (dot_nt(grad_ref[at, :], down_ref[...]) * slope).astype(bf16)
        pre_grad_s[at, :] = pre_grad
        bias_grad += jnp.sum(pre_grad.astype(f32), 0, keepdims=True)
        out_ref[at, :] += dot_nn(hidden, down_ref[...])
        back_s[at, :] += dot_nt(pre_grad, up_ref[...])
    bias_grad_ref[...] = bias_grad
    up_s[step] = dot_tn(pre_grad_s[...], normed_s[...]).astype(bf16).reshape(group, deep, D)
    down_s[step] = dot_nn(grad_t_s[...], hidden_s[...]).astype(bf16).reshape(shares, narrow, D)

    def copies(at):
        return (
            pltpu.make_async_copy(
                up_s.at[at], chunk_ref.at[pl.ds(at * group, group), pl.ds(0, deep)], sems.at[0, at]
            ),
            pltpu.make_async_copy(
                down_s.at[at],
                chunk_ref.at[:, pl.ds(pl.multiple_of(deep + at * narrow, 16), narrow)],
                sems.at[1, at],
            ),
        )

    for copy in copies(step):
        copy.start()

    @pl.when(step == steps - 1)
    def _():
        gain_grad = jnp.zeros((1, D), f32)
        shift_grad = jnp.zeros((1, D), f32)
        for at in tiles_of(rows):
            unit, spread = normalized(second_ref[at, :])
            part, one, two = norm_back(unit, spread, gain_ref[...], back_s[at, :])
            gain_grad += one[None]
            shift_grad += two[None]
            total = grad_ref[at, :].astype(f32) + part
            second_ref[at, :] = total
            low = total.astype(bf16)
            low_ref[at, :] = low
            mixed_grad_ref[at, :] = dot_nt(low, join_ref[...]).astype(bf16)
        gain_grad_ref[...] = gain_grad
        shift_grad_ref[...] = shift_grad
        join_grad_ref[...] = dot_tn(low_ref[...], mixed_ref[...]).astype(bf16)
        for at in range(FF // D):
            for copy in copies(at):
                copy.wait()


FF = 3072


def still(shape):
    return pl.BlockSpec(shape, lambda *_: (0,) * len(shape), pipeline_mode=pl.Buffered(1))


def feed_forward(middle, mixed, join, gain, shift, up, bias, down, grad, shares):
    rows = middle.shape[0]
    steps = FF // D
    deep = FF // shares
    tall = still((rows, D))
    row = still((1, D))
    return pl.pallas_call(
        feed_forward_kernel,
        out_shape=(
            jax.ShapeDtypeStruct((rows, D), f32),
            jax.ShapeDtypeStruct((rows, D), f32),
            jax.ShapeDtypeStruct((rows, D), bf16),
            jax.ShapeDtypeStruct((rows, D), bf16),
            jax.ShapeDtypeStruct((D, D), bf16),
            jax.ShapeDtypeStruct((1, D), f32),
            jax.ShapeDtypeStruct((1, D), f32),
            jax.ShapeDtypeStruct((1, FF), f32),
            jax.ShapeDtypeStruct((shares, 2 * deep, D), bf16),
        ),
        grid_spec=pltpu.PrefetchScalarGridSpec(
            num_scalar_prefetch=0,
            grid=(steps,),
            in_specs=[
                tall, tall, still((D, D)), row, row,
                pl.BlockSpec((D, D), lambda j: (0, j)),
                pl.BlockSpec((1, D), lambda j: (0, j)),
                pl.BlockSpec((D, D), lambda j: (j, 0)),
                tall,
            ],
            out_specs=[
                tall, tall, tall, tall, still((D, D)), row, row,
                pl.BlockSpec((1, D), lambda j: (0, j)),
                pl.BlockSpec(memory_space=pl.ANY),
            ],
            scratch_shapes=[
                pltpu.VMEM((rows, D), bf16),
                pltpu.VMEM((D, rows), bf16),
                pltpu.VMEM((rows, D), f32),
                pltpu.VMEM((rows, D), bf16),
                pltpu.VMEM((rows, D), bf16),
                pltpu.VMEM((steps, D // deep, deep, D), bf16),
                pltpu.VMEM((steps, shares, D // shares, D), bf16),
                pltpu.SemaphoreType.DMA((2, steps)),
            ],
        ),
        compiler_params=pltpu.CompilerParams(vmem_limit_bytes=56 * 2**20),
        cost_estimate=pl.CostEstimate(
            flops=34_000_000_000, bytes_accessed=40_000_000, transcendentals=3_200_000
        ),
        name="feed_forward",
    )(middle, mixed, join, gain[None], shift[None], up, bias[None], down, grad)


def project_back_kernel(
    query_ref, key_ref, value_ref, project_ref, middle_ref, second_ref, gain_ref, shift_ref,
    join_ref, mixed_ref,
    middle_grad_ref, mixed_grad_ref, project_grad_ref, join_grad_ref, gain_grad_ref, shift_grad_ref,
    normed_s, low_s,
):
    rows = middle_ref.shape[0]
    gain_grad = jnp.zeros((1, D), f32)
    shift_grad = jnp.zeros((1, D), f32)
    for at in tiles_of(rows):
        back = dot_nt(query_ref[at, :], project_ref[:, 0:D])
        back += dot_nt(key_ref[at, :], project_ref[:, D : 2 * D])
        back += dot_nt(value_ref[at, :], project_ref[:, 2 * D : 3 * D])
        unit, spread = normalized(middle_ref[at, :])
        normed_s[at, :] = (unit * gain_ref[...] + shift_ref[...]).astype(bf16)
        part, one, two = norm_back(unit, spread, gain_ref[...], back)
        gain_grad += one[None]
        shift_grad += two[None]
        total = second_ref[at, :] + part
        middle_grad_ref[at, :] = total
        low = total.astype(bf16)
        low_s[at, :] = low
        mixed_grad_ref[at, :] = dot_nt(low, join_ref[...]).astype(bf16)
    gain_grad_ref[...] = gain_grad
    shift_grad_ref[...] = shift_grad
    project_grad_ref[0:D] = dot_tn(query_ref[...], normed_s[...]).astype(bf16)
    project_grad_ref[D : 2 * D] = dot_tn(key_ref[...], normed_s[...]).astype(bf16)
    project_grad_ref[2 * D : 3 * D] = dot_tn(value_ref[...], normed_s[...]).astype(bf16)
    join_grad_ref[...] = dot_tn(low_s[...], mixed_ref[...]).astype(bf16)


def project_back(query, key, value, project, middle, second, gain, shift, join, mixed):
    rows = middle.shape[0]
    return pl.pallas_call(
        project_back_kernel,
        out_shape=(
            jax.ShapeDtypeStruct((rows, D), f32),
            jax.ShapeDtypeStruct((rows, D), bf16),
            jax.ShapeDtypeStruct((3 * D, D), bf16),
            jax.ShapeDtypeStruct((D, D), bf16),
            jax.ShapeDtypeStruct((1, D), f32),
            jax.ShapeDtypeStruct((1, D), f32),
        ),
        in_specs=[pl.BlockSpec(memory_space=pltpu.VMEM)] * 10,
        out_specs=[pl.BlockSpec(memory_space=pltpu.VMEM)] * 6,
        scratch_shapes=[pltpu.VMEM((rows, D), bf16), pltpu.VMEM((rows, D), bf16)],
        compiler_params=pltpu.CompilerParams(vmem_limit_bytes=56 * 2**20),
        cost_estimate=pl.CostEstimate(
            flops=10_000_000_000, bytes_accessed=30_000_000, transcendentals=2_000
        ),
        name="project_back",
    )(query, key, value, project, middle, second, gain[None], shift[None], join, mixed)


MESH = pl.DeviceIdType.MESH


def bits_of(count):
    return count.bit_length() - 1


def stream_steps(order, dp_bits, q_bits):
    dp_up = [("dp", b) for b in range(dp_bits)]
    dp_down = dp_up[::-1]
    q_steps = [("q", b) for b in range(q_bits)]
    return {"up": dp_up + q_steps, "down": dp_down + q_steps, "q_up": q_steps + dp_up}[order]


def cut_streams(rows, dp, orders):
    unit = 16 * dp
    units = rows // unit
    plan, at = [], 0
    for number, order in enumerate(orders):
        size = units // len(orders) + (number < units % len(orders))
        if size:
            plan.append((at * unit, size * unit, order))
            at += size
    return plan


def stream_scratch(plan, dp, row, partial):
    dp_bits, q_bits = bits_of(dp), bits_of(row // 2) if partial else 0
    shapes = []
    for _, rows, order in plan:
        lead = q_bits
        shapes.append(pltpu.VMEM((2,) * lead + (rows, D), bf16))
        if partial:
            shapes.append(pltpu.VMEM((2,) * lead + (rows, D), bf16))
        for kind, _ in stream_steps(order, dp_bits, q_bits):
            if kind == "dp":
                rows //= 2
            else:
                lead -= 1
            shapes.append(pltpu.VMEM((2,) * lead + (rows, D), bf16))
    return shapes


class Exchange:
    def __init__(self, dp, row, send_sem, recv_sem, local_sem):
        self.dp, self.row = dp, row
        self.dp_bits, self.q_bits = bits_of(dp), bits_of(row // 2)
        self.me_dp, self.me_row = lax.axis_index("dp"), lax.axis_index("row")
        self.core, self.me_q = lax.rem(self.me_row, 2), self.me_row // 2
        self.send_sem, self.recv_sem, self.local_sem = send_sem, recv_sem, local_sem
        self.remote, self.local, self.started = 0, 0, []

    def bit(self, step):
        kind, b = step
        return lax.rem((self.me_dp if kind == "dp" else self.me_q) // (2**b), 2)

    def partner(self, step):
        kind, b = step
        if kind == "core":
            return self.me_dp, self.me_row + 1 - 2 * self.core
        ahead = (2**b) * (1 - 2 * self.bit(step))
        if kind == "dp":
            return self.me_dp + ahead, self.me_row
        return self.me_dp, self.me_row + 2 * ahead

    def greet(self, devices):
        barrier = pltpu.get_barrier_semaphore()
        for device in devices:
            pl.semaphore_signal(barrier, inc=1, device_id=device, device_id_type=MESH)
        pl.semaphore_wait(barrier, len(devices))

    def push(self, src, dst, device):
        copy = pltpu.make_async_remote_copy(
            src_ref=src, dst_ref=dst, send_sem=self.send_sem.at[self.remote],
            recv_sem=self.recv_sem.at[self.remote], device_id=device, device_id_type=MESH,
        )
        self.remote += 1
        copy.start()
        self.started.append(copy)
        return copy

    def fetch(self, src, dst):
        copy = pltpu.make_async_copy(src, dst, self.local_sem.at[self.local])
        self.local += 1
        copy.start()
        return copy

    def end(self):
        for copy in self.started:
            copy.wait_send()


class Stream:
    def __init__(self, ex, scratch, rows, order, out_ref, out_at, partial):
        self.ex, self.rows, self.off = ex, rows, 0
        self.out_ref, self.out_at = out_ref, out_at
        q_bits = ex.q_bits if partial else 0
        self.q_bits = q_bits
        self.steps = stream_steps(order, ex.dp_bits, q_bits)
        self.todo = list(self.steps)
        self.back = [step for step in self.steps if step[0] == "dp"][::-1]
        self.acc = scratch.pop(0)
        self.landings = [scratch.pop(0) for _ in range(len(self.steps) + partial)]
        self.picked = [None] * q_bits
        self.copies, self.locals, self.landing = [], [], None
        self.gathering, self.done = False, False

    def start_partial(self, segments):
        ex, at = self.ex, 0
        every = (slice(None),) * self.q_bits
        self.landing = self.landings.pop(0)
        for piece, first, rows in segments:
            here = every + (pl.ds(at, rows),)
            there = (pl.ds(first, rows),)
            self.copies.append(
                ex.push(
                    piece.at[every + (1 - ex.core,) + there], self.landing.at[here],
                    ex.partner(("core", 0)),
                )
            )
            self.locals.append(ex.fetch(piece.at[every + (ex.core,) + there], self.acc.at[here]))
            at += rows

    def start_summed(self, source, first):
        self.ex.fetch(source.at[pl.ds(first, self.rows)], self.acc).wait()
        self.send_next()

    def index(self, off, rows):
        picks = tuple(slice(None) if p is None else p for p in self.picked)
        return picks + (pl.ds(pl.multiple_of(off, 16), rows),)

    def send_next(self):
        step = self.todo.pop(0)
        mine = self.ex.bit(step)
        landing = self.landings.pop(0)
        if step[0] == "dp":
            half = self.rows // 2
            src = self.acc.at[self.index(self.off + (1 - mine) * half, half)]
            self.off, self.rows = self.off + mine * half, half
        else:
            place = self.q_bits - 1 - step[1]
            self.picked[place] = 1 - mine
            src = self.acc.at[self.index(self.off, self.rows)]
            self.picked[place] = mine
        self.copies = [self.ex.push(src, landing, self.ex.partner(step))]
        self.landing = landing

    def add_landing(self):
        picks = self.index(0, 16)[:-1]
        lead = (slice(None),) * (len(self.landing.shape) - 2)

        def body(i, carry):
            own = picks + (pl.ds(pl.multiple_of(self.off + i * 16, 16), 16),)
            other = lead + (pl.ds(pl.multiple_of(i * 16, 16), 16),)
            self.acc[own] = (self.acc[own].astype(f32) + self.landing[other].astype(f32)).astype(bf16)
            return carry

        lax.fori_loop(0, self.rows // 16, body, 0)

    def gather_next(self):
        at = pl.ds(pl.multiple_of(self.out_at + self.off, 16), self.rows)
        step = self.back[0]
        self.copies = [self.ex.push(self.out_ref.at[at], self.out_ref.at[at], self.ex.partner(step))]

    def advance(self):
        for copy in self.locals:
            copy.wait()
        self.locals = []
        for copy in self.copies:
            copy.wait_recv()
        if self.gathering:
            step = self.back.pop(0)
            self.off = self.off - self.ex.bit(step) * self.rows
            self.rows *= 2
            if self.back:
                self.gather_next()
            else:
                self.done = True
            return
        self.add_landing()
        if self.todo:
            self.send_next()
            return
        at = pl.ds(pl.multiple_of(self.out_at + self.off, 16), self.rows)
        self.out_ref[at, :] = self.acc[self.index(self.off, self.rows)]
        self.gathering = True
        self.gather_next()


def drain(streams):
    while any(not stream.done for stream in streams):
        for stream in streams:
            if not stream.done:
                stream.advance()


def sum_shares_kernel(dp, row, plan, *refs):
    summed_ref, out_ref = refs[:2]
    scratch, (send_sem, recv_sem, local_sem) = list(refs[2:-3]), refs[-3:]
    ex = Exchange(dp, row, send_sem, recv_sem, local_sem)
    ex.greet([ex.partner(("dp", b)) for b in range(ex.dp_bits)])
    streams = []
    for first, rows, order in plan:
        stream = Stream(ex, scratch, rows, order, out_ref, first, 0)
        stream.start_summed(summed_ref, first)
        streams.append(stream)
    drain(streams)
    ex.end()


def sum_shares(summed, dp, row, orders):
    plan = cut_streams(summed.shape[0], dp, orders)
    copies = 2 * bits_of(dp) * len(plan)
    return pl.pallas_call(
        functools.partial(sum_shares_kernel, dp, row, plan),
        out_shape=jax.ShapeDtypeStruct(summed.shape, bf16),
        in_specs=[pl.BlockSpec(memory_space=pl.ANY)],
        out_specs=pl.BlockSpec(memory_space=pltpu.VMEM),
        scratch_shapes=stream_scratch(plan, dp, row, 0) + [
            pltpu.SemaphoreType.DMA((copies,)),
            pltpu.SemaphoreType.DMA((copies,)),
            pltpu.SemaphoreType.DMA((len(plan),)),
        ],
        compiler_params=pltpu.CompilerParams(
            collective_id=3, has_side_effects=True, vmem_limit_bytes=VMEM_ASK
        ),
        name="sum_shares",
    )(summed)


def row_of(lead, me_row):
    return lead + (me_row,)


def greet_row(row):
    me_dp, me_row = lax.axis_index("dp"), lax.axis_index("row")
    barrier = pltpu.get_barrier_semaphore()
    for ahead in range(1, row):
        pl.semaphore_signal(
            barrier, inc=1, device_id=(me_dp, lax.rem(me_row + ahead, row)), device_id_type=MESH
        )
    pl.semaphore_wait(barrier, row - 1)


def edge_copies(cells, above, below, send_sem, recv_sem, row):
    me_dp, me_row = lax.axis_index("dp"), lax.axis_index("row")
    here = cells.shape[1]
    onward = pltpu.make_async_remote_copy(
        src_ref=cells.at[:, here - 1], dst_ref=above, send_sem=send_sem.at[0],
        recv_sem=recv_sem.at[0], device_id=(me_dp, lax.rem(me_row + 1, row)), device_id_type=MESH,
    )
    back = pltpu.make_async_remote_copy(
        src_ref=cells.at[:, 0], dst_ref=below, send_sem=send_sem.at[1],
        recv_sem=recv_sem.at[1], device_id=(me_dp, lax.rem(me_row + row - 1, row)),
        device_id_type=MESH,
    )
    return onward, back


def start_edges(copies):
    for copy in copies:
        copy.start()


def end_edges(copies):
    for copy in copies:
        copy.wait_send()
        copy.wait_recv()


def put_wide(wide, frame, first, cells):
    column = lax.broadcasted_iota(jnp.int32, cells.shape, 0) % IMG
    cells = cells.astype(f32)
    count = cells.shape[0]
    left = jnp.where(column == 0, 0.0, pltpu.roll(cells, 1, 0))
    right = jnp.where(column == IMG - 1, 0.0, pltpu.roll(cells, count - 1, 0))
    at = pl.ds(first, count)
    wide[frame, at, 0:C] = left.astype(bf16)
    wide[frame, at, C : 2 * C] = cells.astype(bf16)
    wide[frame, at, 2 * C : 3 * C] = right.astype(bf16)


def put_edges(wide, above, below, here, row):
    me_row = lax.axis_index("row")
    keep_above = jnp.where(me_row > 0, 1.0, 0.0)
    keep_below = jnp.where(me_row < row - 1, 1.0, 0.0)
    for frame in range(wide.shape[0]):
        put_wide(wide, frame, 0, above[frame].astype(f32) * keep_above)
        put_wide(wide, frame, (here + 1) * IMG, below[frame].astype(f32) * keep_below)


def conv_forward_kernel(
    row, frames_ref, taps_ref, bias_ref, gain_ref, shift_ref,
    pre_ref, wide_ref, every_ref,
    above_s, below_s, pool_s, edge_send, edge_recv, send_sem, recv_sem,
):
    me_dp, me_row = lax.axis_index("dp"), lax.axis_index("row")
    core, me_q, places = lax.rem(me_row, 2), me_row // 2, row // 2
    count, here = frames_ref.shape[0], frames_ref.shape[1]
    greet_row(row)
    edges = edge_copies(frames_ref, above_s, below_s, edge_send, edge_recv, row)
    start_edges(edges)
    for frame in range(count):
        put_wide(wide_ref, frame, IMG, frames_ref[frame].reshape(here * IMG, C))
    end_edges(edges)
    put_edges(wide_ref, above_s, below_s, here, row)
    tile = POOL * IMG
    for frame in range(count):
        for part in range(here // POOL):
            first = part * tile
            pre = bias_ref[...] + dot_nn(wide_ref[frame, pl.ds(first, tile), :], taps_ref[0])
            pre += dot_nn(wide_ref[frame, pl.ds(first + IMG, tile), :], taps_ref[1])
            pre += dot_nn(wide_ref[frame, pl.ds(first + 2 * IMG, tile), :], taps_ref[2])
            pre_ref[frame, pl.ds(first, tile), :] = pre
            active, _ = gelu_and_slope(pre)
            unit, _ = normalized(active)
            normed = unit * gain_ref[...] + shift_ref[...]
            lines = normed.reshape(POOL, IMG, C)
            lines = lines[0] + lines[1] + lines[2] + lines[3]
            cells = IMG // POOL
            for side in range(C // PAIR):
                lanes = slice(side * PAIR, (side + 1) * PAIR)
                pool_s[side] = lines[:, lanes]
                total = pool_s[side, pl.ds(0, cells, stride=POOL), :]
                for at in range(1, POOL):
                    total += pool_s[side, pl.ds(at, cells, stride=POOL), :]
                every_ref[frame, me_row, pl.ds(part * cells, cells), lanes] = (
                    total * (1.0 / (POOL * POOL))
                ).astype(bf16)

    def push(source_row, to_row, at):
        copy = pltpu.make_async_remote_copy(
            src_ref=every_ref.at[:, source_row], dst_ref=every_ref.at[:, source_row],
            send_sem=send_sem.at[at], recv_sem=recv_sem.at[at], device_id=(me_dp, to_row),
            device_id_type=MESH,
        )
        copy.start()
        return copy

    other = me_row + 1 - 2 * core
    copies = [push(me_row, other, 0)]
    for ahead in range(1, places):
        copies.append(push(me_row, lax.rem(me_q + ahead, places) * 2 + core, ahead))
    for ahead in range(1, places):
        copies[ahead].wait_recv()
        came = lax.rem(me_q + places - ahead, places) * 2 + core
        copies.append(push(came, other, places - 1 + ahead))
    copies[0].wait_recv()
    for copy in copies[places:]:
        copy.wait_recv()
    for copy in copies:
        copy.wait_send()


def conv_forward(frames, taps, bias, gain, shift, row):
    count, here = frames.shape[0], frames.shape[1]
    keys = (here // POOL) * (IMG // POOL)
    return pl.pallas_call(
        functools.partial(conv_forward_kernel, row),
        out_shape=(
            jax.ShapeDtypeStruct((count, here * IMG, C), f32),
            jax.ShapeDtypeStruct((count, (here + 2) * IMG, 3 * C), bf16),
            jax.ShapeDtypeStruct((count, row, keys, C), bf16),
        ),
        in_specs=[pl.BlockSpec(memory_space=pltpu.VMEM)] * 5,
        out_specs=[pl.BlockSpec(memory_space=pltpu.VMEM)] * 3,
        scratch_shapes=[
            pltpu.VMEM((count, IMG, C), bf16),
            pltpu.VMEM((count, IMG, C), bf16),
            pltpu.VMEM((C // PAIR, IMG, PAIR), f32),
            pltpu.SemaphoreType.DMA((2,)),
            pltpu.SemaphoreType.DMA((2,)),
            pltpu.SemaphoreType.DMA((row,)),
            pltpu.SemaphoreType.DMA((row,)),
        ],
        compiler_params=pltpu.CompilerParams(
            collective_id=1, has_side_effects=True, vmem_limit_bytes=VMEM_ASK
        ),
        name="conv_forward",
    )(frames, taps.reshape(3, 3 * C, C), bias[None], gain[None], shift[None])


READY_ORDERS = ("up", "down", "q_up", "up", "down")
CROSS_ORDERS = ("q_up", "up", "down")
FILTER_ORDERS = ("up", "down")


def segments_of(pieces, first, rows):
    parts, at = [], 0
    for piece, start, count in pieces:
        low, high = max(first, at), min(first + rows, at + count)
        if low < high:
            parts.append((piece, start + low - at, high - low))
        at += count
    return parts


def finish_kernel(
    dp, row, plans,
    project_ref, join_ref, cross_join_ref, query_grad_ref, x_ref, query_w_ref, middle_grad_ref,
    keys_grad_ref, values_grad_ref, every_ref, key_w_ref, value_w_ref, pre_ref, wide_ref, taps_ref,
    gain_ref, small_ref,
    tokens_grad_ref, frames_grad_ref, share_ref,
    query_s, both_s, filter_s, x_s, query_w_s, pre_s, wide_in_s, taps_s,
    part_s, landing_s, sum_s, arrive_s, spread_s, grad_s, grad_t_s, wide_s, above_s, below_s,
    edge_send, edge_recv, send_sem, recv_sem, local_sem, *scratch,
):
    scratch = list(scratch)
    ex = Exchange(dp, row, send_sem, recv_sem, local_sem)
    me_dp, me_row, core, me_q, places = ex.me_dp, ex.me_row, ex.core, ex.me_q, row // 2
    count, here = grad_s.shape[0], grad_s.shape[1]
    keys = part_s.shape[3]
    model, own = D // row, C // row
    ex.greet(
        [(me_dp, lax.rem(me_row + ahead, row)) for ahead in range(1, row)]
        + [ex.partner(("dp", b)) for b in range(ex.dp_bits)]
    )
    base, groups = 0, []
    for plan in plans:
        groups.append([
            Stream(ex, scratch, rows, order, share_ref, base + first, 1) for first, rows, order in plan
        ])
        base += sum(rows for _, rows, _ in plan)
    ready, crossed, filtered = groups

    def start(group, plan, pieces):
        for stream, (first, rows, _) in zip(group, plan):
            stream.start_partial(segments_of(pieces, first, rows))

    used = 5 * model
    total_rows = sum(rows for _, rows, _ in plans[0])
    start(ready, plans[0], [
        (project_ref, 0, 3 * model), (join_ref, 0, model), (cross_join_ref, 0, model),
        (project_ref, 0, total_rows - used),
    ])
    x_in = ex.fetch(x_ref, x_s)
    query_in = ex.fetch(query_w_ref, query_w_s)
    pre_in = ex.fetch(pre_ref, pre_s)
    wide_in = ex.fetch(wide_ref, wide_in_s)
    taps_in = ex.fetch(taps_ref, taps_s)

    part = lax.dot_general(
        keys_grad_ref[...], key_w_ref[...], (((0,), (1,)), ((), ())), preferred_element_type=f32
    )
    part += lax.dot_general(
        values_grad_ref[...], value_w_ref[...], (((0,), (1,)), ((), ())), preferred_element_type=f32
    )
    part_s[...] = part.astype(bf16).reshape(count, places, 2, keys, C)
    pooled_core = ex.push(part_s.at[:, :, 1 - core], landing_s, ex.partner(("core", 0)))

    split = (2,) * ex.q_bits + (2,)
    lines = both_s.shape[-2]
    for at, grad_ref in enumerate((keys_grad_ref, values_grad_ref)):
        both_s[..., 0:model, at * C : (at + 1) * C] = (
            dot_nn(grad_ref[...], every_ref[...]).astype(bf16).reshape(split + (model, C))
        )
    both_s[..., 0:model, 2 * C : 3 * C] = jnp.zeros(split + (model, C), bf16)
    if lines > model:
        both_s[..., model:lines, :] = jnp.zeros(split + (lines - model, D), bf16)
    x_in.wait()
    query_s[...] = dot_tn(query_grad_ref[...], x_s[...]).astype(bf16).reshape(split + (model, D))
    start(crossed, plans[1], [(query_s, 0, model), (both_s, 0, lines)])

    pooled_core.wait_recv()
    sum_s[...] = (part_s[:, :, core].astype(f32) + landing_s[...].astype(f32)).astype(bf16)
    pooled_in = []
    for ahead in range(1, places):
        to = lax.rem(me_q + ahead, places)
        pooled_in.append(ex.push(sum_s.at[:, to], arrive_s.at[ahead - 1], (me_dp, to * 2 + core)))
    for stream in ready:
        stream.advance()
    query_in.wait()
    for at in tiles_of(x_s.shape[0]):
        tokens_grad_ref[at, :] = middle_grad_ref[at, :] + dot_nt(query_grad_ref[at, :], query_w_s[...])
    for copy in pooled_in:
        copy.wait_recv()
    pooled = sum_s[:, me_q].astype(f32)
    for ahead in range(1, places):
        pooled += arrive_s[ahead - 1].astype(f32)
    pooled = pooled * (1.0 / (POOL * POOL))
    for stream in crossed:
        stream.advance()

    tile = POOL * IMG
    cells = IMG // POOL
    bias_grad = jnp.zeros((1, C), f32)
    gain_grad = jnp.zeros((1, C), f32)
    shift_grad = jnp.zeros((1, C), f32)
    pre_in.wait()
    for frame in range(count):
        for part in range(here // POOL):
            for side in range(C // PAIR):
                own_cells = pooled[
                    frame, part * cells : (part + 1) * cells, side * PAIR : (side + 1) * PAIR
                ]
                for at in range(POOL):
                    spread_s[side, pl.ds(at, cells, stride=POOL), :] = own_cells
            line = jnp.concatenate([spread_s[side] for side in range(C // PAIR)], 1)
            back = jnp.broadcast_to(line[None], (POOL, IMG, C)).reshape(tile, C)
            active, slope = gelu_and_slope(pre_s[frame, pl.ds(part * tile, tile), :])
            unit, spread = normalized(active)
            grad, one, two = norm_back(unit, spread, gain_ref[...], back)
            gain_grad += one[None]
            shift_grad += two[None]
            grad = (slope * grad).astype(bf16)
            bias_grad += jnp.sum(grad.astype(f32), 0, keepdims=True)
            grad_s[frame, pl.ds(part * POOL, POOL)] = grad.reshape(POOL, IMG, C)
    edges = edge_copies(grad_s, above_s, below_s, edge_send, edge_recv, row)
    start_edges(edges)
    for frame in range(count):
        cells_here = grad_s[frame].reshape(here * IMG, C)
        put_wide(wide_s, frame, IMG, cells_here)
        grad_t_s[frame] = cells_here.T
    for stream in ready[:3]:
        stream.advance()
    wide_in.wait()
    for dy in range(3):
        total = None
        for frame in range(count):
            piece = dot_nn(grad_t_s[frame], wide_in_s[frame, pl.ds(dy * IMG, here * IMG), :])
            total = piece if total is None else total + piece
        filter_s[..., dy * own : (dy + 1) * own, :] = total.astype(bf16).reshape(split + (own, D))
    lines = filter_s.shape[-2] - 3 * own
    line_at = lax.broadcasted_iota(jnp.int32, (lines, D), 0)
    extra = jnp.zeros((lines, D), f32)
    for at, item in enumerate((bias_grad, gain_grad, shift_grad)):
        item = jnp.concatenate([item, jnp.zeros((1, D - C), f32)], 1)
        extra = jnp.where(line_at == 8 + at, item, extra)
    for place in range(places):
        for side in range(2):
            index = tuple((place >> b) & 1 for b in reversed(range(ex.q_bits))) + (side,)
            own_small = small_ref[place * 2 + side].astype(f32)
            filter_s[index + (slice(3 * own, 3 * own + lines),)] = (own_small + extra).astype(bf16)
    start(filtered, plans[2], [(filter_s, 0, 3 * own + lines)])
    for stream in ready[3:] + crossed:
        stream.advance()
    end_edges(edges)
    put_edges(wide_s, above_s, below_s, here, row)
    taps_in.wait()
    for frame in range(count):
        for part in range(here // POOL):
            total = None
            for tap in range(9):
                dy, dx = tap // 3, tap % 3
                window = wide_s[frame, pl.ds(part * tile + dy * IMG, tile), dx * C : (dx + 1) * C]
                piece = dot_nt(window, taps_s[8 - tap])
                total = piece if total is None else total + piece
            frames_grad_ref[frame, pl.ds(part * tile, tile), :] = total
        if frame == 0:
            for stream in filtered:
                stream.advance()
        if frame == 1:
            for stream in ready:
                stream.advance()
    drain(filtered + ready + crossed)
    ex.end()


def finish(project_grad, join_grad, cross_join_grad, query_grad, x, query_w, middle_grad,
           keys_grad_t, values_grad_t, everyone, key_w, value_w, pre, wide, taps, gain, small, dp, row):
    unit = 16 * dp
    model, own = D // row, C // row
    count, here = pre.shape[0], pre.shape[1] // IMG
    keys = (here // POOL) * (IMG // POOL)
    whole_units = lambda rows: -(-rows // unit) * unit
    rows = [whole_units(5 * model), whole_units(2 * model), 3 * own + small.shape[1]]
    plans = [
        cut_streams(count_rows, dp, orders)
        for count_rows, orders in zip(rows, (READY_ORDERS, CROSS_ORDERS, FILTER_ORDERS))
    ]
    split = (2,) * bits_of(row // 2) + (2,)
    view = lambda piece: piece.reshape(split + (piece.shape[0] // row, D))
    streams = [stream for plan in plans for stream in plan]
    per_stream = 2 * bits_of(dp) + bits_of(row // 2)
    remote = per_stream * len(streams) + 8 * len(streams) + row
    local = 8 * len(streams) + 8
    vmem = pl.BlockSpec(memory_space=pltpu.VMEM)
    away = pl.BlockSpec(memory_space=pl.ANY)
    return pl.pallas_call(
        functools.partial(finish_kernel, dp, row, plans),
        out_shape=(
            jax.ShapeDtypeStruct(x.shape, f32),
            jax.ShapeDtypeStruct(pre.shape, f32),
            jax.ShapeDtypeStruct((sum(rows), D), bf16),
        ),
        in_specs=[
            away, away, away, vmem, away, away, vmem, vmem, vmem, vmem, vmem, vmem, away, away, away,
            vmem, vmem,
        ],
        out_specs=[vmem] * 3,
        scratch_shapes=[
            pltpu.VMEM(split + (model, D), bf16),
            pltpu.VMEM(split + (rows[1] - model, D), bf16),
            pltpu.VMEM(split + (rows[2], D), bf16),
            pltpu.VMEM(x.shape, bf16),
            pltpu.VMEM(query_w.shape, bf16),
            pltpu.VMEM(pre.shape, f32),
            pltpu.VMEM(wide.shape, bf16),
            pltpu.VMEM(taps.shape, bf16),
            pltpu.VMEM((count, row // 2, 2, keys, C), bf16),
            pltpu.VMEM((count, row // 2, keys, C), bf16),
            pltpu.VMEM((count, row // 2, keys, C), bf16),
            pltpu.VMEM((row // 2 - 1, count, keys, C), bf16),
            pltpu.VMEM((C // PAIR, IMG, PAIR), f32),
            pltpu.VMEM((count, here, IMG, C), bf16),
            pltpu.VMEM((count, C, here * IMG), bf16),
            pltpu.VMEM((count, (here + 2) * IMG, 3 * C), bf16),
            pltpu.VMEM((count, IMG, C), bf16),
            pltpu.VMEM((count, IMG, C), bf16),
            pltpu.SemaphoreType.DMA((2,)),
            pltpu.SemaphoreType.DMA((2,)),
            pltpu.SemaphoreType.DMA((remote,)),
            pltpu.SemaphoreType.DMA((remote,)),
            pltpu.SemaphoreType.DMA((local,)),
        ] + [shape for plan in plans for shape in stream_scratch(plan, dp, row, 1)],
        compiler_params=pltpu.CompilerParams(
            collective_id=2, has_side_effects=True, vmem_limit_bytes=58 * 2**20
        ),
        name="finish",
    )(
        view(project_grad), view(join_grad), view(cross_join_grad), query_grad, x, query_w,
        middle_grad, keys_grad_t, values_grad_t, everyone, key_w, value_w, pre, wide, taps,
        gain[None], small,
    )


def fast_dot(left, right):
    return jnp.dot(left, right, preferred_element_type=f32)


def shared_rows(matrix, count):
    return matrix.reshape(count, matrix.shape[0] // count, matrix.shape[1])


def on_device(
    frames, tokens, segment_ids, clip_frame, filter_weight, filter_bias, context_gain,
    context_shift, cross_query, cross_key, cross_value, cross_output, first_gain, first_shift,
    self_project, self_output, second_gain, second_shift, up_weight, up_bias, down_weight, cotangent,
):
    shares = lax.axis_size("row")
    x = tokens[0]
    segments = segment_ids[0]
    clip_frames = clip_frame[0]
    out_grad = cotangent[0]
    tags = segment_tags(segments)
    key_tag = key_tags(segments)
    first_blocks = first_block_table(segments)

    pre_act, wide, everyone = conv_forward(
        frames, filter_weight, filter_bias, context_gain, context_shift, shares
    )
    everyone = everyone.reshape(-1, C)
    cross_q = fast_dot(x, cross_query).astype(bf16)
    cross_mixed, cross_extra = cross_forward(
        segments, clip_frames, cross_q, everyone, cross_key, cross_value
    )
    middle = x.astype(f32) + fast_dot(cross_mixed, cross_output)
    first_unit, first_spread = normalized(middle)
    first_normed = (first_unit * first_gain + first_shift).astype(bf16)
    packed = fast_dot(first_normed, self_project).astype(bf16)
    self_mixed, self_extra = self_forward(first_blocks, packed, tags, key_tag)
    (
        output, second_grad, second_low, self_mixed_grad, join_grad, second_gain_grad,
        second_shift_grad, up_bias_grad, chunk_a,
    ) = feed_forward(
        middle, self_mixed, self_output, second_gain, second_shift, up_weight, up_bias, down_weight,
        out_grad, shares,
    )
    share_a = lax.psum_scatter(chunk_a, "row", scatter_dimension=0, tiled=False)
    query_grad, key_grad, value_grad = self_backward(
        first_blocks, packed, key_tag, self_extra, self_mixed, self_mixed_grad
    )
    (
        middle_grad, cross_mixed_grad, project_grad, cross_join_grad, first_gain_grad,
        first_shift_grad,
    ) = project_back(
        query_grad, key_grad, value_grad, self_project, middle, second_grad, first_gain, first_shift,
        cross_output, cross_mixed,
    )
    cross_q_grad, keys_grad_t, values_grad_t = cross_backward(
        segments, clip_frames, cross_q, everyone, cross_key, cross_value, cross_extra, cross_mixed,
        cross_mixed_grad,
    )
    dp = lax.axis_size("dp")
    small = jnp.concatenate(
        [
            item.astype(bf16).reshape(shares, -1)
            for item in (
                first_gain_grad, first_shift_grad, second_gain_grad, second_shift_grad, up_bias_grad,
            )
        ],
        1,
    )
    lines = 16 + -(3 * C // shares + 16) % (16 * dp)
    small = jnp.pad(small, ((0, 0), (0, lines * D - small.shape[1]))).reshape(shares, lines, D)
    tokens_grad, frames_grad, reduced = finish(
        project_grad, join_grad, cross_join_grad, cross_q_grad, x, cross_query, middle_grad,
        keys_grad_t, values_grad_t, everyone, cross_key, cross_value, pre_act, wide, filter_weight,
        context_gain, small, dp, shares,
    )
    share_a = sum_shares(share_a, dp, shares, ("up", "down"))
    cross_at = reduced.shape[0] - (3 * C // shares + lines)
    cross_at = cross_at - -(-2 * D // shares // (16 * dp)) * 16 * dp
    share_b = reduced[:cross_at]
    share_c = reduced[cross_at:]

    wide_part, model_part, own_part = 3072 // shares, D // shares, C // shares
    up_grad = share_a[:wide_part].astype(f32).T
    down_grad = jnp.concatenate(
        [
            share_a[wide_part + part * model_part : wide_part + (part + 1) * model_part].T
            for part in range(4)
        ],
        0,
    ).astype(f32)
    project_grad = share_b[: 3 * model_part].astype(f32).T
    self_output_grad = share_b[3 * model_part : 4 * model_part].astype(f32).T
    cross_output_grad = share_b[4 * model_part : 5 * model_part].astype(f32).T
    cross_query_grad = share_c[:model_part].astype(f32).T
    both = share_c[model_part : 2 * model_part].astype(f32)
    cross_key_grad = both[:, :C].T
    cross_value_grad = both[:, C : 2 * C].T
    late = reduced[reduced.shape[0] - (3 * own_part + lines) :].astype(f32)
    filter_grad = jnp.concatenate(
        [
            jnp.transpose(late[dy * own_part : (dy + 1) * own_part].reshape(own_part, 3, C), (1, 2, 0))
            for dy in range(3)
        ],
        0,
    )
    late = late[3 * own_part :]
    flat = late[:2].reshape(-1)
    sizes = [model_part] * 4 + [wide_part]
    ends = [sum(sizes[: i + 1]) for i in range(len(sizes))]
    vectors = [flat[e - s : e] for e, s in zip(ends, sizes)]
    mine = lax.dynamic_slice_in_dim(late[8:11, :C], lax.axis_index("row") * own_part, own_part, 1)
    vectors = vectors + [mine[0], mine[1], mine[2]]
    return (
        middle[None],
        output[None],
        tokens_grad[None],
        frames_grad.reshape(frames.shape),
        filter_grad,
        vectors[5],
        vectors[6],
        vectors[7],
        cross_query_grad,
        cross_key_grad,
        cross_value_grad,
        cross_output_grad,
        vectors[0],
        vectors[1],
        project_grad,
        self_output_grad,
        vectors[2],
        vectors[3],
        up_grad,
        vectors[4],
        down_grad,
    )


def solution(mesh):
    whole = P()
    by_row = P(("dp", "row"), None, None)
    in_specs = (
        P("dp", "row", None, None),
        by_row,
        P(("dp", "row"), None),
        P(("dp", "row"), None),
    ) + (whole,) * 17 + (by_row,)
    columns = P(None, "row")
    vector = P("row")
    out_specs = (
        by_row, by_row, by_row, P("dp", "row", None, None), P(None, None, "row"), vector, vector,
        vector, columns, columns, columns, columns, vector, vector, columns, columns, vector, vector,
        columns, vector, columns,
    )
    return jax.shard_map(
        on_device, mesh=mesh, in_specs=in_specs, out_specs=out_specs, check_vma=False
    )
```

```python
import functools
import math
import jax
import jax.numpy as jnp
from jax import lax
from jax.experimental import pallas as pl
from jax.experimental.pallas import tpu as pltpu
from jax.sharding import PartitionSpec as P

D = 768
HD = 64
PAIR = 128
BLOCK = 256
KEYS = 256
CLIPS = 4
FAR = 2.0**100
SCALE = 0.125
CROSS_GROUP = 6
FORWARD_GROUP = 3
BACKWARD_GROUP = 3
f32 = jnp.float32
bf16 = jnp.bfloat16
VMEM_ASK = 48 * 2**20


def lane_of(rows):
    return lax.broadcasted_iota(jnp.int32, (rows, PAIR), 1)


def dot_nt(left, right):
    return lax.dot_general(left, right, (((1,), (1,)), ((), ())), preferred_element_type=f32)


def dot_nn(left, right):
    return lax.dot_general(left, right, (((1,), (0,)), ((), ())), preferred_element_type=f32)


def tagged(extra, value, half):
    high = value.astype(bf16).astype(f32)
    rest = value - high
    middle = rest.astype(bf16).astype(f32)
    extra = jnp.where(half == 8, -high, extra)
    extra = jnp.where(half == 9, -middle, extra)
    return jnp.where(half == 10, middle - rest, extra)


def segment_tags(segment_row):
    lane = jnp.arange(PAIR, dtype=jnp.int32) % HD
    wrong = (lane[None, :] < CLIPS) & (lane[None, :] != segment_row[:, None])
    return jnp.where(wrong, -FAR, 0.0).astype(bf16)


def key_tags(segment_row):
    lane = jnp.arange(PAIR, dtype=jnp.int32) % HD
    ones = (lane[None, :] == segment_row[:, None]) | ((lane[None, :] >= 8) & (lane[None, :] <= 10))
    return jnp.where(ones, 1.0, 0.0).astype(bf16)


def ones_tags(rows):
    half = lane_of(rows) % HD
    return jnp.where((half >= 8) & (half <= 10), 1.0, 0.0)


def halves(value, filler):
    left = lane_of(value.shape[0]) < HD
    value = value.astype(f32)
    return jnp.where(left, value, filler).astype(bf16), jnp.where(left, filler, value).astype(bf16)


def put_halves(store, group, value, filler):
    for pair in range(group):
        for at in range(0, value.shape[0], BLOCK):
            rows = slice(at, at + BLOCK)
            fill = filler if filler.shape[0] == BLOCK else filler[rows, :]
            one, two = halves(value[rows, pair * PAIR : (pair + 1) * PAIR], fill)
            store[pair, 0, rows, :] = one
            store[pair, 1, rows, :] = two


def lanes_of(pair):
    return slice(pair * PAIR, (pair + 1) * PAIR)


def cross_forward_kernel(
    group, seg_ref, frame_ref, q_ref, pooled_ref, key_w_ref, value_w_ref, col_ref,
    out_ref, extra_ref, key_s, value_s,
):
    put_halves(key_s, group, dot_nn(pooled_ref[...], key_w_ref[...]), jnp.zeros((BLOCK, PAIR), f32))
    put_halves(value_s, group, dot_nn(pooled_ref[...], value_w_ref[...]), jnp.ones((BLOCK, PAIR), f32))
    left = lane_of(BLOCK) < HD
    half = lane_of(BLOCK) % HD
    for block in range(q_ref.shape[0] // BLOCK):
        rows = pl.ds(block * BLOCK, BLOCK)
        queries = [
            (q_ref[rows, lanes_of(pair)].astype(f32) * SCALE).astype(bf16) for pair in range(group)
        ]

        def one_clip(clip, carry, rows=rows, queries=queries):
            own = pl.ds(pl.multiple_of(frame_ref[clip] * KEYS, KEYS), KEYS)
            mine = col_ref[rows, :] == clip
            scores = [
                dot_nt(queries[pair], key_s[pair, side, own, :])
                for pair in range(group)
                for side in range(2)
            ]
            tops = [jnp.max(score, -1, keepdims=True) for score in scores]
            exps = [jnp.exp(score - top).astype(bf16) for score, top in zip(scores, tops)]
            mixes = [
                dot_nn(exps[2 * pair + side], value_s[pair, side, own, :])
                for pair in range(group)
                for side in range(2)
            ]
            for pair in range(group):
                mix_a, mix_b = mixes[2 * pair : 2 * pair + 2]
                top_a, top_b = tops[2 * pair : 2 * pair + 2]
                total = jnp.where(left, mix_b, mix_a)
                mixed = jnp.where(left, mix_a, mix_b) / pltpu.roll(total, HD, 1)
                log_sum = jnp.where(left, top_b, top_a) + jnp.log(total)
                extra = tagged(jnp.zeros((BLOCK, PAIR), f32), log_sum, half)
                at = (rows, lanes_of(pair))
                out_ref[at] = jnp.where(mine, mixed, out_ref[at].astype(f32)).astype(bf16)
                extra_ref[at] = jnp.where(mine, extra, extra_ref[at].astype(f32)).astype(bf16)
            return carry

        lax.fori_loop(seg_ref[block * BLOCK], seg_ref[block * BLOCK + BLOCK - 1] + 1, one_clip, 0)


def pair_spec(rows, group):
    return pl.BlockSpec((rows, PAIR * group), lambda p, *_: (0, p))


def whole_spec(shape):
    return pl.BlockSpec(shape, lambda p, *_: (0,) * len(shape), pipeline_mode=pl.Buffered(1))


def cross_forward(segments, frames, queries, pooled, key_w, value_w):
    rows = queries.shape[0]
    keys = pooled.shape[0]
    group = CROSS_GROUP
    return pl.pallas_call(
        functools.partial(cross_forward_kernel, group),
        out_shape=(
            jax.ShapeDtypeStruct((rows, D), bf16),
            jax.ShapeDtypeStruct((rows, D), bf16),
        ),
        grid_spec=pltpu.PrefetchScalarGridSpec(
            num_scalar_prefetch=2,
            grid=(D // PAIR // group,),
            in_specs=[
                pair_spec(rows, group),
                whole_spec(pooled.shape),
                pair_spec(key_w.shape[0], group),
                pair_spec(key_w.shape[0], group),
                whole_spec((rows, 1)),
            ],
            out_specs=[pair_spec(rows, group), pair_spec(rows, group)],
            scratch_shapes=[pltpu.VMEM((group, 2, keys, PAIR), bf16)] * 2,
        ),
        compiler_params=pltpu.CompilerParams(vmem_limit_bytes=34 * 2**20),
        cost_estimate=pl.CostEstimate(
            flops=12_000_000_000, bytes_accessed=8_000_000, transcendentals=4_000_000
        ),
        name="cross_forward",
    )(segments, frames, queries, pooled, key_w, value_w, segments[:, None])


def self_forward_kernel(
    group, first_ref, q_ref, k_ref, v_ref, tag_ref, key_tag_ref,
    out_ref, extra_ref, mix_s, top_s, key_s, value_s,
):
    put_halves(key_s, group, k_ref[...], key_tag_ref[...].astype(f32))
    put_halves(value_s, group, v_ref[...], jnp.ones((BLOCK, PAIR), f32))
    left = lane_of(BLOCK) < HD
    half = lane_of(BLOCK) % HD
    row_at = lax.broadcasted_iota(jnp.int32, (BLOCK, BLOCK), 0)
    col_at = lax.broadcasted_iota(jnp.int32, (BLOCK, BLOCK), 1)
    every = [(pair, side) for pair in range(group) for side in range(2)]
    for block in range(q_ref.shape[0] // BLOCK):
        rows = pl.ds(block * BLOCK, BLOCK)
        tags = tag_ref[rows, :].astype(f32)
        queries = [
            halves(q_ref[rows, lanes_of(pair)].astype(f32) * SCALE, tags) for pair in range(group)
        ]
        scores = [dot_nt(queries[pair][side], key_s[pair, side, rows, :]) for pair, side in every]
        scores = [jnp.where(row_at >= col_at, score, -FAR) for score in scores]
        tops = [jnp.max(score, -1, keepdims=True) for score in scores]
        exps = [jnp.exp(score - top).astype(bf16) for score, top in zip(scores, tops)]
        for at, (pair, side) in enumerate(every):
            mix_s[at] = dot_nn(exps[at], value_s[pair, side, rows, :])
            top_s[at] = jnp.broadcast_to(tops[at], (BLOCK, PAIR))

        if block:

            def one_block(other, carry, queries=queries):
                own = pl.ds(pl.multiple_of(other * BLOCK, BLOCK), BLOCK)
                scores = [dot_nt(queries[pair][side], key_s[pair, side, own, :]) for pair, side in every]
                olds = [top_s[at] for at in range(len(every))]
                tops = [
                    jnp.maximum(old, jnp.max(score, -1, keepdims=True))
                    for old, score in zip(olds, scores)
                ]
                exps = [
                    jnp.exp(score - jnp.concatenate([top, top], 1)).astype(bf16)
                    for score, top in zip(scores, tops)
                ]
                for at, (pair, side) in enumerate(every):
                    mix_s[at] = mix_s[at] * jnp.exp(olds[at] - tops[at]) + dot_nn(
                        exps[at], value_s[pair, side, own, :]
                    )
                    top_s[at] = tops[at]
                return carry

            lax.fori_loop(first_ref[block], block, one_block, 0)

        for pair in range(group):
            mix_a, mix_b = mix_s[2 * pair], mix_s[2 * pair + 1]
            total = jnp.where(left, mix_b, mix_a)
            mixed = jnp.where(left, mix_a, mix_b) / pltpu.roll(total, HD, 1)
            log_sum = jnp.where(left, top_s[2 * pair + 1], top_s[2 * pair]) + jnp.log(total)
            out_ref[rows, lanes_of(pair)] = mixed.astype(bf16)
            extra_ref[rows, lanes_of(pair)] = tagged(tags, log_sum, half).astype(bf16)


def packed_spec(rows, group, third):
    return pl.BlockSpec((rows, PAIR * group), lambda p, *_: (0, p + third * (D // PAIR // group)))


def self_forward(first_blocks, packed, tags, key_tag):
    rows = packed.shape[0]
    group = FORWARD_GROUP
    return pl.pallas_call(
        functools.partial(self_forward_kernel, group),
        out_shape=(
            jax.ShapeDtypeStruct((rows, D), bf16),
            jax.ShapeDtypeStruct((rows, D), bf16),
        ),
        grid_spec=pltpu.PrefetchScalarGridSpec(
            num_scalar_prefetch=1,
            grid=(D // PAIR // group,),
            in_specs=[
                packed_spec(rows, group, 0), packed_spec(rows, group, 1), packed_spec(rows, group, 2),
                whole_spec((rows, PAIR)), whole_spec((rows, PAIR)),
            ],
            out_specs=[pair_spec(rows, group), pair_spec(rows, group)],
            scratch_shapes=[pltpu.VMEM((2 * group, BLOCK, PAIR), f32)] * 2
            + [pltpu.VMEM((group, 2, rows, PAIR), bf16)] * 2,
        ),
        compiler_params=pltpu.CompilerParams(vmem_limit_bytes=26 * 2**20),
        cost_estimate=pl.CostEstimate(
            flops=12_000_000_000, bytes_accessed=8_000_000, transcendentals=4_000_000
        ),
        name="self_forward",
    )(first_blocks, packed, packed, packed, tags, key_tag)


def grad_rows(mixed, grad, left, half):
    product = mixed.astype(f32) * grad
    dot_a = jnp.sum(jnp.where(left, product, 0.0), -1, keepdims=True)
    dot_b = jnp.sum(jnp.where(left, 0.0, product), -1, keepdims=True)
    return halves(grad, tagged(jnp.zeros_like(product), jnp.where(left, dot_b, dot_a), half))


def back_step(group, own, queries, grads, turned, key_s, value_s, dq_s, dk_s, dv_s, left,
              masked=None, offset=None, fresh=False):
    every = [(pair, side) for pair in range(group) for side in range(2)]
    scores = [dot_nt(queries[pair][side], key_s[pair, side, own, :]) for pair, side in every]
    slopes = [dot_nt(grads[pair][side], value_s[pair, side, own, :]) for pair, side in every]
    if masked is not None:
        scores = [jnp.where(masked, score, -FAR) for score in scores]
    if offset is not None:
        scores = [score + offset for score in scores]
    probs = [jnp.exp(score) for score in scores]
    backs = [(prob * slope).astype(bf16) for prob, slope in zip(probs, slopes)]
    probs = [prob.astype(bf16) for prob in probs]
    for pair in range(group):
        back_a, back_b = backs[2 * pair : 2 * pair + 2]
        grad = jnp.where(
            left, dot_nn(back_a, key_s[pair, 0, own, :]), dot_nn(back_b, key_s[pair, 1, own, :])
        )
        if fresh:
            dq_s[pair] = grad
        else:
            dq_s[pair] += grad
        query_t, grad_t = turned[pair]
        for side in range(2):
            at = slice(side * HD, (side + 1) * HD)
            dk_s[pair, at, own] += dot_nn(query_t[at], backs[2 * pair + side])
            dv_s[pair, at, own] += dot_nn(grad_t[at], probs[2 * pair + side])


def back_operands(group, rows, q_ref, extra_ref, mixed_ref, grad_ref, left, half):
    queries, grads, turned = [], [], []
    for pair in range(group):
        at = (rows, lanes_of(pair))
        query = q_ref[at].astype(f32) * SCALE
        grad = grad_ref[at]
        queries.append(halves(query, extra_ref[at].astype(f32)))
        grads.append(grad_rows(mixed_ref[at], grad.astype(f32), left, half))
        turned.append((query.astype(bf16).T, grad.T))
    return queries, grads, turned


def cross_backward_kernel(
    group, seg_ref, frame_ref, q_ref, pooled_ref, key_w_ref, value_w_ref, extra_ref, mixed_ref,
    grad_ref, col_ref, dq_ref, dk_ref, dv_ref, key_s, value_s, dk_s, dv_s, dq_s,
):
    ones = ones_tags(BLOCK)
    put_halves(key_s, group, dot_nn(pooled_ref[...], key_w_ref[...]), ones)
    put_halves(value_s, group, dot_nn(pooled_ref[...], value_w_ref[...]), ones)
    dk_s[...] = jnp.zeros_like(dk_s)
    dv_s[...] = jnp.zeros_like(dv_s)
    left = lane_of(BLOCK) < HD
    half = lane_of(BLOCK) % HD
    for block in range(q_ref.shape[0] // BLOCK):
        rows = pl.ds(block * BLOCK, BLOCK)
        operands = back_operands(group, rows, q_ref, extra_ref, mixed_ref, grad_ref, left, half)
        dq_s[...] = jnp.zeros_like(dq_s)

        def one_clip(clip, carry, rows=rows, operands=operands):
            own = pl.ds(pl.multiple_of(frame_ref[clip] * KEYS, KEYS), KEYS)
            offset = jnp.where(col_ref[rows, :] == clip, 0.0, -FAR)
            back_step(group, own, *operands, key_s, value_s, dq_s, dk_s, dv_s, left, offset=offset)
            return carry

        lax.fori_loop(seg_ref[block * BLOCK], seg_ref[block * BLOCK + BLOCK - 1] + 1, one_clip, 0)
        for pair in range(group):
            dq_ref[rows, lanes_of(pair)] = (dq_s[pair] * SCALE).astype(bf16)
    for pair in range(group):
        dk_ref[lanes_of(pair), :] = dk_s[pair].astype(bf16)
        dv_ref[lanes_of(pair), :] = dv_s[pair].astype(bf16)


def cross_backward(segments, frames, queries, pooled, key_w, value_w, extra, mixed, grad):
    rows = queries.shape[0]
    keys = pooled.shape[0]
    group = BACKWARD_GROUP
    upright = pl.BlockSpec((PAIR * group, keys), lambda p, *_: (p, 0))
    own = pair_spec(rows, group)
    return pl.pallas_call(
        functools.partial(cross_backward_kernel, group),
        out_shape=(
            jax.ShapeDtypeStruct((rows, D), bf16),
            jax.ShapeDtypeStruct((D, keys), bf16),
            jax.ShapeDtypeStruct((D, keys), bf16),
        ),
        grid_spec=pltpu.PrefetchScalarGridSpec(
            num_scalar_prefetch=2,
            grid=(D // PAIR // group,),
            in_specs=[
                own,
                whole_spec(pooled.shape),
                pair_spec(key_w.shape[0], group),
                pair_spec(key_w.shape[0], group),
                own, own, own, whole_spec((rows, 1)),
            ],
            out_specs=[own, upright, upright],
            scratch_shapes=[pltpu.VMEM((group, 2, keys, PAIR), bf16)] * 2
            + [pltpu.VMEM((group, PAIR, keys), f32)] * 2
            + [pltpu.VMEM((group, BLOCK, PAIR), f32)],
        ),
        compiler_params=pltpu.CompilerParams(vmem_limit_bytes=VMEM_ASK),
        cost_estimate=pl.CostEstimate(
            flops=24_000_000_000, bytes_accessed=16_000_000, transcendentals=4_000_000
        ),
        name="cross_backward",
    )(segments, frames, queries, pooled, key_w, value_w, extra, mixed, grad, segments[:, None])


def self_backward_kernel(
    group, first_ref, q_ref, k_ref, v_ref, key_tag_ref, extra_ref, mixed_ref, grad_ref,
    dq_ref, dk_ref, dv_ref, key_s, value_s, dk_s, dv_s, dq_s,
):
    key_tag = key_tag_ref[...].astype(f32)
    put_halves(key_s, group, k_ref[...], key_tag)
    put_halves(value_s, group, v_ref[...], key_tag)
    dk_s[...] = jnp.zeros_like(dk_s)
    dv_s[...] = jnp.zeros_like(dv_s)
    left = lane_of(BLOCK) < HD
    half = lane_of(BLOCK) % HD
    row_at = lax.broadcasted_iota(jnp.int32, (BLOCK, BLOCK), 0)
    col_at = lax.broadcasted_iota(jnp.int32, (BLOCK, BLOCK), 1)
    for block in range(q_ref.shape[0] // BLOCK):
        rows = pl.ds(block * BLOCK, BLOCK)
        operands = back_operands(group, rows, q_ref, extra_ref, mixed_ref, grad_ref, left, half)
        back_step(
            group, rows, *operands, key_s, value_s, dq_s, dk_s, dv_s, left,
            masked=row_at >= col_at, fresh=True,
        )
        if block:

            def step(other, carry, operands=operands):
                own = pl.ds(pl.multiple_of(other * BLOCK, BLOCK), BLOCK)
                back_step(group, own, *operands, key_s, value_s, dq_s, dk_s, dv_s, left)
                return carry

            lax.fori_loop(first_ref[block], block, step, 0)
        for pair in range(group):
            dq_ref[rows, lanes_of(pair)] = (dq_s[pair] * SCALE).astype(bf16)
    for pair in range(group):
        dk_ref[:, lanes_of(pair)] = dk_s[pair].T.astype(bf16)
        dv_ref[:, lanes_of(pair)] = dv_s[pair].T.astype(bf16)


def self_backward(first_blocks, packed, key_tag, extra, mixed, grad):
    rows = packed.shape[0]
    group = BACKWARD_GROUP
    own = pair_spec(rows, group)
    return pl.pallas_call(
        functools.partial(self_backward_kernel, group),
        out_shape=(jax.ShapeDtypeStruct((rows, D), bf16),) * 3,
        grid_spec=pltpu.PrefetchScalarGridSpec(
            num_scalar_prefetch=1,
            grid=(D // PAIR // group,),
            in_specs=[
                packed_spec(rows, group, 0), packed_spec(rows, group, 1), packed_spec(rows, group, 2),
                whole_spec((rows, PAIR)),
                own, own, own,
            ],
            out_specs=[own] * 3,
            scratch_shapes=[pltpu.VMEM((group, 2, rows, PAIR), bf16)] * 2
            + [pltpu.VMEM((group, PAIR, rows), f32)] * 2
            + [pltpu.VMEM((group, BLOCK, PAIR), f32)],
        ),
        compiler_params=pltpu.CompilerParams(vmem_limit_bytes=VMEM_ASK),
        cost_estimate=pl.CostEstimate(
            flops=24_000_000_000, bytes_accessed=16_000_000, transcendentals=4_000_000
        ),
        name="self_backward",
    )(first_blocks, packed, packed, packed, key_tag, extra, mixed, grad)


def first_block_table(segment_row):
    clips = jnp.arange(CLIPS, dtype=jnp.int32)
    starts = jnp.sum((segment_row[:, None] < clips[None, :]).astype(jnp.int32), 0)
    heads = segment_row[::BLOCK]
    first = jnp.sum(jnp.where(heads[:, None] == clips[None, :], starts[None, :], 0), 1)
    return (first // BLOCK).astype(jnp.int32)


epsilon = 1e-05
ROOT = math.sqrt(2.0 / math.pi)
CUBE = 0.044715
C = 256
IMG = 64
POOL = 4


TILE = 256


def dot_tn(left, right):
    return lax.dot_general(left, right, (((0,), (0,)), ((), ())), preferred_element_type=f32)


def normalized(values):
    average = jnp.mean(values, -1, keepdims=True)
    centred = values - average
    spread = lax.rsqrt(jnp.mean(centred * centred, -1, keepdims=True) + epsilon)
    return centred * spread, spread


def norm_back(unit, spread, gain, grad):
    scaled = grad * gain
    mean_scaled = jnp.mean(scaled, -1, keepdims=True)
    mean_along = jnp.mean(scaled * unit, -1, keepdims=True)
    lead = tuple(range(grad.ndim - 1))
    return (
        (scaled - mean_scaled - unit * mean_along) * spread,
        jnp.sum(grad * unit, lead),
        jnp.sum(grad, lead),
    )


def gelu_and_slope(value):
    square = value * value
    bent = jnp.tanh(value * (ROOT + (ROOT * CUBE) * square))
    half = 0.5 + 0.5 * bent
    slope = half + value * (0.5 - 0.5 * bent * bent) * (ROOT + (3.0 * ROOT * CUBE) * square)
    return value * half, slope


def tiles_of(count):
    return [pl.ds(at, TILE) for at in range(0, count, TILE)]


def feed_forward_kernel(
    middle_ref, mixed_ref, join_ref, gain_ref, shift_ref, up_ref, bias_ref, down_ref, grad_ref,
    out_ref, second_ref, mixed_grad_ref, join_grad_ref, gain_grad_ref, shift_grad_ref,
    bias_grad_ref, chunk_ref,
    normed_s, grad_t_s, back_s, hidden_s, pre_grad_s, low_s, up_s, down_s, sems,
):
    step = pl.program_id(0)
    steps = pl.num_programs(0)
    rows = middle_ref.shape[0]
    shares, deep = chunk_ref.shape[0], chunk_ref.shape[1] // 2
    group, narrow = D // deep, D // shares

    @pl.when(step == 0)
    def _():
        for at in tiles_of(rows):
            total = middle_ref[at, :] + dot_nn(mixed_ref[at, :], join_ref[...])
            out_ref[at, :] = total
            second_ref[at, :] = total
            unit, _ = normalized(total)
            normed_s[at, :] = (unit * gain_ref[...] + shift_ref[...]).astype(bf16)
            back_s[at, :] = jnp.zeros((TILE, D), f32)
            grad_t_s[:, at] = grad_ref[at, :].T

    bias_grad = jnp.zeros((1, D), f32)
    for at in tiles_of(rows):
        hidden, slope = gelu_and_slope(dot_nn(normed_s[at, :], up_ref[...]) + bias_ref[...])
        hidden = hidden.astype(bf16)
        hidden_s[at, :] = hidden
        pre_grad = (dot_nt(grad_ref[at, :], down_ref[...]) * slope).astype(bf16)
        pre_grad_s[at, :] = pre_grad
        bias_grad += jnp.sum(pre_grad.astype(f32), 0, keepdims=True)
        out_ref[at, :] += dot_nn(hidden, down_ref[...])
        back_s[at, :] += dot_nt(pre_grad, up_ref[...])
    bias_grad_ref[...] = bias_grad
    up_s[step] = dot_tn(pre_grad_s[...], normed_s[...]).astype(bf16).reshape(group, deep, D)
    down_s[step] = dot_nn(grad_t_s[...], hidden_s[...]).astype(bf16).reshape(shares, narrow, D)

    def copies(at):
        return (
            pltpu.make_async_copy(
                up_s.at[at], chunk_ref.at[pl.ds(at * group, group), pl.ds(0, deep)], sems.at[0, at]
            ),
            pltpu.make_async_copy(
                down_s.at[at],
                chunk_ref.at[:, pl.ds(pl.multiple_of(deep + at * narrow, 16), narrow)],
                sems.at[1, at],
            ),
        )

    for copy in copies(step):
        copy.start()

    @pl.when(step == steps - 1)
    def _():
        gain_grad = jnp.zeros((1, D), f32)
        shift_grad = jnp.zeros((1, D), f32)
        for at in tiles_of(rows):
            unit, spread = normalized(second_ref[at, :])
            part, one, two = norm_back(unit, spread, gain_ref[...], back_s[at, :])
            gain_grad += one[None]
            shift_grad += two[None]
            total = grad_ref[at, :].astype(f32) + part
            second_ref[at, :] = total
            low = total.astype(bf16)
            low_s[at, :] = low
            mixed_grad_ref[at, :] = dot_nt(low, join_ref[...]).astype(bf16)
        gain_grad_ref[...] = gain_grad
        shift_grad_ref[...] = shift_grad
        join_grad_ref[...] = dot_tn(low_s[...], mixed_ref[...]).astype(bf16)
        for at in range(FF // D):
            for copy in copies(at):
                copy.wait()


FF = 3072


def still(shape):
    return pl.BlockSpec(shape, lambda *_: (0,) * len(shape), pipeline_mode=pl.Buffered(1))


def feed_forward(middle, mixed, join, gain, shift, up, bias, down, grad, shares):
    rows = middle.shape[0]
    steps = FF // D
    deep = FF // shares
    tall = still((rows, D))
    row = still((1, D))
    return pl.pallas_call(
        feed_forward_kernel,
        out_shape=(
            jax.ShapeDtypeStruct((rows, D), f32),
            jax.ShapeDtypeStruct((rows, D), f32),
            jax.ShapeDtypeStruct((rows, D), bf16),
            jax.ShapeDtypeStruct((D, D), bf16),
            jax.ShapeDtypeStruct((1, D), f32),
            jax.ShapeDtypeStruct((1, D), f32),
            jax.ShapeDtypeStruct((1, FF), f32),
            jax.ShapeDtypeStruct((shares, 2 * deep, D), bf16),
        ),
        grid_spec=pltpu.PrefetchScalarGridSpec(
            num_scalar_prefetch=0,
            grid=(steps,),
            in_specs=[
                tall, tall, still((D, D)), row, row,
                pl.BlockSpec((D, D), lambda j: (0, j)),
                pl.BlockSpec((1, D), lambda j: (0, j)),
                pl.BlockSpec((D, D), lambda j: (j, 0)),
                tall,
            ],
            out_specs=[
                tall, tall, tall, still((D, D)), row, row,
                pl.BlockSpec((1, D), lambda j: (0, j)),
                pl.BlockSpec(memory_space=pl.ANY),
            ],
            scratch_shapes=[
                pltpu.VMEM((rows, D), bf16),
                pltpu.VMEM((D, rows), bf16),
                pltpu.VMEM((rows, D), f32),
                pltpu.VMEM((rows, D), bf16),
                pltpu.VMEM((rows, D), bf16),
                pltpu.VMEM((rows, D), bf16),
                pltpu.VMEM((steps, D // deep, deep, D), bf16),
                pltpu.VMEM((steps, shares, D // shares, D), bf16),
                pltpu.SemaphoreType.DMA((2, steps)),
            ],
        ),
        compiler_params=pltpu.CompilerParams(vmem_limit_bytes=52 * 2**20),
        cost_estimate=pl.CostEstimate(
            flops=34_000_000_000, bytes_accessed=40_000_000, transcendentals=3_200_000
        ),
        name="feed_forward",
    )(middle, mixed, join, gain[None], shift[None], up, bias[None], down, grad)


def project_back_kernel(
    query_ref, key_ref, value_ref, project_ref, middle_ref, second_ref, gain_ref, shift_ref,
    join_ref, mixed_ref,
    middle_grad_ref, mixed_grad_ref, project_grad_ref, join_grad_ref, gain_grad_ref, shift_grad_ref,
    normed_s, low_s,
):
    rows = middle_ref.shape[0]
    gain_grad = jnp.zeros((1, D), f32)
    shift_grad = jnp.zeros((1, D), f32)
    for at in tiles_of(rows):
        back = dot_nt(query_ref[at, :], project_ref[:, 0:D])
        back += dot_nt(key_ref[at, :], project_ref[:, D : 2 * D])
        back += dot_nt(value_ref[at, :], project_ref[:, 2 * D : 3 * D])
        unit, spread = normalized(middle_ref[at, :])
        normed_s[at, :] = (unit * gain_ref[...] + shift_ref[...]).astype(bf16)
        part, one, two = norm_back(unit, spread, gain_ref[...], back)
        gain_grad += one[None]
        shift_grad += two[None]
        total = second_ref[at, :] + part
        middle_grad_ref[at, :] = total
        low = total.astype(bf16)
        low_s[at, :] = low
        mixed_grad_ref[at, :] = dot_nt(low, join_ref[...]).astype(bf16)
    gain_grad_ref[...] = gain_grad
    shift_grad_ref[...] = shift_grad
    project_grad_ref[0:D] = dot_tn(query_ref[...], normed_s[...]).astype(bf16)
    project_grad_ref[D : 2 * D] = dot_tn(key_ref[...], normed_s[...]).astype(bf16)
    project_grad_ref[2 * D : 3 * D] = dot_tn(value_ref[...], normed_s[...]).astype(bf16)
    join_grad_ref[...] = dot_tn(low_s[...], mixed_ref[...]).astype(bf16)


def project_back(query, key, value, project, middle, second, gain, shift, join, mixed):
    rows = middle.shape[0]
    return pl.pallas_call(
        project_back_kernel,
        out_shape=(
            jax.ShapeDtypeStruct((rows, D), f32),
            jax.ShapeDtypeStruct((rows, D), bf16),
            jax.ShapeDtypeStruct((3 * D, D), bf16),
            jax.ShapeDtypeStruct((D, D), bf16),
            jax.ShapeDtypeStruct((1, D), f32),
            jax.ShapeDtypeStruct((1, D), f32),
        ),
        in_specs=[pl.BlockSpec(memory_space=pltpu.VMEM)] * 10,
        out_specs=[pl.BlockSpec(memory_space=pltpu.VMEM)] * 6,
        scratch_shapes=[pltpu.VMEM((rows, D), bf16), pltpu.VMEM((rows, D), bf16)],
        compiler_params=pltpu.CompilerParams(vmem_limit_bytes=52 * 2**20),
        cost_estimate=pl.CostEstimate(
            flops=10_000_000_000, bytes_accessed=30_000_000, transcendentals=2_000
        ),
        name="project_back",
    )(query, key, value, project, middle, second, gain[None], shift[None], join, mixed)


def unpack_kernel(
    row, cross_at, filter_at, share_ref, summed_ref,
    up_ref, down_ref, project_ref, join_ref, cross_join_ref, query_ref, key_ref, value_ref, filter_ref,
):
    deep, model, own = FF // row, D // row, C // row
    up_ref[...] = summed_ref[0:deep, :].astype(f32)
    for part in range(FF // D):
        at = deep + part * model
        down_ref[:, part * D : (part + 1) * D] = summed_ref[at : at + model, :].astype(f32)
    project_ref[...] = share_ref[0 : 3 * model, :].astype(f32)
    join_ref[...] = share_ref[3 * model : 4 * model, :].astype(f32)
    cross_join_ref[...] = share_ref[4 * model : 5 * model, :].astype(f32)
    query_ref[...] = share_ref[cross_at : cross_at + model, :].astype(f32)
    key_ref[...] = share_ref[cross_at + model : cross_at + 2 * model, 0:C].astype(f32)
    value_ref[...] = share_ref[cross_at + model : cross_at + 2 * model, C : 2 * C].astype(f32)
    for tap in range(9):
        at = filter_at + tap // 3 * own
        lanes = slice(tap % 3 * C, (tap % 3 + 1) * C)
        filter_ref[tap] = share_ref[at : at + own, lanes].astype(f32)


def unpack(share, summed, row, cross_at, filter_at):
    deep, model, own = FF // row, D // row, C // row
    shapes = [
        (deep, D), (model, FF), (3 * model, D), (model, D), (model, D), (model, D), (model, C),
        (model, C), (9, own, C),
    ]
    vmem = pl.BlockSpec(memory_space=pltpu.VMEM)
    return pl.pallas_call(
        functools.partial(unpack_kernel, row, cross_at, filter_at),
        out_shape=tuple(jax.ShapeDtypeStruct(shape, f32) for shape in shapes),
        in_specs=[vmem] * 2,
        out_specs=[vmem] * len(shapes),
        name="unpack",
    )(share, summed)


MESH = pl.DeviceIdType.MESH


def bits_of(count):
    return count.bit_length() - 1


def stream_steps(order, dp_bits, q_bits):
    dp_up = [("dp", b) for b in range(dp_bits)]
    dp_down = dp_up[::-1]
    q_steps = [("q", b) for b in range(q_bits)]
    return {"up": dp_up + q_steps, "down": dp_down + q_steps, "q_up": q_steps + dp_up}[order]


def cut_streams(rows, dp, orders):
    unit = 16 * dp
    units = rows // unit
    plan, at = [], 0
    for number, order in enumerate(orders):
        size = units // len(orders) + (number < units % len(orders))
        if size:
            plan.append((at * unit, size * unit, order))
            at += size
    return plan


def stream_scratch(plan, dp, row, partial):
    dp_bits, q_bits = bits_of(dp), bits_of(row // 2) if partial else 0
    shapes = []
    for _, rows, order in plan:
        lead = q_bits
        shapes.append(pltpu.VMEM((2,) * lead + (rows, D), bf16))
        if partial:
            shapes.append(pltpu.VMEM((2,) * lead + (rows, D), bf16))
        for kind, _ in stream_steps(order, dp_bits, q_bits):
            if kind == "dp":
                rows //= 2
            else:
                lead -= 1
            shapes.append(pltpu.VMEM((2,) * lead + (rows, D), bf16))
    return shapes


class Exchange:
    def __init__(self, dp, row, send_sem, recv_sem, local_sem):
        self.dp, self.row = dp, row
        self.dp_bits, self.q_bits = bits_of(dp), bits_of(row // 2)
        self.me_dp, self.me_row = lax.axis_index("dp"), lax.axis_index("row")
        self.core, self.me_q = lax.rem(self.me_row, 2), self.me_row // 2
        self.send_sem, self.recv_sem, self.local_sem = send_sem, recv_sem, local_sem
        self.remote, self.local, self.started = 0, 0, []

    def bit(self, step):
        kind, b = step
        return lax.rem((self.me_dp if kind == "dp" else self.me_q) // (2**b), 2)

    def partner(self, step):
        kind, b = step
        if kind == "core":
            return self.me_dp, self.me_row + 1 - 2 * self.core
        ahead = (2**b) * (1 - 2 * self.bit(step))
        if kind == "dp":
            return self.me_dp + ahead, self.me_row
        return self.me_dp, self.me_row + 2 * ahead

    def greet(self, devices):
        barrier = pltpu.get_barrier_semaphore()
        for device in devices:
            pl.semaphore_signal(barrier, inc=1, device_id=device, device_id_type=MESH)
        pl.semaphore_wait(barrier, len(devices))

    def push(self, src, dst, device):
        copy = pltpu.make_async_remote_copy(
            src_ref=src, dst_ref=dst, send_sem=self.send_sem.at[self.remote],
            recv_sem=self.recv_sem.at[self.remote], device_id=device, device_id_type=MESH,
        )
        self.remote += 1
        copy.start()
        self.started.append(copy)
        return copy

    def fetch(self, src, dst):
        copy = pltpu.make_async_copy(src, dst, self.local_sem.at[self.local])
        self.local += 1
        copy.start()
        return copy

    def end(self):
        for copy in self.started:
            copy.wait_send()


class Stream:
    def __init__(self, ex, scratch, rows, order, out_ref, out_at, partial):
        self.ex, self.rows, self.off = ex, rows, 0
        self.out_ref, self.out_at = out_ref, out_at
        q_bits = ex.q_bits if partial else 0
        self.q_bits = q_bits
        self.steps = stream_steps(order, ex.dp_bits, q_bits)
        self.todo = list(self.steps)
        self.back = [step for step in self.steps if step[0] == "dp"][::-1]
        self.acc = scratch.pop(0)
        self.landings = [scratch.pop(0) for _ in range(len(self.steps) + partial)]
        self.picked = [None] * q_bits
        self.copies, self.locals, self.landing = [], [], None
        self.gathering, self.done = False, False

    def start_partial(self, segments):
        ex, at = self.ex, 0
        every = (slice(None),) * self.q_bits
        self.landing = self.landings.pop(0)
        for piece, first, rows in segments:
            here = every + (pl.ds(at, rows),)
            there = (pl.ds(first, rows),)
            self.copies.append(
                ex.push(
                    piece.at[every + (1 - ex.core,) + there], self.landing.at[here],
                    ex.partner(("core", 0)),
                )
            )
            self.locals.append(ex.fetch(piece.at[every + (ex.core,) + there], self.acc.at[here]))
            at += rows

    def start_summed(self, source, first):
        self.ex.fetch(source.at[pl.ds(first, self.rows)], self.acc).wait()
        self.send_next()

    def index(self, off, rows):
        picks = tuple(slice(None) if p is None else p for p in self.picked)
        return picks + (pl.ds(pl.multiple_of(off, 16), rows),)

    def send_next(self):
        step = self.todo.pop(0)
        mine = self.ex.bit(step)
        landing = self.landings.pop(0)
        if step[0] == "dp":
            half = self.rows // 2
            src = self.acc.at[self.index(self.off + (1 - mine) * half, half)]
            self.off, self.rows = self.off + mine * half, half
        else:
            place = self.q_bits - 1 - step[1]
            self.picked[place] = 1 - mine
            src = self.acc.at[self.index(self.off, self.rows)]
            self.picked[place] = mine
        self.copies = [self.ex.push(src, landing, self.ex.partner(step))]
        self.landing = landing

    def add_landing(self):
        picks = self.index(0, 16)[:-1]
        lead = (slice(None),) * (len(self.landing.shape) - 2)

        def body(i, carry):
            own = picks + (pl.ds(pl.multiple_of(self.off + i * 16, 16), 16),)
            other = lead + (pl.ds(pl.multiple_of(i * 16, 16), 16),)
            self.acc[own] = (self.acc[own].astype(f32) + self.landing[other].astype(f32)).astype(bf16)
            return carry

        lax.fori_loop(0, self.rows // 16, body, 0)

    def gather_next(self):
        at = pl.ds(pl.multiple_of(self.out_at + self.off, 16), self.rows)
        step = self.back[0]
        self.copies = [self.ex.push(self.out_ref.at[at], self.out_ref.at[at], self.ex.partner(step))]

    def advance(self):
        for copy in self.locals:
            copy.wait()
        self.locals = []
        for copy in self.copies:
            copy.wait_recv()
        if self.gathering:
            step = self.back.pop(0)
            self.off = self.off - self.ex.bit(step) * self.rows
            self.rows *= 2
            if self.back:
                self.gather_next()
            else:
                self.done = True
            return
        self.add_landing()
        if self.todo:
            self.send_next()
            return
        at = pl.ds(pl.multiple_of(self.out_at + self.off, 16), self.rows)
        self.out_ref[at, :] = self.acc[self.index(self.off, self.rows)]
        self.gathering = True
        self.gather_next()


def drain(streams):
    while any(not stream.done for stream in streams):
        for stream in streams:
            if not stream.done:
                stream.advance()


def sum_shares_kernel(dp, row, plan, *refs):
    summed_ref, out_ref = refs[:2]
    scratch, (send_sem, recv_sem, local_sem) = list(refs[2:-3]), refs[-3:]
    ex = Exchange(dp, row, send_sem, recv_sem, local_sem)
    ex.greet([ex.partner(("dp", b)) for b in range(ex.dp_bits)])
    streams = []
    for first, rows, order in plan:
        stream = Stream(ex, scratch, rows, order, out_ref, first, 0)
        stream.start_summed(summed_ref, first)
        streams.append(stream)
    drain(streams)
    ex.end()


def sum_shares(summed, dp, row, orders):
    plan = cut_streams(summed.shape[0], dp, orders)
    copies = 2 * bits_of(dp) * len(plan)
    return pl.pallas_call(
        functools.partial(sum_shares_kernel, dp, row, plan),
        out_shape=jax.ShapeDtypeStruct(summed.shape, bf16),
        in_specs=[pl.BlockSpec(memory_space=pl.ANY)],
        out_specs=pl.BlockSpec(memory_space=pltpu.VMEM),
        scratch_shapes=stream_scratch(plan, dp, row, 0) + [
            pltpu.SemaphoreType.DMA((copies,)),
            pltpu.SemaphoreType.DMA((copies,)),
            pltpu.SemaphoreType.DMA((len(plan),)),
        ],
        compiler_params=pltpu.CompilerParams(
            collective_id=3, has_side_effects=True, vmem_limit_bytes=VMEM_ASK
        ),
        name="sum_shares",
    )(summed)


def row_of(lead, me_row):
    return lead + (me_row,)


def greet_row(row):
    me_dp, me_row = lax.axis_index("dp"), lax.axis_index("row")
    barrier = pltpu.get_barrier_semaphore()
    for ahead in range(1, row):
        pl.semaphore_signal(
            barrier, inc=1, device_id=(me_dp, lax.rem(me_row + ahead, row)), device_id_type=MESH
        )
    pl.semaphore_wait(barrier, row - 1)


def edge_copies(cells, above, below, send_sem, recv_sem, row):
    me_dp, me_row = lax.axis_index("dp"), lax.axis_index("row")
    here = cells.shape[1]
    onward = pltpu.make_async_remote_copy(
        src_ref=cells.at[:, here - 1], dst_ref=above, send_sem=send_sem.at[0],
        recv_sem=recv_sem.at[0], device_id=(me_dp, lax.rem(me_row + 1, row)), device_id_type=MESH,
    )
    back = pltpu.make_async_remote_copy(
        src_ref=cells.at[:, 0], dst_ref=below, send_sem=send_sem.at[1],
        recv_sem=recv_sem.at[1], device_id=(me_dp, lax.rem(me_row + row - 1, row)),
        device_id_type=MESH,
    )
    return onward, back


def start_edges(copies):
    for copy in copies:
        copy.start()


def end_edges(copies):
    for copy in copies:
        copy.wait_send()
        copy.wait_recv()


def put_wide(wide, frame, first, cells):
    column = lax.broadcasted_iota(jnp.int32, cells.shape, 0) % IMG
    cells = cells.astype(f32)
    count = cells.shape[0]
    left = jnp.where(column == 0, 0.0, pltpu.roll(cells, 1, 0))
    right = jnp.where(column == IMG - 1, 0.0, pltpu.roll(cells, count - 1, 0))
    at = pl.ds(first, count)
    wide[frame, at, 0:C] = left.astype(bf16)
    wide[frame, at, C : 2 * C] = cells.astype(bf16)
    wide[frame, at, 2 * C : 3 * C] = right.astype(bf16)


def put_edges(wide, above, below, here, row):
    me_row = lax.axis_index("row")
    keep_above = jnp.where(me_row > 0, 1.0, 0.0)
    keep_below = jnp.where(me_row < row - 1, 1.0, 0.0)
    for frame in range(wide.shape[0]):
        put_wide(wide, frame, 0, above[frame].astype(f32) * keep_above)
        put_wide(wide, frame, (here + 1) * IMG, below[frame].astype(f32) * keep_below)


def conv_forward_kernel(
    row, frames_ref, taps_ref, bias_ref, gain_ref, shift_ref,
    pre_ref, wide_ref, every_ref,
    above_s, below_s, pool_s, edge_send, edge_recv, send_sem, recv_sem,
):
    me_dp, me_row = lax.axis_index("dp"), lax.axis_index("row")
    core, me_q, places = lax.rem(me_row, 2), me_row // 2, row // 2
    count, here = frames_ref.shape[0], frames_ref.shape[1]
    greet_row(row)
    edges = edge_copies(frames_ref, above_s, below_s, edge_send, edge_recv, row)
    start_edges(edges)
    for frame in range(count):
        put_wide(wide_ref, frame, IMG, frames_ref[frame].reshape(here * IMG, C))
    end_edges(edges)
    put_edges(wide_ref, above_s, below_s, here, row)
    tile = POOL * IMG
    for frame in range(count):
        for part in range(here // POOL):
            first = part * tile
            pre = bias_ref[...] + dot_nn(wide_ref[frame, pl.ds(first, tile), :], taps_ref[0])
            pre += dot_nn(wide_ref[frame, pl.ds(first + IMG, tile), :], taps_ref[1])
            pre += dot_nn(wide_ref[frame, pl.ds(first + 2 * IMG, tile), :], taps_ref[2])
            pre_ref[frame, pl.ds(first, tile), :] = pre
            active, _ = gelu_and_slope(pre)
            unit, _ = normalized(active)
            normed = unit * gain_ref[...] + shift_ref[...]
            lines = normed.reshape(POOL, IMG, C)
            lines = lines[0] + lines[1] + lines[2] + lines[3]
            cells = IMG // POOL
            for side in range(C // PAIR):
                lanes = slice(side * PAIR, (side + 1) * PAIR)
                pool_s[side] = lines[:, lanes]
                total = pool_s[side, pl.ds(0, cells, stride=POOL), :]
                for at in range(1, POOL):
                    total += pool_s[side, pl.ds(at, cells, stride=POOL), :]
                every_ref[frame, me_row, pl.ds(part * cells, cells), lanes] = (
                    total * (1.0 / (POOL * POOL))
                ).astype(bf16)

    def push(source_row, to_row, at):
        copy = pltpu.make_async_remote_copy(
            src_ref=every_ref.at[:, source_row], dst_ref=every_ref.at[:, source_row],
            send_sem=send_sem.at[at], recv_sem=recv_sem.at[at], device_id=(me_dp, to_row),
            device_id_type=MESH,
        )
        copy.start()
        return copy

    other = me_row + 1 - 2 * core
    copies = [push(me_row, other, 0)]
    for ahead in range(1, places):
        copies.append(push(me_row, lax.rem(me_q + ahead, places) * 2 + core, ahead))
    for ahead in range(1, places):
        copies[ahead].wait_recv()
        came = lax.rem(me_q + places - ahead, places) * 2 + core
        copies.append(push(came, other, places - 1 + ahead))
    copies[0].wait_recv()
    for copy in copies[places:]:
        copy.wait_recv()
    for copy in copies:
        copy.wait_send()


def conv_forward(frames, taps, bias, gain, shift, row):
    count, here = frames.shape[0], frames.shape[1]
    keys = (here // POOL) * (IMG // POOL)
    return pl.pallas_call(
        functools.partial(conv_forward_kernel, row),
        out_shape=(
            jax.ShapeDtypeStruct((count, here * IMG, C), f32),
            jax.ShapeDtypeStruct((count, (here + 2) * IMG, 3 * C), bf16),
            jax.ShapeDtypeStruct((count, row, keys, C), bf16),
        ),
        in_specs=[pl.BlockSpec(memory_space=pltpu.VMEM)] * 5,
        out_specs=[pl.BlockSpec(memory_space=pltpu.VMEM)] * 3,
        scratch_shapes=[
            pltpu.VMEM((count, IMG, C), bf16),
            pltpu.VMEM((count, IMG, C), bf16),
            pltpu.VMEM((C // PAIR, IMG, PAIR), f32),
            pltpu.SemaphoreType.DMA((2,)),
            pltpu.SemaphoreType.DMA((2,)),
            pltpu.SemaphoreType.DMA((row,)),
            pltpu.SemaphoreType.DMA((row,)),
        ],
        compiler_params=pltpu.CompilerParams(
            collective_id=1, has_side_effects=True, vmem_limit_bytes=20 * 2**20
        ),
        name="conv_forward",
    )(frames, taps.reshape(3, 3 * C, C), bias[None], gain[None], shift[None])


READY_ORDERS = ("up", "down", "up", "down")
CROSS_ORDERS = ("q_up", "up", "down")
FILTER_ORDERS = ("up", "down")


def segments_of(pieces, first, rows):
    parts, at = [], 0
    for piece, start, count in pieces:
        low, high = max(first, at), min(first + rows, at + count)
        if low < high:
            parts.append((piece, start + low - at, high - low))
        at += count
    return parts


def finish_kernel(
    dp, row, plans,
    project_ref, join_ref, cross_join_ref, query_grad_ref, x_ref, query_w_ref, middle_grad_ref,
    keys_grad_ref, values_grad_ref, every_ref, key_w_ref, value_w_ref, pre_ref, wide_ref, taps_ref,
    gain_ref, small_ref,
    tokens_grad_ref, frames_grad_ref, share_ref,
    query_s, both_s, filter_s, x_s, query_w_s, pre_s, wide_in_s, taps_s, keys_grad_s, values_grad_s,
    part_s, landing_s, sum_s, arrive_s, spread_s, grad_s, grad_t_s, wide_s, above_s, below_s,
    edge_send, edge_recv, send_sem, recv_sem, local_sem, *scratch,
):
    scratch = list(scratch)
    ex = Exchange(dp, row, send_sem, recv_sem, local_sem)
    me_dp, me_row, core, me_q, places = ex.me_dp, ex.me_row, ex.core, ex.me_q, row // 2
    count, here = grad_s.shape[0], grad_s.shape[1]
    keys = part_s.shape[3]
    model, own = D // row, C // row
    ex.greet(
        [(me_dp, lax.rem(me_row + ahead, row)) for ahead in range(1, row)]
        + [ex.partner(("dp", b)) for b in range(ex.dp_bits)]
    )
    keys_in = ex.fetch(keys_grad_ref, keys_grad_s)
    values_in = ex.fetch(values_grad_ref, values_grad_s)
    base, groups = 0, []
    for plan in plans:
        groups.append([
            Stream(ex, scratch, rows, order, share_ref, base + first, 1) for first, rows, order in plan
        ])
        base += sum(rows for _, rows, _ in plan)
    ready, crossed, filtered = groups

    def start(group, plan, pieces):
        for stream, (first, rows, _) in zip(group, plan):
            stream.start_partial(segments_of(pieces, first, rows))

    used = 5 * model
    total_rows = sum(rows for _, rows, _ in plans[0])
    start(ready, plans[0], [
        (project_ref, 0, 3 * model), (join_ref, 0, model), (cross_join_ref, 0, model),
        (project_ref, 0, total_rows - used),
    ])
    x_in = ex.fetch(x_ref, x_s)
    query_in = ex.fetch(query_w_ref, query_w_s)
    pre_in = ex.fetch(pre_ref, pre_s)
    wide_in = ex.fetch(wide_ref, wide_in_s)
    taps_in = ex.fetch(taps_ref, taps_s)

    keys_in.wait()
    part = lax.dot_general(
        keys_grad_s[...], key_w_ref[...], (((0,), (1,)), ((), ())), preferred_element_type=f32
    )
    values_in.wait()
    part += lax.dot_general(
        values_grad_s[...], value_w_ref[...], (((0,), (1,)), ((), ())), preferred_element_type=f32
    )
    part_s[...] = part.astype(bf16).reshape(count, places, 2, keys, C)
    pooled_core = ex.push(part_s.at[:, :, 1 - core], landing_s, ex.partner(("core", 0)))

    split = (2,) * ex.q_bits + (2,)
    lines = both_s.shape[-2]
    for at, grad_ref in enumerate((keys_grad_s, values_grad_s)):
        both_s[..., 0:model, at * C : (at + 1) * C] = (
            dot_nn(grad_ref[...], every_ref[...]).astype(bf16).reshape(split + (model, C))
        )
    both_s[..., 0:model, 2 * C : 3 * C] = jnp.zeros(split + (model, C), bf16)
    if lines > model:
        both_s[..., model:lines, :] = jnp.zeros(split + (lines - model, D), bf16)
    x_in.wait()
    query_s[...] = dot_tn(query_grad_ref[...], x_s[...]).astype(bf16).reshape(split + (model, D))
    start(crossed, plans[1], [(query_s, 0, model), (both_s, 0, lines)])

    pooled_core.wait_recv()
    sum_s[...] = (part_s[:, :, core].astype(f32) + landing_s[...].astype(f32)).astype(bf16)
    pooled_in = []
    for ahead in range(1, places):
        to = lax.rem(me_q + ahead, places)
        pooled_in.append(ex.push(sum_s.at[:, to], arrive_s.at[ahead - 1], (me_dp, to * 2 + core)))
    for stream in ready:
        stream.advance()
    query_in.wait()
    for at in tiles_of(x_s.shape[0]):
        tokens_grad_ref[at, :] = middle_grad_ref[at, :] + dot_nt(query_grad_ref[at, :], query_w_s[...])
    for copy in pooled_in:
        copy.wait_recv()
    pooled = sum_s[:, me_q].astype(f32)
    for ahead in range(1, places):
        pooled += arrive_s[ahead - 1].astype(f32)
    pooled = pooled * (1.0 / (POOL * POOL))
    for stream in crossed:
        stream.advance()

    tile = POOL * IMG
    cells = IMG // POOL
    bias_grad = jnp.zeros((1, C), f32)
    gain_grad = jnp.zeros((1, C), f32)
    shift_grad = jnp.zeros((1, C), f32)
    pre_in.wait()
    for frame in range(count):
        for part in range(here // POOL):
            for side in range(C // PAIR):
                own_cells = pooled[
                    frame, part * cells : (part + 1) * cells, side * PAIR : (side + 1) * PAIR
                ]
                for at in range(POOL):
                    spread_s[side, pl.ds(at, cells, stride=POOL), :] = own_cells
            line = jnp.concatenate([spread_s[side] for side in range(C // PAIR)], 1)
            back = jnp.broadcast_to(line[None], (POOL, IMG, C)).reshape(tile, C)
            active, slope = gelu_and_slope(pre_s[frame, pl.ds(part * tile, tile), :])
            unit, spread = normalized(active)
            grad, one, two = norm_back(unit, spread, gain_ref[...], back)
            gain_grad += one[None]
            shift_grad += two[None]
            grad = (slope * grad).astype(bf16)
            bias_grad += jnp.sum(grad.astype(f32), 0, keepdims=True)
            grad_s[frame, pl.ds(part * POOL, POOL)] = grad.reshape(POOL, IMG, C)
    edges = edge_copies(grad_s, above_s, below_s, edge_send, edge_recv, row)
    start_edges(edges)
    for frame in range(count):
        cells_here = grad_s[frame].reshape(here * IMG, C)
        put_wide(wide_s, frame, IMG, cells_here)
        grad_t_s[frame] = cells_here.T
    for stream in ready[:3]:
        stream.advance()
    wide_in.wait()
    for dy in range(3):
        total = None
        for frame in range(count):
            piece = dot_nn(grad_t_s[frame], wide_in_s[frame, pl.ds(dy * IMG, here * IMG), :])
            total = piece if total is None else total + piece
        filter_s[..., dy * own : (dy + 1) * own, :] = total.astype(bf16).reshape(split + (own, D))
    lines = filter_s.shape[-2] - 3 * own
    line_at = lax.broadcasted_iota(jnp.int32, (lines, D), 0)
    extra = jnp.zeros((lines, D), f32)
    for at, item in enumerate((bias_grad, gain_grad, shift_grad)):
        item = jnp.concatenate([item, jnp.zeros((1, D - C), f32)], 1)
        extra = jnp.where(line_at == 8 + at, item, extra)
    for place in range(places):
        for side in range(2):
            index = tuple((place >> b) & 1 for b in reversed(range(ex.q_bits))) + (side,)
            own_small = small_ref[place * 2 + side].astype(f32)
            filter_s[index + (slice(3 * own, 3 * own + lines),)] = (own_small + extra).astype(bf16)
    start(filtered, plans[2], [(filter_s, 0, 3 * own + lines)])
    for stream in ready[3:] + crossed:
        stream.advance()
    end_edges(edges)
    put_edges(wide_s, above_s, below_s, here, row)
    taps_in.wait()
    for frame in range(count):
        for part in range(here // POOL):
            total = None
            for tap in range(9):
                dy, dx = tap // 3, tap % 3
                window = wide_s[frame, pl.ds(part * tile + dy * IMG, tile), dx * C : (dx + 1) * C]
                piece = dot_nt(window, taps_s[8 - tap])
                total = piece if total is None else total + piece
            frames_grad_ref[frame, pl.ds(part * tile, tile), :] = total
        if frame == 0:
            for stream in filtered:
                stream.advance()
        if frame == 1:
            for stream in ready:
                stream.advance()
    drain(filtered + ready + crossed)
    ex.end()


def finish(project_grad, join_grad, cross_join_grad, query_grad, x, query_w, middle_grad,
           keys_grad_t, values_grad_t, everyone, key_w, value_w, pre, wide, taps, gain, small, dp, row):
    unit = 16 * dp
    model, own = D // row, C // row
    count, here = pre.shape[0], pre.shape[1] // IMG
    keys = (here // POOL) * (IMG // POOL)
    whole_units = lambda rows: -(-rows // unit) * unit
    rows = [whole_units(5 * model), whole_units(2 * model), 3 * own + small.shape[1]]
    plans = [
        cut_streams(count_rows, dp, orders)
        for count_rows, orders in zip(rows, (READY_ORDERS, CROSS_ORDERS, FILTER_ORDERS))
    ]
    split = (2,) * bits_of(row // 2) + (2,)
    view = lambda piece: piece.reshape(split + (piece.shape[0] // row, D))
    streams = [stream for plan in plans for stream in plan]
    per_stream = 2 * bits_of(dp) + bits_of(row // 2)
    remote = per_stream * len(streams) + 8 * len(streams) + row
    local = 8 * len(streams) + 8
    vmem = pl.BlockSpec(memory_space=pltpu.VMEM)
    away = pl.BlockSpec(memory_space=pl.ANY)
    return pl.pallas_call(
        functools.partial(finish_kernel, dp, row, plans),
        out_shape=(
            jax.ShapeDtypeStruct(x.shape, f32),
            jax.ShapeDtypeStruct(pre.shape, f32),
            jax.ShapeDtypeStruct((sum(rows), D), bf16),
        ),
        in_specs=[
            away, away, away, vmem, away, away, vmem, away, away, vmem, vmem, vmem, away, away, away,
            vmem, vmem,
        ],
        out_specs=[vmem] * 3,
        scratch_shapes=[
            pltpu.VMEM(split + (model, D), bf16),
            pltpu.VMEM(split + (rows[1] - model, D), bf16),
            pltpu.VMEM(split + (rows[2], D), bf16),
            pltpu.VMEM(x.shape, bf16),
            pltpu.VMEM(query_w.shape, bf16),
            pltpu.VMEM(pre.shape, f32),
            pltpu.VMEM(wide.shape, bf16),
            pltpu.VMEM(taps.shape, bf16),
            pltpu.VMEM(keys_grad_t.shape, bf16),
            pltpu.VMEM(values_grad_t.shape, bf16),
            pltpu.VMEM((count, row // 2, 2, keys, C), bf16),
            pltpu.VMEM((count, row // 2, keys, C), bf16),
            pltpu.VMEM((count, row // 2, keys, C), bf16),
            pltpu.VMEM((row // 2 - 1, count, keys, C), bf16),
            pltpu.VMEM((C // PAIR, IMG, PAIR), f32),
            pltpu.VMEM((count, here, IMG, C), bf16),
            pltpu.VMEM((count, C, here * IMG), bf16),
            pltpu.VMEM((count, (here + 2) * IMG, 3 * C), bf16),
            pltpu.VMEM((count, IMG, C), bf16),
            pltpu.VMEM((count, IMG, C), bf16),
            pltpu.SemaphoreType.DMA((2,)),
            pltpu.SemaphoreType.DMA((2,)),
            pltpu.SemaphoreType.DMA((remote,)),
            pltpu.SemaphoreType.DMA((remote,)),
            pltpu.SemaphoreType.DMA((local,)),
        ] + [shape for plan in plans for shape in stream_scratch(plan, dp, row, 1)],
        compiler_params=pltpu.CompilerParams(
            collective_id=2, has_side_effects=True, vmem_limit_bytes=54 * 2**20
        ),
        name="finish",
    )(
        view(project_grad), view(join_grad), view(cross_join_grad), query_grad, x, query_w,
        middle_grad, keys_grad_t, values_grad_t, everyone, key_w, value_w, pre, wide, taps,
        gain[None], small,
    )


def fast_dot(left, right):
    return jnp.dot(left, right, preferred_element_type=f32)


def shared_rows(matrix, count):
    return matrix.reshape(count, matrix.shape[0] // count, matrix.shape[1])


def on_device(
    frames, tokens, segment_ids, clip_frame, filter_weight, filter_bias, context_gain,
    context_shift, cross_query, cross_key, cross_value, cross_output, first_gain, first_shift,
    self_project, self_output, second_gain, second_shift, up_weight, up_bias, down_weight, cotangent,
):
    shares = lax.axis_size("row")
    x = tokens[0]
    segments = segment_ids[0]
    clip_frames = clip_frame[0]
    out_grad = cotangent[0]
    tags = segment_tags(segments)
    key_tag = key_tags(segments)
    first_blocks = first_block_table(segments)

    pre_act, wide, everyone = conv_forward(
        frames, filter_weight, filter_bias, context_gain, context_shift, shares
    )
    everyone = everyone.reshape(-1, C)
    cross_q = fast_dot(x, cross_query).astype(bf16)
    cross_mixed, cross_extra = cross_forward(
        segments, clip_frames, cross_q, everyone, cross_key, cross_value
    )
    middle = x.astype(f32) + fast_dot(cross_mixed, cross_output)
    first_unit, first_spread = normalized(middle)
    first_normed = (first_unit * first_gain + first_shift).astype(bf16)
    packed = fast_dot(first_normed, self_project).astype(bf16)
    self_mixed, self_extra = self_forward(first_blocks, packed, tags, key_tag)
    (
        output, second_grad, self_mixed_grad, join_grad, second_gain_grad,
        second_shift_grad, up_bias_grad, chunk_a,
    ) = feed_forward(
        middle, self_mixed, self_output, second_gain, second_shift, up_weight, up_bias, down_weight,
        out_grad, shares,
    )
    share_a = lax.psum_scatter(chunk_a, "row", scatter_dimension=0, tiled=False)
    query_grad, key_grad, value_grad = self_backward(
        first_blocks, packed, key_tag, self_extra, self_mixed, self_mixed_grad
    )
    (
        middle_grad, cross_mixed_grad, project_grad, cross_join_grad, first_gain_grad,
        first_shift_grad,
    ) = project_back(
        query_grad, key_grad, value_grad, self_project, middle, second_grad, first_gain, first_shift,
        cross_output, cross_mixed,
    )
    cross_q_grad, keys_grad_t, values_grad_t = cross_backward(
        segments, clip_frames, cross_q, everyone, cross_key, cross_value, cross_extra, cross_mixed,
        cross_mixed_grad,
    )
    dp = lax.axis_size("dp")
    small = jnp.concatenate(
        [
            item.astype(bf16).reshape(shares, -1)
            for item in (
                first_gain_grad, first_shift_grad, second_gain_grad, second_shift_grad, up_bias_grad,
            )
        ],
        1,
    )
    lines = 16 + -(3 * C // shares + 16) % (16 * dp)
    small = jnp.pad(small, ((0, 0), (0, lines * D - small.shape[1]))).reshape(shares, lines, D)
    tokens_grad, frames_grad, reduced = finish(
        project_grad, join_grad, cross_join_grad, cross_q_grad, x, cross_query, middle_grad,
        keys_grad_t, values_grad_t, everyone, cross_key, cross_value, pre_act, wide, filter_weight,
        context_gain, small, dp, shares,
    )
    share_a = sum_shares(share_a, dp, shares, ("up", "down"))
    own_part = C // shares
    filter_at = reduced.shape[0] - (3 * own_part + lines)
    cross_at = filter_at - -(-2 * D // shares // (16 * dp)) * 16 * dp
    (
        up_grad, down_grad, project_grad, self_output_grad, cross_output_grad, cross_query_grad,
        cross_key_grad, cross_value_grad, filter_grad,
    ) = unpack(reduced, share_a, shares, cross_at, filter_at)
    late = reduced[filter_at + 3 * own_part :].astype(f32)
    flat = late[:2].reshape(-1)
    sizes = [D // shares] * 4 + [3072 // shares]
    ends = [sum(sizes[: i + 1]) for i in range(len(sizes))]
    vectors = [flat[e - s : e] for e, s in zip(ends, sizes)]
    mine = lax.dynamic_slice_in_dim(late[8:11, :C], lax.axis_index("row") * own_part, own_part, 1)
    vectors = vectors + [mine[0], mine[1], mine[2]]
    return (
        middle[None],
        output[None],
        tokens_grad[None],
        frames_grad.reshape(frames.shape),
        jnp.transpose(filter_grad, (0, 2, 1)),
        vectors[5],
        vectors[6],
        vectors[7],
        cross_query_grad.T,
        cross_key_grad.T,
        cross_value_grad.T,
        cross_output_grad.T,
        vectors[0],
        vectors[1],
        project_grad.T,
        self_output_grad.T,
        vectors[2],
        vectors[3],
        up_grad.T,
        vectors[4],
        down_grad.T,
    )


def solution(mesh):
    whole = P()
    by_row = P(("dp", "row"), None, None)
    in_specs = (
        P("dp", "row", None, None),
        by_row,
        P(("dp", "row"), None),
        P(("dp", "row"), None),
    ) + (whole,) * 17 + (by_row,)
    columns = P(None, "row")
    vector = P("row")
    out_specs = (
        by_row, by_row, by_row, P("dp", "row", None, None), P(None, None, "row"), vector, vector,
        vector, columns, columns, columns, columns, vector, vector, columns, columns, vector, vector,
        columns, vector, columns,
    )
    return jax.shard_map(
        on_device, mesh=mesh, in_specs=in_specs, out_specs=out_specs, check_vma=False
    )
```

```python
import functools
import math
import jax
import jax.numpy as jnp
from jax import lax
from jax.experimental import pallas as pl
from jax.experimental.pallas import tpu as pltpu
from jax.sharding import PartitionSpec as P

D = 768
HD = 64
PAIR = 128
BLOCK = 256
KEYS = 256
CLIPS = 4
FAR = 2.0**100
SCALE = 0.125
CROSS_GROUP = 6
FORWARD_GROUP = 3
BACKWARD_GROUP = 3
f32 = jnp.float32
bf16 = jnp.bfloat16
VMEM_ASK = 48 * 2**20


def lane_of(rows):
    return lax.broadcasted_iota(jnp.int32, (rows, PAIR), 1)


def dot_nt(left, right):
    return lax.dot_general(left, right, (((1,), (1,)), ((), ())), preferred_element_type=f32)


def dot_nn(left, right):
    return lax.dot_general(left, right, (((1,), (0,)), ((), ())), preferred_element_type=f32)


def tagged(extra, value, half):
    high = value.astype(bf16).astype(f32)
    rest = value - high
    middle = rest.astype(bf16).astype(f32)
    extra = jnp.where(half == 8, -high, extra)
    extra = jnp.where(half == 9, -middle, extra)
    return jnp.where(half == 10, middle - rest, extra)


def segment_tags(segment_row):
    lane = jnp.arange(PAIR, dtype=jnp.int32) % HD
    wrong = (lane[None, :] < CLIPS) & (lane[None, :] != segment_row[:, None])
    return jnp.where(wrong, -FAR, 0.0).astype(bf16)


def key_tags(segment_row):
    lane = jnp.arange(PAIR, dtype=jnp.int32) % HD
    ones = (lane[None, :] == segment_row[:, None]) | ((lane[None, :] >= 8) & (lane[None, :] <= 10))
    return jnp.where(ones, 1.0, 0.0).astype(bf16)


def ones_tags(rows):
    half = lane_of(rows) % HD
    return jnp.where((half >= 8) & (half <= 10), 1.0, 0.0)


def halves(value, filler):
    left = lane_of(value.shape[0]) < HD
    value = value.astype(f32)
    return jnp.where(left, value, filler).astype(bf16), jnp.where(left, filler, value).astype(bf16)


def put_halves(store, group, value, filler):
    for pair in range(group):
        for at in range(0, value.shape[0], BLOCK):
            rows = slice(at, at + BLOCK)
            fill = filler if filler.shape[0] == BLOCK else filler[rows, :]
            one, two = halves(value[rows, pair * PAIR : (pair + 1) * PAIR], fill)
            store[pair, 0, rows, :] = one
            store[pair, 1, rows, :] = two


def lanes_of(pair):
    return slice(pair * PAIR, (pair + 1) * PAIR)


def cross_forward_kernel(
    group, seg_ref, frame_ref, q_ref, pooled_ref, key_w_ref, value_w_ref, col_ref,
    out_ref, extra_ref, key_s, value_s,
):
    put_halves(key_s, group, dot_nn(pooled_ref[...], key_w_ref[...]), jnp.zeros((BLOCK, PAIR), f32))
    put_halves(value_s, group, dot_nn(pooled_ref[...], value_w_ref[...]), jnp.ones((BLOCK, PAIR), f32))
    left = lane_of(BLOCK) < HD
    half = lane_of(BLOCK) % HD
    for block in range(q_ref.shape[0] // BLOCK):
        rows = pl.ds(block * BLOCK, BLOCK)
        queries = [
            (q_ref[rows, lanes_of(pair)].astype(f32) * SCALE).astype(bf16) for pair in range(group)
        ]

        def one_clip(clip, carry, rows=rows, queries=queries):
            own = pl.ds(pl.multiple_of(frame_ref[clip] * KEYS, KEYS), KEYS)
            mine = col_ref[rows, :] == clip
            scores = [
                dot_nt(queries[pair], key_s[pair, side, own, :])
                for pair in range(group)
                for side in range(2)
            ]
            tops = [jnp.max(score, -1, keepdims=True) for score in scores]
            exps = [jnp.exp(score - top).astype(bf16) for score, top in zip(scores, tops)]
            mixes = [
                dot_nn(exps[2 * pair + side], value_s[pair, side, own, :])
                for pair in range(group)
                for side in range(2)
            ]
            for pair in range(group):
                mix_a, mix_b = mixes[2 * pair : 2 * pair + 2]
                top_a, top_b = tops[2 * pair : 2 * pair + 2]
                total = jnp.where(left, mix_b, mix_a)
                mixed = jnp.where(left, mix_a, mix_b) / pltpu.roll(total, HD, 1)
                log_sum = jnp.where(left, top_b, top_a) + jnp.log(total)
                extra = tagged(jnp.zeros((BLOCK, PAIR), f32), log_sum, half)
                at = (rows, lanes_of(pair))
                out_ref[at] = jnp.where(mine, mixed, out_ref[at].astype(f32)).astype(bf16)
                extra_ref[at] = jnp.where(mine, extra, extra_ref[at].astype(f32)).astype(bf16)
            return carry

        lax.fori_loop(seg_ref[block * BLOCK], seg_ref[block * BLOCK + BLOCK - 1] + 1, one_clip, 0)


def pair_spec(rows, group):
    return pl.BlockSpec((rows, PAIR * group), lambda p, *_: (0, p))


def whole_spec(shape):
    return pl.BlockSpec(shape, lambda p, *_: (0,) * len(shape), pipeline_mode=pl.Buffered(1))


def cross_forward(segments, frames, queries, pooled, key_w, value_w):
    rows = queries.shape[0]
    keys = pooled.shape[0]
    group = CROSS_GROUP
    return pl.pallas_call(
        functools.partial(cross_forward_kernel, group),
        out_shape=(
            jax.ShapeDtypeStruct((rows, D), bf16),
            jax.ShapeDtypeStruct((rows, D), bf16),
        ),
        grid_spec=pltpu.PrefetchScalarGridSpec(
            num_scalar_prefetch=2,
            grid=(D // PAIR // group,),
            in_specs=[
                pair_spec(rows, group),
                whole_spec(pooled.shape),
                pair_spec(key_w.shape[0], group),
                pair_spec(key_w.shape[0], group),
                whole_spec((rows, 1)),
            ],
            out_specs=[pair_spec(rows, group), pair_spec(rows, group)],
            scratch_shapes=[pltpu.VMEM((group, 2, keys, PAIR), bf16)] * 2,
        ),
        compiler_params=pltpu.CompilerParams(vmem_limit_bytes=34 * 2**20),
        cost_estimate=pl.CostEstimate(
            flops=12_000_000_000, bytes_accessed=8_000_000, transcendentals=4_000_000
        ),
        name="cross_forward",
    )(segments, frames, queries, pooled, key_w, value_w, segments[:, None])


def self_forward_kernel(
    group, first_ref, q_ref, k_ref, v_ref, tag_ref, key_tag_ref,
    out_ref, extra_ref, mix_s, top_s, key_s, value_s,
):
    put_halves(key_s, group, k_ref[...], key_tag_ref[...].astype(f32))
    put_halves(value_s, group, v_ref[...], jnp.ones((BLOCK, PAIR), f32))
    left = lane_of(BLOCK) < HD
    half = lane_of(BLOCK) % HD
    row_at = lax.broadcasted_iota(jnp.int32, (BLOCK, BLOCK), 0)
    col_at = lax.broadcasted_iota(jnp.int32, (BLOCK, BLOCK), 1)
    every = [(pair, side) for pair in range(group) for side in range(2)]
    for block in range(q_ref.shape[0] // BLOCK):
        rows = pl.ds(block * BLOCK, BLOCK)
        tags = tag_ref[rows, :].astype(f32)
        queries = [
            halves(q_ref[rows, lanes_of(pair)].astype(f32) * SCALE, tags) for pair in range(group)
        ]
        scores = [dot_nt(queries[pair][side], key_s[pair, side, rows, :]) for pair, side in every]
        scores = [jnp.where(row_at >= col_at, score, -FAR) for score in scores]
        tops = [jnp.max(score, -1, keepdims=True) for score in scores]
        exps = [jnp.exp(score - top).astype(bf16) for score, top in zip(scores, tops)]
        for at, (pair, side) in enumerate(every):
            mix_s[at] = dot_nn(exps[at], value_s[pair, side, rows, :])
            top_s[at] = jnp.broadcast_to(tops[at], (BLOCK, PAIR))

        if block:

            def one_block(other, carry, queries=queries):
                own = pl.ds(pl.multiple_of(other * BLOCK, BLOCK), BLOCK)
                scores = [dot_nt(queries[pair][side], key_s[pair, side, own, :]) for pair, side in every]
                olds = [top_s[at] for at in range(len(every))]
                tops = [
                    jnp.maximum(old, jnp.max(score, -1, keepdims=True))
                    for old, score in zip(olds, scores)
                ]
                exps = [
                    jnp.exp(score - jnp.concatenate([top, top], 1)).astype(bf16)
                    for score, top in zip(scores, tops)
                ]
                for at, (pair, side) in enumerate(every):
                    mix_s[at] = mix_s[at] * jnp.exp(olds[at] - tops[at]) + dot_nn(
                        exps[at], value_s[pair, side, own, :]
                    )
                    top_s[at] = tops[at]
                return carry

            lax.fori_loop(first_ref[block], block, one_block, 0)

        for pair in range(group):
            mix_a, mix_b = mix_s[2 * pair], mix_s[2 * pair + 1]
            total = jnp.where(left, mix_b, mix_a)
            mixed = jnp.where(left, mix_a, mix_b) / pltpu.roll(total, HD, 1)
            log_sum = jnp.where(left, top_s[2 * pair + 1], top_s[2 * pair]) + jnp.log(total)
            out_ref[rows, lanes_of(pair)] = mixed.astype(bf16)
            extra_ref[rows, lanes_of(pair)] = tagged(tags, log_sum, half).astype(bf16)


def packed_spec(rows, group, third):
    return pl.BlockSpec((rows, PAIR * group), lambda p, *_: (0, p + third * (D // PAIR // group)))


def self_forward(first_blocks, packed, tags, key_tag):
    rows = packed.shape[0]
    group = FORWARD_GROUP
    return pl.pallas_call(
        functools.partial(self_forward_kernel, group),
        out_shape=(
            jax.ShapeDtypeStruct((rows, D), bf16),
            jax.ShapeDtypeStruct((rows, D), bf16),
        ),
        grid_spec=pltpu.PrefetchScalarGridSpec(
            num_scalar_prefetch=1,
            grid=(D // PAIR // group,),
            in_specs=[
                packed_spec(rows, group, 0), packed_spec(rows, group, 1), packed_spec(rows, group, 2),
                whole_spec((rows, PAIR)), whole_spec((rows, PAIR)),
            ],
            out_specs=[pair_spec(rows, group), pair_spec(rows, group)],
            scratch_shapes=[pltpu.VMEM((2 * group, BLOCK, PAIR), f32)] * 2
            + [pltpu.VMEM((group, 2, rows, PAIR), bf16)] * 2,
        ),
        compiler_params=pltpu.CompilerParams(vmem_limit_bytes=26 * 2**20),
        cost_estimate=pl.CostEstimate(
            flops=12_000_000_000, bytes_accessed=8_000_000, transcendentals=4_000_000
        ),
        name="self_forward",
    )(first_blocks, packed, packed, packed, tags, key_tag)


def grad_rows(mixed, grad, left, half):
    product = mixed.astype(f32) * grad
    dot_a = jnp.sum(jnp.where(left, product, 0.0), -1, keepdims=True)
    dot_b = jnp.sum(jnp.where(left, 0.0, product), -1, keepdims=True)
    return halves(grad, tagged(jnp.zeros_like(product), jnp.where(left, dot_b, dot_a), half))


def back_step(group, own, queries, grads, turned, key_s, value_s, dq_s, dk_s, dv_s, left,
              masked=None, offset=None, fresh=False):
    every = [(pair, side) for pair in range(group) for side in range(2)]
    scores = [dot_nt(queries[pair][side], key_s[pair, side, own, :]) for pair, side in every]
    slopes = [dot_nt(grads[pair][side], value_s[pair, side, own, :]) for pair, side in every]
    if masked is not None:
        scores = [jnp.where(masked, score, -FAR) for score in scores]
    if offset is not None:
        scores = [score + offset for score in scores]
    probs = [jnp.exp(score) for score in scores]
    backs = [(prob * slope).astype(bf16) for prob, slope in zip(probs, slopes)]
    probs = [prob.astype(bf16) for prob in probs]
    for pair in range(group):
        back_a, back_b = backs[2 * pair : 2 * pair + 2]
        grad = jnp.where(
            left, dot_nn(back_a, key_s[pair, 0, own, :]), dot_nn(back_b, key_s[pair, 1, own, :])
        )
        if fresh:
            dq_s[pair] = grad
        else:
            dq_s[pair] += grad
        query_t, grad_t = turned[pair]
        for side in range(2):
            at = slice(side * HD, (side + 1) * HD)
            dk_s[pair, at, own] += dot_nn(query_t[at], backs[2 * pair + side])
            dv_s[pair, at, own] += dot_nn(grad_t[at], probs[2 * pair + side])


def back_operands(group, rows, q_ref, extra_ref, mixed_ref, grad_ref, left, half):
    queries, grads, turned = [], [], []
    for pair in range(group):
        at = (rows, lanes_of(pair))
        query = q_ref[at].astype(f32) * SCALE
        grad = grad_ref[at]
        queries.append(halves(query, extra_ref[at].astype(f32)))
        grads.append(grad_rows(mixed_ref[at], grad.astype(f32), left, half))
        turned.append((query.astype(bf16).T, grad.T))
    return queries, grads, turned


def cross_backward_kernel(
    group, seg_ref, frame_ref, q_ref, pooled_ref, key_w_ref, value_w_ref, extra_ref, mixed_ref,
    grad_ref, col_ref, dq_ref, dk_ref, dv_ref, key_s, value_s, dk_s, dv_s, dq_s,
):
    ones = ones_tags(BLOCK)
    put_halves(key_s, group, dot_nn(pooled_ref[...], key_w_ref[...]), ones)
    put_halves(value_s, group, dot_nn(pooled_ref[...], value_w_ref[...]), ones)
    dk_s[...] = jnp.zeros_like(dk_s)
    dv_s[...] = jnp.zeros_like(dv_s)
    left = lane_of(BLOCK) < HD
    half = lane_of(BLOCK) % HD
    for block in range(q_ref.shape[0] // BLOCK):
        rows = pl.ds(block * BLOCK, BLOCK)
        operands = back_operands(group, rows, q_ref, extra_ref, mixed_ref, grad_ref, left, half)
        dq_s[...] = jnp.zeros_like(dq_s)

        def one_clip(clip, carry, rows=rows, operands=operands):
            own = pl.ds(pl.multiple_of(frame_ref[clip] * KEYS, KEYS), KEYS)
            offset = jnp.where(col_ref[rows, :] == clip, 0.0, -FAR)
            back_step(group, own, *operands, key_s, value_s, dq_s, dk_s, dv_s, left, offset=offset)
            return carry

        lax.fori_loop(seg_ref[block * BLOCK], seg_ref[block * BLOCK + BLOCK - 1] + 1, one_clip, 0)
        for pair in range(group):
            dq_ref[rows, lanes_of(pair)] = (dq_s[pair] * SCALE).astype(bf16)
    for pair in range(group):
        dk_ref[lanes_of(pair), :] = dk_s[pair].astype(bf16)
        dv_ref[lanes_of(pair), :] = dv_s[pair].astype(bf16)


def cross_backward(segments, frames, queries, pooled, key_w, value_w, extra, mixed, grad):
    rows = queries.shape[0]
    keys = pooled.shape[0]
    group = BACKWARD_GROUP
    upright = pl.BlockSpec((PAIR * group, keys), lambda p, *_: (p, 0))
    own = pair_spec(rows, group)
    return pl.pallas_call(
        functools.partial(cross_backward_kernel, group),
        out_shape=(
            jax.ShapeDtypeStruct((rows, D), bf16),
            jax.ShapeDtypeStruct((D, keys), bf16),
            jax.ShapeDtypeStruct((D, keys), bf16),
        ),
        grid_spec=pltpu.PrefetchScalarGridSpec(
            num_scalar_prefetch=2,
            grid=(D // PAIR // group,),
            in_specs=[
                own,
                whole_spec(pooled.shape),
                pair_spec(key_w.shape[0], group),
                pair_spec(key_w.shape[0], group),
                own, own, own, whole_spec((rows, 1)),
            ],
            out_specs=[own, upright, upright],
            scratch_shapes=[pltpu.VMEM((group, 2, keys, PAIR), bf16)] * 2
            + [pltpu.VMEM((group, PAIR, keys), f32)] * 2
            + [pltpu.VMEM((group, BLOCK, PAIR), f32)],
        ),
        compiler_params=pltpu.CompilerParams(vmem_limit_bytes=VMEM_ASK),
        cost_estimate=pl.CostEstimate(
            flops=24_000_000_000, bytes_accessed=16_000_000, transcendentals=4_000_000
        ),
        name="cross_backward",
    )(segments, frames, queries, pooled, key_w, value_w, extra, mixed, grad, segments[:, None])


def self_backward_kernel(
    group, first_ref, q_ref, k_ref, v_ref, key_tag_ref, extra_ref, mixed_ref, grad_ref,
    dq_ref, dk_ref, dv_ref, key_s, value_s, dk_s, dv_s, dq_s,
):
    key_tag = key_tag_ref[...].astype(f32)
    put_halves(key_s, group, k_ref[...], key_tag)
    put_halves(value_s, group, v_ref[...], key_tag)
    dk_s[...] = jnp.zeros_like(dk_s)
    dv_s[...] = jnp.zeros_like(dv_s)
    left = lane_of(BLOCK) < HD
    half = lane_of(BLOCK) % HD
    row_at = lax.broadcasted_iota(jnp.int32, (BLOCK, BLOCK), 0)
    col_at = lax.broadcasted_iota(jnp.int32, (BLOCK, BLOCK), 1)
    for block in range(q_ref.shape[0] // BLOCK):
        rows = pl.ds(block * BLOCK, BLOCK)
        operands = back_operands(group, rows, q_ref, extra_ref, mixed_ref, grad_ref, left, half)
        back_step(
            group, rows, *operands, key_s, value_s, dq_s, dk_s, dv_s, left,
            masked=row_at >= col_at, fresh=True,
        )
        if block:

            def step(other, carry, operands=operands):
                own = pl.ds(pl.multiple_of(other * BLOCK, BLOCK), BLOCK)
                back_step(group, own, *operands, key_s, value_s, dq_s, dk_s, dv_s, left)
                return carry

            lax.fori_loop(first_ref[block], block, step, 0)
        for pair in range(group):
            dq_ref[rows, lanes_of(pair)] = (dq_s[pair] * SCALE).astype(bf16)
    for pair in range(group):
        dk_ref[:, lanes_of(pair)] = dk_s[pair].T.astype(bf16)
        dv_ref[:, lanes_of(pair)] = dv_s[pair].T.astype(bf16)


def self_backward(first_blocks, packed, key_tag, extra, mixed, grad):
    rows = packed.shape[0]
    group = BACKWARD_GROUP
    own = pair_spec(rows, group)
    return pl.pallas_call(
        functools.partial(self_backward_kernel, group),
        out_shape=(jax.ShapeDtypeStruct((rows, D), bf16),) * 3,
        grid_spec=pltpu.PrefetchScalarGridSpec(
            num_scalar_prefetch=1,
            grid=(D // PAIR // group,),
            in_specs=[
                packed_spec(rows, group, 0), packed_spec(rows, group, 1), packed_spec(rows, group, 2),
                whole_spec((rows, PAIR)),
                own, own, own,
            ],
            out_specs=[own] * 3,
            scratch_shapes=[pltpu.VMEM((group, 2, rows, PAIR), bf16)] * 2
            + [pltpu.VMEM((group, PAIR, rows), f32)] * 2
            + [pltpu.VMEM((group, BLOCK, PAIR), f32)],
        ),
        compiler_params=pltpu.CompilerParams(vmem_limit_bytes=VMEM_ASK),
        cost_estimate=pl.CostEstimate(
            flops=24_000_000_000, bytes_accessed=16_000_000, transcendentals=4_000_000
        ),
        name="self_backward",
    )(first_blocks, packed, packed, packed, key_tag, extra, mixed, grad)


def first_block_table(segment_row):
    clips = jnp.arange(CLIPS, dtype=jnp.int32)
    starts = jnp.sum((segment_row[:, None] < clips[None, :]).astype(jnp.int32), 0)
    heads = segment_row[::BLOCK]
    first = jnp.sum(jnp.where(heads[:, None] == clips[None, :], starts[None, :], 0), 1)
    return (first // BLOCK).astype(jnp.int32)


epsilon = 1e-05
ROOT = math.sqrt(2.0 / math.pi)
CUBE = 0.044715
C = 256
IMG = 64
POOL = 4


TILE = 256


def dot_tn(left, right):
    return lax.dot_general(left, right, (((0,), (0,)), ((), ())), preferred_element_type=f32)


def normalized(values):
    average = jnp.mean(values, -1, keepdims=True)
    centred = values - average
    spread = lax.rsqrt(jnp.mean(centred * centred, -1, keepdims=True) + epsilon)
    return centred * spread, spread


def norm_back(unit, spread, gain, grad):
    scaled = grad * gain
    mean_scaled = jnp.mean(scaled, -1, keepdims=True)
    mean_along = jnp.mean(scaled * unit, -1, keepdims=True)
    lead = tuple(range(grad.ndim - 1))
    return (
        (scaled - mean_scaled - unit * mean_along) * spread,
        jnp.sum(grad * unit, lead),
        jnp.sum(grad, lead),
    )


def gelu_and_slope(value):
    square = value * value
    bent = jnp.tanh(value * (ROOT + (ROOT * CUBE) * square))
    half = 0.5 + 0.5 * bent
    slope = half + value * (0.5 - 0.5 * bent * bent) * (ROOT + (3.0 * ROOT * CUBE) * square)
    return value * half, slope


def tiles_of(count):
    return [pl.ds(at, TILE) for at in range(0, count, TILE)]


def feed_forward_kernel(
    middle_ref, mixed_ref, join_ref, gain_ref, shift_ref, up_ref, bias_ref, down_ref, grad_ref,
    out_ref, second_ref, mixed_grad_ref, join_grad_ref, gain_grad_ref, shift_grad_ref,
    bias_grad_ref, chunk_ref,
    normed_s, grad_t_s, back_s, hidden_s, pre_grad_s, low_s, up_s, down_s, sems,
):
    step = pl.program_id(0)
    steps = pl.num_programs(0)
    rows = middle_ref.shape[0]
    shares, deep = chunk_ref.shape[0], chunk_ref.shape[1] // 2
    group, narrow = D // deep, D // shares

    @pl.when(step == 0)
    def _():
        for at in tiles_of(rows):
            total = middle_ref[at, :] + dot_nn(mixed_ref[at, :], join_ref[...])
            out_ref[at, :] = total
            second_ref[at, :] = total
            unit, _ = normalized(total)
            normed_s[at, :] = (unit * gain_ref[...] + shift_ref[...]).astype(bf16)
            back_s[at, :] = jnp.zeros((TILE, D), f32)
            grad_t_s[:, at] = grad_ref[at, :].T

    bias_grad = jnp.zeros((1, D), f32)
    for at in tiles_of(rows):
        hidden, slope = gelu_and_slope(dot_nn(normed_s[at, :], up_ref[...]) + bias_ref[...])
        hidden = hidden.astype(bf16)
        hidden_s[at, :] = hidden
        pre_grad = (dot_nt(grad_ref[at, :], down_ref[...]) * slope).astype(bf16)
        pre_grad_s[at, :] = pre_grad
        bias_grad += jnp.sum(pre_grad.astype(f32), 0, keepdims=True)
        out_ref[at, :] += dot_nn(hidden, down_ref[...])
        back_s[at, :] += dot_nt(pre_grad, up_ref[...])
    bias_grad_ref[...] = bias_grad
    up_s[step] = dot_tn(pre_grad_s[...], normed_s[...]).astype(bf16).reshape(group, deep, D)
    down_s[step] = dot_nn(grad_t_s[...], hidden_s[...]).astype(bf16).reshape(shares, narrow, D)

    def copies(at):
        return (
            pltpu.make_async_copy(
                up_s.at[at], chunk_ref.at[pl.ds(at * group, group), pl.ds(0, deep)], sems.at[0, at]
            ),
            pltpu.make_async_copy(
                down_s.at[at],
                chunk_ref.at[:, pl.ds(pl.multiple_of(deep + at * narrow, 16), narrow)],
                sems.at[1, at],
            ),
        )

    for copy in copies(step):
        copy.start()

    @pl.when(step == steps - 1)
    def _():
        gain_grad = jnp.zeros((1, D), f32)
        shift_grad = jnp.zeros((1, D), f32)
        for at in tiles_of(rows):
            unit, spread = normalized(second_ref[at, :])
            part, one, two = norm_back(unit, spread, gain_ref[...], back_s[at, :])
            gain_grad += one[None]
            shift_grad += two[None]
            total = grad_ref[at, :].astype(f32) + part
            second_ref[at, :] = total
            low = total.astype(bf16)
            low_s[at, :] = low
            mixed_grad_ref[at, :] = dot_nt(low, join_ref[...]).astype(bf16)
        gain_grad_ref[...] = gain_grad
        shift_grad_ref[...] = shift_grad
        join_grad_ref[...] = dot_tn(low_s[...], mixed_ref[...]).astype(bf16)
        for at in range(FF // D):
            for copy in copies(at):
                copy.wait()


FF = 3072


def still(shape):
    return pl.BlockSpec(shape, lambda *_: (0,) * len(shape), pipeline_mode=pl.Buffered(1))


def feed_forward(middle, mixed, join, gain, shift, up, bias, down, grad, shares):
    rows = middle.shape[0]
    steps = FF // D
    deep = FF // shares
    tall = still((rows, D))
    row = still((1, D))
    return pl.pallas_call(
        feed_forward_kernel,
        out_shape=(
            jax.ShapeDtypeStruct((rows, D), f32),
            jax.ShapeDtypeStruct((rows, D), f32),
            jax.ShapeDtypeStruct((rows, D), bf16),
            jax.ShapeDtypeStruct((D, D), bf16),
            jax.ShapeDtypeStruct((1, D), f32),
            jax.ShapeDtypeStruct((1, D), f32),
            jax.ShapeDtypeStruct((1, FF), f32),
            jax.ShapeDtypeStruct((shares, 2 * deep, D), bf16),
        ),
        grid_spec=pltpu.PrefetchScalarGridSpec(
            num_scalar_prefetch=0,
            grid=(steps,),
            in_specs=[
                tall, tall, still((D, D)), row, row,
                pl.BlockSpec((D, D), lambda j: (0, j)),
                pl.BlockSpec((1, D), lambda j: (0, j)),
                pl.BlockSpec((D, D), lambda j: (j, 0)),
                tall,
            ],
            out_specs=[
                tall, tall, tall, still((D, D)), row, row,
                pl.BlockSpec((1, D), lambda j: (0, j)),
                pl.BlockSpec(memory_space=pl.ANY),
            ],
            scratch_shapes=[
                pltpu.VMEM((rows, D), bf16),
                pltpu.VMEM((D, rows), bf16),
                pltpu.VMEM((rows, D), f32),
                pltpu.VMEM((rows, D), bf16),
                pltpu.VMEM((rows, D), bf16),
                pltpu.VMEM((rows, D), bf16),
                pltpu.VMEM((steps, D // deep, deep, D), bf16),
                pltpu.VMEM((steps, shares, D // shares, D), bf16),
                pltpu.SemaphoreType.DMA((2, steps)),
            ],
        ),
        compiler_params=pltpu.CompilerParams(vmem_limit_bytes=52 * 2**20),
        cost_estimate=pl.CostEstimate(
            flops=34_000_000_000, bytes_accessed=40_000_000, transcendentals=3_200_000
        ),
        name="feed_forward",
    )(middle, mixed, join, gain[None], shift[None], up, bias[None], down, grad)


def project_back_kernel(
    query_ref, key_ref, value_ref, project_ref, middle_ref, second_ref, gain_ref, shift_ref,
    join_ref, mixed_ref,
    middle_grad_ref, mixed_grad_ref, project_grad_ref, join_grad_ref, gain_grad_ref, shift_grad_ref,
    normed_s, low_s,
):
    rows = middle_ref.shape[0]
    gain_grad = jnp.zeros((1, D), f32)
    shift_grad = jnp.zeros((1, D), f32)
    for at in tiles_of(rows):
        back = dot_nt(query_ref[at, :], project_ref[:, 0:D])
        back += dot_nt(key_ref[at, :], project_ref[:, D : 2 * D])
        back += dot_nt(value_ref[at, :], project_ref[:, 2 * D : 3 * D])
        unit, spread = normalized(middle_ref[at, :])
        normed_s[at, :] = (unit * gain_ref[...] + shift_ref[...]).astype(bf16)
        part, one, two = norm_back(unit, spread, gain_ref[...], back)
        gain_grad += one[None]
        shift_grad += two[None]
        total = second_ref[at, :] + part
        middle_grad_ref[at, :] = total
        low = total.astype(bf16)
        low_s[at, :] = low
        mixed_grad_ref[at, :] = dot_nt(low, join_ref[...]).astype(bf16)
    gain_grad_ref[...] = gain_grad
    shift_grad_ref[...] = shift_grad
    project_grad_ref[0:D] = dot_tn(query_ref[...], normed_s[...]).astype(bf16)
    project_grad_ref[D : 2 * D] = dot_tn(key_ref[...], normed_s[...]).astype(bf16)
    project_grad_ref[2 * D : 3 * D] = dot_tn(value_ref[...], normed_s[...]).astype(bf16)
    join_grad_ref[...] = dot_tn(low_s[...], mixed_ref[...]).astype(bf16)


def project_back(query, key, value, project, middle, second, gain, shift, join, mixed):
    rows = middle.shape[0]
    return pl.pallas_call(
        project_back_kernel,
        out_shape=(
            jax.ShapeDtypeStruct((rows, D), f32),
            jax.ShapeDtypeStruct((rows, D), bf16),
            jax.ShapeDtypeStruct((3 * D, D), bf16),
            jax.ShapeDtypeStruct((D, D), bf16),
            jax.ShapeDtypeStruct((1, D), f32),
            jax.ShapeDtypeStruct((1, D), f32),
        ),
        in_specs=[pl.BlockSpec(memory_space=pltpu.VMEM)] * 10,
        out_specs=[pl.BlockSpec(memory_space=pltpu.VMEM)] * 6,
        scratch_shapes=[pltpu.VMEM((rows, D), bf16), pltpu.VMEM((rows, D), bf16)],
        compiler_params=pltpu.CompilerParams(vmem_limit_bytes=52 * 2**20),
        cost_estimate=pl.CostEstimate(
            flops=10_000_000_000, bytes_accessed=30_000_000, transcendentals=2_000
        ),
        name="project_back",
    )(query, key, value, project, middle, second, gain[None], shift[None], join, mixed)


def unpack_kernel(
    row, cross_at, filter_at, share_ref, summed_ref,
    up_ref, down_ref, project_ref, join_ref, cross_join_ref, query_ref, key_ref, value_ref, filter_ref,
):
    deep, model, own = FF // row, D // row, C // row
    up_ref[...] = summed_ref[0:deep, :].astype(f32).T
    for part in range(FF // D):
        at = deep + part * model
        down_ref[:, part * D : (part + 1) * D] = summed_ref[at : at + model, :].astype(f32)
    project_ref[...] = share_ref[0 : 3 * model, :].astype(f32)
    join_ref[...] = share_ref[3 * model : 4 * model, :].astype(f32)
    cross_join_ref[...] = share_ref[4 * model : 5 * model, :].astype(f32)
    query_ref[...] = share_ref[cross_at : cross_at + model, :].astype(f32)
    key_ref[...] = share_ref[cross_at + model : cross_at + 2 * model, 0:C].astype(f32)
    value_ref[...] = share_ref[cross_at + model : cross_at + 2 * model, C : 2 * C].astype(f32)
    for tap in range(9):
        at = filter_at + tap // 3 * own
        lanes = slice(tap % 3 * C, (tap % 3 + 1) * C)
        filter_ref[tap] = share_ref[at : at + own, lanes].astype(f32)


def unpack(share, summed, row, cross_at, filter_at):
    deep, model, own = FF // row, D // row, C // row
    shapes = [
        (D, deep), (model, FF), (3 * model, D), (model, D), (model, D), (model, D), (model, C),
        (model, C), (9, own, C),
    ]
    vmem = pl.BlockSpec(memory_space=pltpu.VMEM)
    return pl.pallas_call(
        functools.partial(unpack_kernel, row, cross_at, filter_at),
        out_shape=tuple(jax.ShapeDtypeStruct(shape, f32) for shape in shapes),
        in_specs=[vmem] * 2,
        out_specs=[vmem] * len(shapes),
        name="unpack",
    )(share, summed)


MESH = pl.DeviceIdType.MESH


def bits_of(count):
    return count.bit_length() - 1


def stream_steps(order, dp_bits, q_bits):
    dp_up = [("dp", b) for b in range(dp_bits)]
    dp_down = dp_up[::-1]
    q_steps = [("q", b) for b in range(q_bits)]
    return {"up": dp_up + q_steps, "down": dp_down + q_steps, "q_up": q_steps + dp_up}[order]


def cut_streams(rows, dp, orders):
    unit = 16 * dp
    units = rows // unit
    plan, at = [], 0
    for number, order in enumerate(orders):
        size = units // len(orders) + (number < units % len(orders))
        if size:
            plan.append((at * unit, size * unit, order))
            at += size
    return plan


def stream_scratch(plan, dp, row, partial):
    dp_bits, q_bits = bits_of(dp), bits_of(row // 2) if partial else 0
    shapes = []
    for _, rows, order in plan:
        lead = q_bits
        shapes.append(pltpu.VMEM((2,) * lead + (rows, D), bf16))
        if partial:
            shapes.append(pltpu.VMEM((2,) * lead + (rows, D), bf16))
        for kind, _ in stream_steps(order, dp_bits, q_bits):
            if kind == "dp":
                rows //= 2
            else:
                lead -= 1
            shapes.append(pltpu.VMEM((2,) * lead + (rows, D), bf16))
    return shapes


class Exchange:
    def __init__(self, dp, row, send_sem, recv_sem, local_sem):
        self.dp, self.row = dp, row
        self.dp_bits, self.q_bits = bits_of(dp), bits_of(row // 2)
        self.me_dp, self.me_row = lax.axis_index("dp"), lax.axis_index("row")
        self.core, self.me_q = lax.rem(self.me_row, 2), self.me_row // 2
        self.send_sem, self.recv_sem, self.local_sem = send_sem, recv_sem, local_sem
        self.remote, self.local, self.started = 0, 0, []

    def bit(self, step):
        kind, b = step
        return lax.rem((self.me_dp if kind == "dp" else self.me_q) // (2**b), 2)

    def partner(self, step):
        kind, b = step
        if kind == "core":
            return self.me_dp, self.me_row + 1 - 2 * self.core
        ahead = (2**b) * (1 - 2 * self.bit(step))
        if kind == "dp":
            return self.me_dp + ahead, self.me_row
        return self.me_dp, self.me_row + 2 * ahead

    def greet(self, devices):
        barrier = pltpu.get_barrier_semaphore()
        for device in devices:
            pl.semaphore_signal(barrier, inc=1, device_id=device, device_id_type=MESH)
        pl.semaphore_wait(barrier, len(devices))

    def push(self, src, dst, device):
        copy = pltpu.make_async_remote_copy(
            src_ref=src, dst_ref=dst, send_sem=self.send_sem.at[self.remote],
            recv_sem=self.recv_sem.at[self.remote], device_id=device, device_id_type=MESH,
        )
        self.remote += 1
        copy.start()
        self.started.append(copy)
        return copy

    def fetch(self, src, dst):
        copy = pltpu.make_async_copy(src, dst, self.local_sem.at[self.local])
        self.local += 1
        copy.start()
        return copy

    def end(self):
        for copy in self.started:
            copy.wait_send()


class Stream:
    def __init__(self, ex, scratch, rows, order, out_ref, out_at, partial):
        self.ex, self.rows, self.off = ex, rows, 0
        self.out_ref, self.out_at = out_ref, out_at
        q_bits = ex.q_bits if partial else 0
        self.q_bits = q_bits
        self.steps = stream_steps(order, ex.dp_bits, q_bits)
        self.todo = list(self.steps)
        self.back = [step for step in self.steps if step[0] == "dp"][::-1]
        self.acc = scratch.pop(0)
        self.landings = [scratch.pop(0) for _ in range(len(self.steps) + partial)]
        self.picked = [None] * q_bits
        self.copies, self.locals, self.landing = [], [], None
        self.gathering, self.done = False, False

    def start_partial(self, segments):
        ex, at = self.ex, 0
        every = (slice(None),) * self.q_bits
        self.landing = self.landings.pop(0)
        for piece, first, rows in segments:
            here = every + (pl.ds(at, rows),)
            there = (pl.ds(first, rows),)
            self.copies.append(
                ex.push(
                    piece.at[every + (1 - ex.core,) + there], self.landing.at[here],
                    ex.partner(("core", 0)),
                )
            )
            self.locals.append(ex.fetch(piece.at[every + (ex.core,) + there], self.acc.at[here]))
            at += rows

    def start_summed(self, source, first):
        self.ex.fetch(source.at[pl.ds(first, self.rows)], self.acc).wait()
        self.send_next()

    def index(self, off, rows):
        picks = tuple(slice(None) if p is None else p for p in self.picked)
        return picks + (pl.ds(pl.multiple_of(off, 16), rows),)

    def send_next(self):
        step = self.todo.pop(0)
        mine = self.ex.bit(step)
        landing = self.landings.pop(0)
        if step[0] == "dp":
            half = self.rows // 2
            src = self.acc.at[self.index(self.off + (1 - mine) * half, half)]
            self.off, self.rows = self.off + mine * half, half
        else:
            place = self.q_bits - 1 - step[1]
            self.picked[place] = 1 - mine
            src = self.acc.at[self.index(self.off, self.rows)]
            self.picked[place] = mine
        self.copies = [self.ex.push(src, landing, self.ex.partner(step))]
        self.landing = landing

    def add_landing(self):
        picks = self.index(0, 16)[:-1]
        lead = (slice(None),) * (len(self.landing.shape) - 2)

        def body(i, carry):
            own = picks + (pl.ds(pl.multiple_of(self.off + i * 16, 16), 16),)
            other = lead + (pl.ds(pl.multiple_of(i * 16, 16), 16),)
            self.acc[own] = (self.acc[own].astype(f32) + self.landing[other].astype(f32)).astype(bf16)
            return carry

        lax.fori_loop(0, self.rows // 16, body, 0)

    def gather_next(self):
        at = pl.ds(pl.multiple_of(self.out_at + self.off, 16), self.rows)
        step = self.back[0]
        self.copies = [self.ex.push(self.out_ref.at[at], self.out_ref.at[at], self.ex.partner(step))]

    def advance(self):
        for copy in self.locals:
            copy.wait()
        self.locals = []
        for copy in self.copies:
            copy.wait_recv()
        if self.gathering:
            step = self.back.pop(0)
            self.off = self.off - self.ex.bit(step) * self.rows
            self.rows *= 2
            if self.back:
                self.gather_next()
            else:
                self.done = True
            return
        self.add_landing()
        if self.todo:
            self.send_next()
            return
        at = pl.ds(pl.multiple_of(self.out_at + self.off, 16), self.rows)
        self.out_ref[at, :] = self.acc[self.index(self.off, self.rows)]
        self.gathering = True
        self.gather_next()


def drain(streams):
    while any(not stream.done for stream in streams):
        for stream in streams:
            if not stream.done:
                stream.advance()


def sum_shares_kernel(dp, row, plan, *refs):
    summed_ref, out_ref = refs[:2]
    scratch, (send_sem, recv_sem, local_sem) = list(refs[2:-3]), refs[-3:]
    ex = Exchange(dp, row, send_sem, recv_sem, local_sem)
    ex.greet([ex.partner(("dp", b)) for b in range(ex.dp_bits)])
    streams = []
    for first, rows, order in plan:
        stream = Stream(ex, scratch, rows, order, out_ref, first, 0)
        stream.start_summed(summed_ref, first)
        streams.append(stream)
    drain(streams)
    ex.end()


def sum_shares(summed, dp, row, orders):
    plan = cut_streams(summed.shape[0], dp, orders)
    copies = 2 * bits_of(dp) * len(plan)
    return pl.pallas_call(
        functools.partial(sum_shares_kernel, dp, row, plan),
        out_shape=jax.ShapeDtypeStruct(summed.shape, bf16),
        in_specs=[pl.BlockSpec(memory_space=pl.ANY)],
        out_specs=pl.BlockSpec(memory_space=pltpu.VMEM),
        scratch_shapes=stream_scratch(plan, dp, row, 0) + [
            pltpu.SemaphoreType.DMA((copies,)),
            pltpu.SemaphoreType.DMA((copies,)),
            pltpu.SemaphoreType.DMA((len(plan),)),
        ],
        compiler_params=pltpu.CompilerParams(
            collective_id=3, has_side_effects=True, vmem_limit_bytes=VMEM_ASK
        ),
        name="sum_shares",
    )(summed)


def row_of(lead, me_row):
    return lead + (me_row,)


def greet_row(row):
    me_dp, me_row = lax.axis_index("dp"), lax.axis_index("row")
    barrier = pltpu.get_barrier_semaphore()
    for ahead in range(1, row):
        pl.semaphore_signal(
            barrier, inc=1, device_id=(me_dp, lax.rem(me_row + ahead, row)), device_id_type=MESH
        )
    pl.semaphore_wait(barrier, row - 1)


def edge_copies(cells, above, below, send_sem, recv_sem, row):
    me_dp, me_row = lax.axis_index("dp"), lax.axis_index("row")
    here = cells.shape[1]
    onward = pltpu.make_async_remote_copy(
        src_ref=cells.at[:, here - 1], dst_ref=above, send_sem=send_sem.at[0],
        recv_sem=recv_sem.at[0], device_id=(me_dp, lax.rem(me_row + 1, row)), device_id_type=MESH,
    )
    back = pltpu.make_async_remote_copy(
        src_ref=cells.at[:, 0], dst_ref=below, send_sem=send_sem.at[1],
        recv_sem=recv_sem.at[1], device_id=(me_dp, lax.rem(me_row + row - 1, row)),
        device_id_type=MESH,
    )
    return onward, back


def start_edges(copies):
    for copy in copies:
        copy.start()


def end_edges(copies):
    for copy in copies:
        copy.wait_send()
        copy.wait_recv()


def put_wide(wide, frame, first, cells):
    column = lax.broadcasted_iota(jnp.int32, cells.shape, 0) % IMG
    cells = cells.astype(f32)
    count = cells.shape[0]
    left = jnp.where(column == 0, 0.0, pltpu.roll(cells, 1, 0))
    right = jnp.where(column == IMG - 1, 0.0, pltpu.roll(cells, count - 1, 0))
    at = pl.ds(first, count)
    wide[frame, at, 0:C] = left.astype(bf16)
    wide[frame, at, C : 2 * C] = cells.astype(bf16)
    wide[frame, at, 2 * C : 3 * C] = right.astype(bf16)


def put_edges(wide, above, below, here, row):
    me_row = lax.axis_index("row")
    keep_above = jnp.where(me_row > 0, 1.0, 0.0)
    keep_below = jnp.where(me_row < row - 1, 1.0, 0.0)
    for frame in range(wide.shape[0]):
        put_wide(wide, frame, 0, above[frame].astype(f32) * keep_above)
        put_wide(wide, frame, (here + 1) * IMG, below[frame].astype(f32) * keep_below)


def conv_forward_kernel(
    row, frames_ref, taps_ref, bias_ref, gain_ref, shift_ref,
    pre_ref, wide_ref, every_ref,
    above_s, below_s, pool_s, edge_send, edge_recv, send_sem, recv_sem,
):
    me_dp, me_row = lax.axis_index("dp"), lax.axis_index("row")
    core, me_q, places = lax.rem(me_row, 2), me_row // 2, row // 2
    count, here = frames_ref.shape[0], frames_ref.shape[1]
    greet_row(row)
    edges = edge_copies(frames_ref, above_s, below_s, edge_send, edge_recv, row)
    start_edges(edges)
    for frame in range(count):
        put_wide(wide_ref, frame, IMG, frames_ref[frame].reshape(here * IMG, C))
    end_edges(edges)
    put_edges(wide_ref, above_s, below_s, here, row)
    tile = POOL * IMG
    for frame in range(count):
        for part in range(here // POOL):
            first = part * tile
            pre = bias_ref[...] + dot_nn(wide_ref[frame, pl.ds(first, tile), :], taps_ref[0])
            pre += dot_nn(wide_ref[frame, pl.ds(first + IMG, tile), :], taps_ref[1])
            pre += dot_nn(wide_ref[frame, pl.ds(first + 2 * IMG, tile), :], taps_ref[2])
            pre_ref[frame, pl.ds(first, tile), :] = pre
            active, _ = gelu_and_slope(pre)
            unit, _ = normalized(active)
            normed = unit * gain_ref[...] + shift_ref[...]
            lines = normed.reshape(POOL, IMG, C)
            lines = lines[0] + lines[1] + lines[2] + lines[3]
            cells = IMG // POOL
            for side in range(C // PAIR):
                lanes = slice(side * PAIR, (side + 1) * PAIR)
                pool_s[side] = lines[:, lanes]
                total = pool_s[side, pl.ds(0, cells, stride=POOL), :]
                for at in range(1, POOL):
                    total += pool_s[side, pl.ds(at, cells, stride=POOL), :]
                every_ref[frame, me_row, pl.ds(part * cells, cells), lanes] = (
                    total * (1.0 / (POOL * POOL))
                ).astype(bf16)

    def push(source_row, to_row, at):
        copy = pltpu.make_async_remote_copy(
            src_ref=every_ref.at[:, source_row], dst_ref=every_ref.at[:, source_row],
            send_sem=send_sem.at[at], recv_sem=recv_sem.at[at], device_id=(me_dp, to_row),
            device_id_type=MESH,
        )
        copy.start()
        return copy

    other = me_row + 1 - 2 * core
    copies = [push(me_row, other, 0)]
    for ahead in range(1, places):
        copies.append(push(me_row, lax.rem(me_q + ahead, places) * 2 + core, ahead))
    for ahead in range(1, places):
        copies[ahead].wait_recv()
        came = lax.rem(me_q + places - ahead, places) * 2 + core
        copies.append(push(came, other, places - 1 + ahead))
    copies[0].wait_recv()
    for copy in copies[places:]:
        copy.wait_recv()
    for copy in copies:
        copy.wait_send()


def conv_forward(frames, taps, bias, gain, shift, row):
    count, here = frames.shape[0], frames.shape[1]
    keys = (here // POOL) * (IMG // POOL)
    return pl.pallas_call(
        functools.partial(conv_forward_kernel, row),
        out_shape=(
            jax.ShapeDtypeStruct((count, here * IMG, C), f32),
            jax.ShapeDtypeStruct((count, (here + 2) * IMG, 3 * C), bf16),
            jax.ShapeDtypeStruct((count, row, keys, C), bf16),
        ),
        in_specs=[pl.BlockSpec(memory_space=pltpu.VMEM)] * 5,
        out_specs=[pl.BlockSpec(memory_space=pltpu.VMEM)] * 3,
        scratch_shapes=[
            pltpu.VMEM((count, IMG, C), bf16),
            pltpu.VMEM((count, IMG, C), bf16),
            pltpu.VMEM((C // PAIR, IMG, PAIR), f32),
            pltpu.SemaphoreType.DMA((2,)),
            pltpu.SemaphoreType.DMA((2,)),
            pltpu.SemaphoreType.DMA((row,)),
            pltpu.SemaphoreType.DMA((row,)),
        ],
        compiler_params=pltpu.CompilerParams(
            collective_id=1, has_side_effects=True, vmem_limit_bytes=20 * 2**20
        ),
        name="conv_forward",
    )(frames, taps.reshape(3, 3 * C, C), bias[None], gain[None], shift[None])


READY_ORDERS = ("up", "down", "up", "down")
CROSS_ORDERS = ("q_up", "up", "down")
FILTER_ORDERS = ("up", "down")


def segments_of(pieces, first, rows):
    parts, at = [], 0
    for piece, start, count in pieces:
        low, high = max(first, at), min(first + rows, at + count)
        if low < high:
            parts.append((piece, start + low - at, high - low))
        at += count
    return parts


def finish_kernel(
    dp, row, plans,
    project_ref, join_ref, cross_join_ref, query_grad_ref, x_ref, query_w_ref, middle_grad_ref,
    keys_grad_ref, values_grad_ref, every_ref, key_w_ref, value_w_ref, pre_ref, wide_ref, taps_ref,
    gain_ref, small_ref,
    tokens_grad_ref, frames_grad_ref, share_ref,
    query_s, both_s, filter_s, x_s, query_w_s, pre_s, wide_in_s, taps_s, keys_grad_s, values_grad_s,
    part_s, landing_s, sum_s, arrive_s, spread_s, grad_s, grad_t_s, wide_s, above_s, below_s,
    edge_send, edge_recv, send_sem, recv_sem, local_sem, *scratch,
):
    scratch = list(scratch)
    ex = Exchange(dp, row, send_sem, recv_sem, local_sem)
    me_dp, me_row, core, me_q, places = ex.me_dp, ex.me_row, ex.core, ex.me_q, row // 2
    count, here = grad_s.shape[0], grad_s.shape[1]
    keys = part_s.shape[3]
    model, own = D // row, C // row
    ex.greet(
        [(me_dp, lax.rem(me_row + ahead, row)) for ahead in range(1, row)]
        + [ex.partner(("dp", b)) for b in range(ex.dp_bits)]
    )
    keys_in = ex.fetch(keys_grad_ref, keys_grad_s)
    values_in = ex.fetch(values_grad_ref, values_grad_s)
    base, groups = 0, []
    for plan in plans:
        groups.append([
            Stream(ex, scratch, rows, order, share_ref, base + first, 1) for first, rows, order in plan
        ])
        base += sum(rows for _, rows, _ in plan)
    ready, crossed, filtered = groups

    def start(group, plan, pieces):
        for stream, (first, rows, _) in zip(group, plan):
            stream.start_partial(segments_of(pieces, first, rows))

    used = 5 * model
    total_rows = sum(rows for _, rows, _ in plans[0])
    start(ready, plans[0], [
        (project_ref, 0, 3 * model), (join_ref, 0, model), (cross_join_ref, 0, model),
        (project_ref, 0, total_rows - used),
    ])
    x_in = ex.fetch(x_ref, x_s)
    query_in = ex.fetch(query_w_ref, query_w_s)
    pre_in = ex.fetch(pre_ref, pre_s)
    wide_in = ex.fetch(wide_ref, wide_in_s)
    taps_in = ex.fetch(taps_ref, taps_s)

    keys_in.wait()
    part = lax.dot_general(
        keys_grad_s[...], key_w_ref[...], (((0,), (1,)), ((), ())), preferred_element_type=f32
    )
    values_in.wait()
    part += lax.dot_general(
        values_grad_s[...], value_w_ref[...], (((0,), (1,)), ((), ())), preferred_element_type=f32
    )
    part_s[...] = part.astype(bf16).reshape(count, places, 2, keys, C)
    pooled_core = ex.push(part_s.at[:, :, 1 - core], landing_s, ex.partner(("core", 0)))

    split = (2,) * ex.q_bits + (2,)
    lines = both_s.shape[-2]
    for at, grad_ref in enumerate((keys_grad_s, values_grad_s)):
        both_s[..., 0:model, at * C : (at + 1) * C] = (
            dot_nn(grad_ref[...], every_ref[...]).astype(bf16).reshape(split + (model, C))
        )
    both_s[..., 0:model, 2 * C : 3 * C] = jnp.zeros(split + (model, C), bf16)
    if lines > model:
        both_s[..., model:lines, :] = jnp.zeros(split + (lines - model, D), bf16)
    x_in.wait()
    query_s[...] = dot_tn(query_grad_ref[...], x_s[...]).astype(bf16).reshape(split + (model, D))
    start(crossed, plans[1], [(query_s, 0, model), (both_s, 0, lines)])

    pooled_core.wait_recv()
    sum_s[...] = (part_s[:, :, core].astype(f32) + landing_s[...].astype(f32)).astype(bf16)
    pooled_in = []
    for ahead in range(1, places):
        to = lax.rem(me_q + ahead, places)
        pooled_in.append(ex.push(sum_s.at[:, to], arrive_s.at[ahead - 1], (me_dp, to * 2 + core)))
    for stream in ready:
        stream.advance()
    query_in.wait()
    for at in tiles_of(x_s.shape[0]):
        tokens_grad_ref[at, :] = middle_grad_ref[at, :] + dot_nt(query_grad_ref[at, :], query_w_s[...])
    for copy in pooled_in:
        copy.wait_recv()
    pooled = sum_s[:, me_q].astype(f32)
    for ahead in range(1, places):
        pooled += arrive_s[ahead - 1].astype(f32)
    pooled = pooled * (1.0 / (POOL * POOL))
    for stream in crossed:
        stream.advance()

    tile = POOL * IMG
    cells = IMG // POOL
    bias_grad = jnp.zeros((1, C), f32)
    gain_grad = jnp.zeros((1, C), f32)
    shift_grad = jnp.zeros((1, C), f32)
    pre_in.wait()
    for frame in range(count):
        for part in range(here // POOL):
            for side in range(C // PAIR):
                own_cells = pooled[
                    frame, part * cells : (part + 1) * cells, side * PAIR : (side + 1) * PAIR
                ]
                for at in range(POOL):
                    spread_s[side, pl.ds(at, cells, stride=POOL), :] = own_cells
            line = jnp.concatenate([spread_s[side] for side in range(C // PAIR)], 1)
            back = jnp.broadcast_to(line[None], (POOL, IMG, C)).reshape(tile, C)
            active, slope = gelu_and_slope(pre_s[frame, pl.ds(part * tile, tile), :])
            unit, spread = normalized(active)
            grad, one, two = norm_back(unit, spread, gain_ref[...], back)
            gain_grad += one[None]
            shift_grad += two[None]
            grad = (slope * grad).astype(bf16)
            bias_grad += jnp.sum(grad.astype(f32), 0, keepdims=True)
            grad_s[frame, pl.ds(part * POOL, POOL)] = grad.reshape(POOL, IMG, C)
    edges = edge_copies(grad_s, above_s, below_s, edge_send, edge_recv, row)
    start_edges(edges)
    for frame in range(count):
        cells_here = grad_s[frame].reshape(here * IMG, C)
        put_wide(wide_s, frame, IMG, cells_here)
        grad_t_s[frame] = cells_here.T
    for stream in ready[:3]:
        stream.advance()
    wide_in.wait()
    for dy in range(3):
        total = None
        for frame in range(count):
            piece = dot_nn(grad_t_s[frame], wide_in_s[frame, pl.ds(dy * IMG, here * IMG), :])
            total = piece if total is None else total + piece
        filter_s[..., dy * own : (dy + 1) * own, :] = total.astype(bf16).reshape(split + (own, D))
    lines = filter_s.shape[-2] - 3 * own
    line_at = lax.broadcasted_iota(jnp.int32, (lines, D), 0)
    extra = jnp.zeros((lines, D), f32)
    for at, item in enumerate((bias_grad, gain_grad, shift_grad)):
        item = jnp.concatenate([item, jnp.zeros((1, D - C), f32)], 1)
        extra = jnp.where(line_at == 8 + at, item, extra)
    for place in range(places):
        for side in range(2):
            index = tuple((place >> b) & 1 for b in reversed(range(ex.q_bits))) + (side,)
            own_small = small_ref[place * 2 + side].astype(f32)
            filter_s[index + (slice(3 * own, 3 * own + lines),)] = (own_small + extra).astype(bf16)
    start(filtered, plans[2], [(filter_s, 0, 3 * own + lines)])
    for stream in ready[3:] + crossed:
        stream.advance()
    end_edges(edges)
    put_edges(wide_s, above_s, below_s, here, row)
    taps_in.wait()
    for frame in range(count):
        for part in range(here // POOL):
            total = None
            for tap in range(9):
                dy, dx = tap // 3, tap % 3
                window = wide_s[frame, pl.ds(part * tile + dy * IMG, tile), dx * C : (dx + 1) * C]
                piece = dot_nt(window, taps_s[8 - tap])
                total = piece if total is None else total + piece
            frames_grad_ref[frame, pl.ds(part * tile, tile), :] = total
        if frame == 0:
            for stream in filtered:
                stream.advance()
        if frame == 1:
            for stream in ready:
                stream.advance()
    drain(filtered + ready + crossed)
    ex.end()


def finish(project_grad, join_grad, cross_join_grad, query_grad, x, query_w, middle_grad,
           keys_grad_t, values_grad_t, everyone, key_w, value_w, pre, wide, taps, gain, small, dp, row):
    unit = 16 * dp
    model, own = D // row, C // row
    count, here = pre.shape[0], pre.shape[1] // IMG
    keys = (here // POOL) * (IMG // POOL)
    whole_units = lambda rows: -(-rows // unit) * unit
    rows = [whole_units(5 * model), whole_units(2 * model), 3 * own + small.shape[1]]
    plans = [
        cut_streams(count_rows, dp, orders)
        for count_rows, orders in zip(rows, (READY_ORDERS, CROSS_ORDERS, FILTER_ORDERS))
    ]
    split = (2,) * bits_of(row // 2) + (2,)
    view = lambda piece: piece.reshape(split + (piece.shape[0] // row, D))
    streams = [stream for plan in plans for stream in plan]
    per_stream = 2 * bits_of(dp) + bits_of(row // 2)
    remote = per_stream * len(streams) + 8 * len(streams) + row
    local = 8 * len(streams) + 8
    vmem = pl.BlockSpec(memory_space=pltpu.VMEM)
    away = pl.BlockSpec(memory_space=pl.ANY)
    return pl.pallas_call(
        functools.partial(finish_kernel, dp, row, plans),
        out_shape=(
            jax.ShapeDtypeStruct(x.shape, f32),
            jax.ShapeDtypeStruct(pre.shape, f32),
            jax.ShapeDtypeStruct((sum(rows), D), bf16),
        ),
        in_specs=[
            away, away, away, vmem, away, away, vmem, away, away, vmem, vmem, vmem, away, away, away,
            vmem, vmem,
        ],
        out_specs=[vmem] * 3,
        scratch_shapes=[
            pltpu.VMEM(split + (model, D), bf16),
            pltpu.VMEM(split + (rows[1] - model, D), bf16),
            pltpu.VMEM(split + (rows[2], D), bf16),
            pltpu.VMEM(x.shape, bf16),
            pltpu.VMEM(query_w.shape, bf16),
            pltpu.VMEM(pre.shape, f32),
            pltpu.VMEM(wide.shape, bf16),
            pltpu.VMEM(taps.shape, bf16),
            pltpu.VMEM(keys_grad_t.shape, bf16),
            pltpu.VMEM(values_grad_t.shape, bf16),
            pltpu.VMEM((count, row // 2, 2, keys, C), bf16),
            pltpu.VMEM((count, row // 2, keys, C), bf16),
            pltpu.VMEM((count, row // 2, keys, C), bf16),
            pltpu.VMEM((row // 2 - 1, count, keys, C), bf16),
            pltpu.VMEM((C // PAIR, IMG, PAIR), f32),
            pltpu.VMEM((count, here, IMG, C), bf16),
            pltpu.VMEM((count, C, here * IMG), bf16),
            pltpu.VMEM((count, (here + 2) * IMG, 3 * C), bf16),
            pltpu.VMEM((count, IMG, C), bf16),
            pltpu.VMEM((count, IMG, C), bf16),
            pltpu.SemaphoreType.DMA((2,)),
            pltpu.SemaphoreType.DMA((2,)),
            pltpu.SemaphoreType.DMA((remote,)),
            pltpu.SemaphoreType.DMA((remote,)),
            pltpu.SemaphoreType.DMA((local,)),
        ] + [shape for plan in plans for shape in stream_scratch(plan, dp, row, 1)],
        compiler_params=pltpu.CompilerParams(
            collective_id=2, has_side_effects=True, vmem_limit_bytes=54 * 2**20
        ),
        name="finish",
    )(
        view(project_grad), view(join_grad), view(cross_join_grad), query_grad, x, query_w,
        middle_grad, keys_grad_t, values_grad_t, everyone, key_w, value_w, pre, wide, taps,
        gain[None], small,
    )


def fast_dot(left, right):
    return jnp.dot(left, right, preferred_element_type=f32)


def shared_rows(matrix, count):
    return matrix.reshape(count, matrix.shape[0] // count, matrix.shape[1])


def on_device(
    frames, tokens, segment_ids, clip_frame, filter_weight, filter_bias, context_gain,
    context_shift, cross_query, cross_key, cross_value, cross_output, first_gain, first_shift,
    self_project, self_output, second_gain, second_shift, up_weight, up_bias, down_weight, cotangent,
):
    shares = lax.axis_size("row")
    x = tokens[0]
    segments = segment_ids[0]
    clip_frames = clip_frame[0]
    out_grad = cotangent[0]
    tags = segment_tags(segments)
    key_tag = key_tags(segments)
    first_blocks = first_block_table(segments)

    pre_act, wide, everyone = conv_forward(
        frames, filter_weight, filter_bias, context_gain, context_shift, shares
    )
    everyone = everyone.reshape(-1, C)
    cross_q = fast_dot(x, cross_query).astype(bf16)
    cross_mixed, cross_extra = cross_forward(
        segments, clip_frames, cross_q, everyone, cross_key, cross_value
    )
    middle = x.astype(f32) + fast_dot(cross_mixed, cross_output)
    first_unit, first_spread = normalized(middle)
    first_normed = (first_unit * first_gain + first_shift).astype(bf16)
    packed = fast_dot(first_normed, self_project).astype(bf16)
    self_mixed, self_extra = self_forward(first_blocks, packed, tags, key_tag)
    (
        output, second_grad, self_mixed_grad, join_grad, second_gain_grad,
        second_shift_grad, up_bias_grad, chunk_a,
    ) = feed_forward(
        middle, self_mixed, self_output, second_gain, second_shift, up_weight, up_bias, down_weight,
        out_grad, shares,
    )
    share_a = lax.psum_scatter(chunk_a, "row", scatter_dimension=0, tiled=False)
    query_grad, key_grad, value_grad = self_backward(
        first_blocks, packed, key_tag, self_extra, self_mixed, self_mixed_grad
    )
    (
        middle_grad, cross_mixed_grad, project_grad, cross_join_grad, first_gain_grad,
        first_shift_grad,
    ) = project_back(
        query_grad, key_grad, value_grad, self_project, middle, second_grad, first_gain, first_shift,
        cross_output, cross_mixed,
    )
    cross_q_grad, keys_grad_t, values_grad_t = cross_backward(
        segments, clip_frames, cross_q, everyone, cross_key, cross_value, cross_extra, cross_mixed,
        cross_mixed_grad,
    )
    dp = lax.axis_size("dp")
    small = jnp.concatenate(
        [
            item.astype(bf16).reshape(shares, -1)
            for item in (
                first_gain_grad, first_shift_grad, second_gain_grad, second_shift_grad, up_bias_grad,
            )
        ],
        1,
    )
    lines = 16 + -(3 * C // shares + 16) % (16 * dp)
    small = jnp.pad(small, ((0, 0), (0, lines * D - small.shape[1]))).reshape(shares, lines, D)
    tokens_grad, frames_grad, reduced = finish(
        project_grad, join_grad, cross_join_grad, cross_q_grad, x, cross_query, middle_grad,
        keys_grad_t, values_grad_t, everyone, cross_key, cross_value, pre_act, wide, filter_weight,
        context_gain, small, dp, shares,
    )
    share_a = sum_shares(share_a, dp, shares, ("up", "down"))
    own_part = C // shares
    filter_at = reduced.shape[0] - (3 * own_part + lines)
    cross_at = filter_at - -(-2 * D // shares // (16 * dp)) * 16 * dp
    (
        up_grad, down_grad, project_grad, self_output_grad, cross_output_grad, cross_query_grad,
        cross_key_grad, cross_value_grad, filter_grad,
    ) = unpack(reduced, share_a, shares, cross_at, filter_at)
    late = reduced[filter_at + 3 * own_part :].astype(f32)
    flat = late[:2].reshape(-1)
    sizes = [D // shares] * 4 + [3072 // shares]
    ends = [sum(sizes[: i + 1]) for i in range(len(sizes))]
    vectors = [flat[e - s : e] for e, s in zip(ends, sizes)]
    mine = lax.dynamic_slice_in_dim(late[8:11, :C], lax.axis_index("row") * own_part, own_part, 1)
    vectors = vectors + [mine[0], mine[1], mine[2]]
    return (
        middle[None],
        output[None],
        tokens_grad[None],
        frames_grad.reshape(frames.shape),
        jnp.transpose(filter_grad, (0, 2, 1)),
        vectors[5],
        vectors[6],
        vectors[7],
        cross_query_grad.T,
        cross_key_grad.T,
        cross_value_grad.T,
        cross_output_grad.T,
        vectors[0],
        vectors[1],
        project_grad.T,
        self_output_grad.T,
        vectors[2],
        vectors[3],
        up_grad,
        vectors[4],
        down_grad.T,
    )


def solution(mesh):
    whole = P()
    by_row = P(("dp", "row"), None, None)
    in_specs = (
        P("dp", "row", None, None),
        by_row,
        P(("dp", "row"), None),
        P(("dp", "row"), None),
    ) + (whole,) * 17 + (by_row,)
    columns = P(None, "row")
    vector = P("row")
    out_specs = (
        by_row, by_row, by_row, P("dp", "row", None, None), P(None, None, "row"), vector, vector,
        vector, columns, columns, columns, columns, vector, vector, columns, columns, vector, vector,
        columns, vector, columns,
    )
    return jax.shard_map(
        on_device, mesh=mesh, in_specs=in_specs, out_specs=out_specs, check_vma=False
    )
```

```python
import functools
import math
import jax
import jax.numpy as jnp
from jax import lax
from jax.experimental import pallas as pl
from jax.experimental.pallas import tpu as pltpu
from jax.sharding import PartitionSpec as P

D = 768
HD = 64
PAIR = 128
BLOCK = 256
KEYS = 256
CLIPS = 4
FAR = 2.0**100
SCALE = 0.125
CROSS_GROUP = 6
FORWARD_GROUP = 3
BACKWARD_GROUP = 3
f32 = jnp.float32
bf16 = jnp.bfloat16
VMEM_ASK = 48 * 2**20


def lane_of(rows):
    return lax.broadcasted_iota(jnp.int32, (rows, PAIR), 1)


def dot_nt(left, right):
    return lax.dot_general(left, right, (((1,), (1,)), ((), ())), preferred_element_type=f32)


def dot_nn(left, right):
    return lax.dot_general(left, right, (((1,), (0,)), ((), ())), preferred_element_type=f32)


def tagged(extra, value, half):
    high = value.astype(bf16).astype(f32)
    rest = value - high
    middle = rest.astype(bf16).astype(f32)
    extra = jnp.where(half == 8, -high, extra)
    extra = jnp.where(half == 9, -middle, extra)
    return jnp.where(half == 10, middle - rest, extra)


def segment_tags(segment_row):
    lane = jnp.arange(PAIR, dtype=jnp.int32) % HD
    wrong = (lane[None, :] < CLIPS) & (lane[None, :] != segment_row[:, None])
    return jnp.where(wrong, -FAR, 0.0).astype(bf16)


def key_tags(segment_row):
    lane = jnp.arange(PAIR, dtype=jnp.int32) % HD
    ones = (lane[None, :] == segment_row[:, None]) | ((lane[None, :] >= 8) & (lane[None, :] <= 10))
    return jnp.where(ones, 1.0, 0.0).astype(bf16)


def ones_tags(rows):
    half = lane_of(rows) % HD
    return jnp.where((half >= 8) & (half <= 10), 1.0, 0.0)


def halves(value, filler):
    left = lane_of(value.shape[0]) < HD
    value = value.astype(f32)
    return jnp.where(left, value, filler).astype(bf16), jnp.where(left, filler, value).astype(bf16)


def put_halves(store, group, value, filler):
    for pair in range(group):
        for at in range(0, value.shape[0], BLOCK):
            rows = slice(at, at + BLOCK)
            fill = filler if filler.shape[0] == BLOCK else filler[rows, :]
            one, two = halves(value[rows, pair * PAIR : (pair + 1) * PAIR], fill)
            store[pair, 0, rows, :] = one
            store[pair, 1, rows, :] = two


def lanes_of(pair):
    return slice(pair * PAIR, (pair + 1) * PAIR)


def cross_forward_kernel(
    group, seg_ref, frame_ref, q_ref, pooled_ref, key_w_ref, value_w_ref, col_ref,
    out_ref, extra_ref, key_s, value_s,
):
    put_halves(key_s, group, dot_nn(pooled_ref[...], key_w_ref[...]), jnp.zeros((BLOCK, PAIR), f32))
    put_halves(value_s, group, dot_nn(pooled_ref[...], value_w_ref[...]), jnp.ones((BLOCK, PAIR), f32))
    left = lane_of(BLOCK) < HD
    half = lane_of(BLOCK) % HD
    for block in range(q_ref.shape[0] // BLOCK):
        rows = pl.ds(block * BLOCK, BLOCK)
        queries = [
            (q_ref[rows, lanes_of(pair)].astype(f32) * SCALE).astype(bf16) for pair in range(group)
        ]

        def one_clip(clip, carry, rows=rows, queries=queries):
            own = pl.ds(pl.multiple_of(frame_ref[clip] * KEYS, KEYS), KEYS)
            mine = col_ref[rows, :] == clip
            scores = [
                dot_nt(queries[pair], key_s[pair, side, own, :])
                for pair in range(group)
                for side in range(2)
            ]
            tops = [jnp.max(score, -1, keepdims=True) for score in scores]
            exps = [jnp.exp(score - top).astype(bf16) for score, top in zip(scores, tops)]
            mixes = [
                dot_nn(exps[2 * pair + side], value_s[pair, side, own, :])
                for pair in range(group)
                for side in range(2)
            ]
            for pair in range(group):
                mix_a, mix_b = mixes[2 * pair : 2 * pair + 2]
                top_a, top_b = tops[2 * pair : 2 * pair + 2]
                total = jnp.where(left, mix_b, mix_a)
                mixed = jnp.where(left, mix_a, mix_b) / pltpu.roll(total, HD, 1)
                log_sum = jnp.where(left, top_b, top_a) + jnp.log(total)
                extra = tagged(jnp.zeros((BLOCK, PAIR), f32), log_sum, half)
                at = (rows, lanes_of(pair))
                out_ref[at] = jnp.where(mine, mixed, out_ref[at].astype(f32)).astype(bf16)
                extra_ref[at] = jnp.where(mine, extra, extra_ref[at].astype(f32)).astype(bf16)
            return carry

        lax.fori_loop(seg_ref[block * BLOCK], seg_ref[block * BLOCK + BLOCK - 1] + 1, one_clip, 0)


def pair_spec(rows, group):
    return pl.BlockSpec((rows, PAIR * group), lambda p, *_: (0, p))


def whole_spec(shape):
    return pl.BlockSpec(shape, lambda p, *_: (0,) * len(shape), pipeline_mode=pl.Buffered(1))


def cross_forward(segments, frames, queries, pooled, key_w, value_w):
    rows = queries.shape[0]
    keys = pooled.shape[0]
    group = CROSS_GROUP
    return pl.pallas_call(
        functools.partial(cross_forward_kernel, group),
        out_shape=(
            jax.ShapeDtypeStruct((rows, D), bf16),
            jax.ShapeDtypeStruct((rows, D), bf16),
        ),
        grid_spec=pltpu.PrefetchScalarGridSpec(
            num_scalar_prefetch=2,
            grid=(D // PAIR // group,),
            in_specs=[
                pair_spec(rows, group),
                whole_spec(pooled.shape),
                pair_spec(key_w.shape[0], group),
                pair_spec(key_w.shape[0], group),
                whole_spec((rows, 1)),
            ],
            out_specs=[pair_spec(rows, group), pair_spec(rows, group)],
            scratch_shapes=[pltpu.VMEM((group, 2, keys, PAIR), bf16)] * 2,
        ),
        compiler_params=pltpu.CompilerParams(vmem_limit_bytes=34 * 2**20),
        cost_estimate=pl.CostEstimate(
            flops=12_000_000_000, bytes_accessed=8_000_000, transcendentals=4_000_000
        ),
        name="cross_forward",
    )(segments, frames, queries, pooled, key_w, value_w, segments[:, None])


def self_forward_kernel(
    group, first_ref, q_ref, k_ref, v_ref, tag_ref, key_tag_ref,
    out_ref, extra_ref, mix_s, top_s, key_s, value_s,
):
    put_halves(key_s, group, k_ref[...], key_tag_ref[...].astype(f32))
    put_halves(value_s, group, v_ref[...], jnp.ones((BLOCK, PAIR), f32))
    left = lane_of(BLOCK) < HD
    half = lane_of(BLOCK) % HD
    row_at = lax.broadcasted_iota(jnp.int32, (BLOCK, BLOCK), 0)
    col_at = lax.broadcasted_iota(jnp.int32, (BLOCK, BLOCK), 1)
    every = [(pair, side) for pair in range(group) for side in range(2)]
    for block in range(q_ref.shape[0] // BLOCK):
        rows = pl.ds(block * BLOCK, BLOCK)
        tags = tag_ref[rows, :].astype(f32)
        queries = [
            halves(q_ref[rows, lanes_of(pair)].astype(f32) * SCALE, tags) for pair in range(group)
        ]
        scores = [dot_nt(queries[pair][side], key_s[pair, side, rows, :]) for pair, side in every]
        scores = [jnp.where(row_at >= col_at, score, -FAR) for score in scores]
        tops = [jnp.max(score, -1, keepdims=True) for score in scores]
        exps = [jnp.exp(score - top).astype(bf16) for score, top in zip(scores, tops)]
        for at, (pair, side) in enumerate(every):
            mix_s[at] = dot_nn(exps[at], value_s[pair, side, rows, :])
            top_s[at] = jnp.broadcast_to(tops[at], (BLOCK, PAIR))

        if block:

            def one_block(other, carry, queries=queries):
                own = pl.ds(pl.multiple_of(other * BLOCK, BLOCK), BLOCK)
                scores = [dot_nt(queries[pair][side], key_s[pair, side, own, :]) for pair, side in every]
                olds = [top_s[at] for at in range(len(every))]
                tops = [
                    jnp.maximum(old, jnp.max(score, -1, keepdims=True))
                    for old, score in zip(olds, scores)
                ]
                exps = [
                    jnp.exp(score - jnp.concatenate([top, top], 1)).astype(bf16)
                    for score, top in zip(scores, tops)
                ]
                for at, (pair, side) in enumerate(every):
                    mix_s[at] = mix_s[at] * jnp.exp(olds[at] - tops[at]) + dot_nn(
                        exps[at], value_s[pair, side, own, :]
                    )
                    top_s[at] = tops[at]
                return carry

            lax.fori_loop(first_ref[block], block, one_block, 0)

        for pair in range(group):
            mix_a, mix_b = mix_s[2 * pair], mix_s[2 * pair + 1]
            total = jnp.where(left, mix_b, mix_a)
            mixed = jnp.where(left, mix_a, mix_b) / pltpu.roll(total, HD, 1)
            log_sum = jnp.where(left, top_s[2 * pair + 1], top_s[2 * pair]) + jnp.log(total)
            out_ref[rows, lanes_of(pair)] = mixed.astype(bf16)
            extra_ref[rows, lanes_of(pair)] = tagged(tags, log_sum, half).astype(bf16)


def packed_spec(rows, group, third):
    return pl.BlockSpec((rows, PAIR * group), lambda p, *_: (0, p + third * (D // PAIR // group)))


def self_forward(first_blocks, packed, tags, key_tag):
    rows = packed.shape[0]
    group = FORWARD_GROUP
    return pl.pallas_call(
        functools.partial(self_forward_kernel, group),
        out_shape=(
            jax.ShapeDtypeStruct((rows, D), bf16),
            jax.ShapeDtypeStruct((rows, D), bf16),
        ),
        grid_spec=pltpu.PrefetchScalarGridSpec(
            num_scalar_prefetch=1,
            grid=(D // PAIR // group,),
            in_specs=[
                packed_spec(rows, group, 0), packed_spec(rows, group, 1), packed_spec(rows, group, 2),
                whole_spec((rows, PAIR)), whole_spec((rows, PAIR)),
            ],
            out_specs=[pair_spec(rows, group), pair_spec(rows, group)],
            scratch_shapes=[pltpu.VMEM((2 * group, BLOCK, PAIR), f32)] * 2
            + [pltpu.VMEM((group, 2, rows, PAIR), bf16)] * 2,
        ),
        compiler_params=pltpu.CompilerParams(vmem_limit_bytes=26 * 2**20),
        cost_estimate=pl.CostEstimate(
            flops=12_000_000_000, bytes_accessed=8_000_000, transcendentals=4_000_000
        ),
        name="self_forward",
    )(first_blocks, packed, packed, packed, tags, key_tag)


def grad_rows(mixed, grad, left, half):
    product = mixed.astype(f32) * grad
    dot_a = jnp.sum(jnp.where(left, product, 0.0), -1, keepdims=True)
    dot_b = jnp.sum(jnp.where(left, 0.0, product), -1, keepdims=True)
    return halves(grad, tagged(jnp.zeros_like(product), jnp.where(left, dot_b, dot_a), half))


def back_step(group, own, queries, grads, turned, key_s, value_s, dq_s, dk_s, dv_s, left,
              masked=None, offset=None, fresh=False):
    every = [(pair, side) for pair in range(group) for side in range(2)]
    scores = [dot_nt(queries[pair][side], key_s[pair, side, own, :]) for pair, side in every]
    slopes = [dot_nt(grads[pair][side], value_s[pair, side, own, :]) for pair, side in every]
    if masked is not None:
        scores = [jnp.where(masked, score, -FAR) for score in scores]
    if offset is not None:
        scores = [score + offset for score in scores]
    probs = [jnp.exp(score) for score in scores]
    backs = [(prob * slope).astype(bf16) for prob, slope in zip(probs, slopes)]
    probs = [prob.astype(bf16) for prob in probs]
    for pair in range(group):
        back_a, back_b = backs[2 * pair : 2 * pair + 2]
        grad = jnp.where(
            left, dot_nn(back_a, key_s[pair, 0, own, :]), dot_nn(back_b, key_s[pair, 1, own, :])
        )
        if fresh:
            dq_s[pair] = grad
        else:
            dq_s[pair] += grad
        query_t, grad_t = turned[pair]
        for side in range(2):
            at = slice(side * HD, (side + 1) * HD)
            dk_s[pair, at, own] += dot_nn(query_t[at], backs[2 * pair + side])
            dv_s[pair, at, own] += dot_nn(grad_t[at], probs[2 * pair + side])


def back_operands(group, rows, q_ref, extra_ref, mixed_ref, grad_ref, left, half):
    queries, grads, turned = [], [], []
    for pair in range(group):
        at = (rows, lanes_of(pair))
        query = q_ref[at].astype(f32) * SCALE
        grad = grad_ref[at]
        queries.append(halves(query, extra_ref[at].astype(f32)))
        grads.append(grad_rows(mixed_ref[at], grad.astype(f32), left, half))
        turned.append((query.astype(bf16).T, grad.T))
    return queries, grads, turned


def cross_backward_kernel(
    group, seg_ref, frame_ref, q_ref, pooled_ref, key_w_ref, value_w_ref, extra_ref, mixed_ref,
    grad_ref, col_ref, dq_ref, dk_ref, dv_ref, key_s, value_s, dk_s, dv_s, dq_s,
):
    ones = ones_tags(BLOCK)
    put_halves(key_s, group, dot_nn(pooled_ref[...], key_w_ref[...]), ones)
    put_halves(value_s, group, dot_nn(pooled_ref[...], value_w_ref[...]), ones)
    dk_s[...] = jnp.zeros_like(dk_s)
    dv_s[...] = jnp.zeros_like(dv_s)
    left = lane_of(BLOCK) < HD
    half = lane_of(BLOCK) % HD
    for block in range(q_ref.shape[0] // BLOCK):
        rows = pl.ds(block * BLOCK, BLOCK)
        operands = back_operands(group, rows, q_ref, extra_ref, mixed_ref, grad_ref, left, half)
        dq_s[...] = jnp.zeros_like(dq_s)

        def one_clip(clip, carry, rows=rows, operands=operands):
            own = pl.ds(pl.multiple_of(frame_ref[clip] * KEYS, KEYS), KEYS)
            offset = jnp.where(col_ref[rows, :] == clip, 0.0, -FAR)
            back_step(group, own, *operands, key_s, value_s, dq_s, dk_s, dv_s, left, offset=offset)
            return carry

        lax.fori_loop(seg_ref[block * BLOCK], seg_ref[block * BLOCK + BLOCK - 1] + 1, one_clip, 0)
        for pair in range(group):
            dq_ref[rows, lanes_of(pair)] = (dq_s[pair] * SCALE).astype(bf16)
    for pair in range(group):
        dk_ref[lanes_of(pair), :] = dk_s[pair].astype(bf16)
        dv_ref[lanes_of(pair), :] = dv_s[pair].astype(bf16)


def cross_backward(segments, frames, queries, pooled, key_w, value_w, extra, mixed, grad):
    rows = queries.shape[0]
    keys = pooled.shape[0]
    group = BACKWARD_GROUP
    upright = pl.BlockSpec((PAIR * group, keys), lambda p, *_: (p, 0))
    own = pair_spec(rows, group)
    return pl.pallas_call(
        functools.partial(cross_backward_kernel, group),
        out_shape=(
            jax.ShapeDtypeStruct((rows, D), bf16),
            jax.ShapeDtypeStruct((D, keys), bf16),
            jax.ShapeDtypeStruct((D, keys), bf16),
        ),
        grid_spec=pltpu.PrefetchScalarGridSpec(
            num_scalar_prefetch=2,
            grid=(D // PAIR // group,),
            in_specs=[
                own,
                whole_spec(pooled.shape),
                pair_spec(key_w.shape[0], group),
                pair_spec(key_w.shape[0], group),
                own, own, own, whole_spec((rows, 1)),
            ],
            out_specs=[own, upright, upright],
            scratch_shapes=[pltpu.VMEM((group, 2, keys, PAIR), bf16)] * 2
            + [pltpu.VMEM((group, PAIR, keys), f32)] * 2
            + [pltpu.VMEM((group, BLOCK, PAIR), f32)],
        ),
        compiler_params=pltpu.CompilerParams(vmem_limit_bytes=VMEM_ASK),
        cost_estimate=pl.CostEstimate(
            flops=24_000_000_000, bytes_accessed=16_000_000, transcendentals=4_000_000
        ),
        name="cross_backward",
    )(segments, frames, queries, pooled, key_w, value_w, extra, mixed, grad, segments[:, None])


def self_backward_kernel(
    group, first_ref, q_ref, k_ref, v_ref, key_tag_ref, extra_ref, mixed_ref, grad_ref,
    dq_ref, dk_ref, dv_ref, key_s, value_s, dk_s, dv_s, dq_s,
):
    key_tag = key_tag_ref[...].astype(f32)
    put_halves(key_s, group, k_ref[...], key_tag)
    put_halves(value_s, group, v_ref[...], key_tag)
    dk_s[...] = jnp.zeros_like(dk_s)
    dv_s[...] = jnp.zeros_like(dv_s)
    left = lane_of(BLOCK) < HD
    half = lane_of(BLOCK) % HD
    row_at = lax.broadcasted_iota(jnp.int32, (BLOCK, BLOCK), 0)
    col_at = lax.broadcasted_iota(jnp.int32, (BLOCK, BLOCK), 1)
    for block in range(q_ref.shape[0] // BLOCK):
        rows = pl.ds(block * BLOCK, BLOCK)
        operands = back_operands(group, rows, q_ref, extra_ref, mixed_ref, grad_ref, left, half)
        back_step(
            group, rows, *operands, key_s, value_s, dq_s, dk_s, dv_s, left,
            masked=row_at >= col_at, fresh=True,
        )
        if block:

            def step(other, carry, operands=operands):
                own = pl.ds(pl.multiple_of(other * BLOCK, BLOCK), BLOCK)
                back_step(group, own, *operands, key_s, value_s, dq_s, dk_s, dv_s, left)
                return carry

            lax.fori_loop(first_ref[block], block, step, 0)
        for pair in range(group):
            dq_ref[rows, lanes_of(pair)] = (dq_s[pair] * SCALE).astype(bf16)
    for pair in range(group):
        dk_ref[:, lanes_of(pair)] = dk_s[pair].T.astype(bf16)
        dv_ref[:, lanes_of(pair)] = dv_s[pair].T.astype(bf16)


def self_backward(first_blocks, packed, key_tag, extra, mixed, grad):
    rows = packed.shape[0]
    group = BACKWARD_GROUP
    own = pair_spec(rows, group)
    return pl.pallas_call(
        functools.partial(self_backward_kernel, group),
        out_shape=(jax.ShapeDtypeStruct((rows, D), bf16),) * 3,
        grid_spec=pltpu.PrefetchScalarGridSpec(
            num_scalar_prefetch=1,
            grid=(D // PAIR // group,),
            in_specs=[
                packed_spec(rows, group, 0), packed_spec(rows, group, 1), packed_spec(rows, group, 2),
                whole_spec((rows, PAIR)),
                own, own, own,
            ],
            out_specs=[own] * 3,
            scratch_shapes=[pltpu.VMEM((group, 2, rows, PAIR), bf16)] * 2
            + [pltpu.VMEM((group, PAIR, rows), f32)] * 2
            + [pltpu.VMEM((group, BLOCK, PAIR), f32)],
        ),
        compiler_params=pltpu.CompilerParams(vmem_limit_bytes=VMEM_ASK),
        cost_estimate=pl.CostEstimate(
            flops=24_000_000_000, bytes_accessed=16_000_000, transcendentals=4_000_000
        ),
        name="self_backward",
    )(first_blocks, packed, packed, packed, key_tag, extra, mixed, grad)


def first_block_table(segment_row):
    clips = jnp.arange(CLIPS, dtype=jnp.int32)
    starts = jnp.sum((segment_row[:, None] < clips[None, :]).astype(jnp.int32), 0)
    heads = segment_row[::BLOCK]
    first = jnp.sum(jnp.where(heads[:, None] == clips[None, :], starts[None, :], 0), 1)
    return (first // BLOCK).astype(jnp.int32)


epsilon = 1e-05
ROOT = math.sqrt(2.0 / math.pi)
CUBE = 0.044715
C = 256
IMG = 64
POOL = 4


TILE = 256


def dot_tn(left, right):
    return lax.dot_general(left, right, (((0,), (0,)), ((), ())), preferred_element_type=f32)


def normalized(values):
    average = jnp.mean(values, -1, keepdims=True)
    centred = values - average
    spread = lax.rsqrt(jnp.mean(centred * centred, -1, keepdims=True) + epsilon)
    return centred * spread, spread


def norm_back(unit, spread, gain, grad):
    scaled = grad * gain
    mean_scaled = jnp.mean(scaled, -1, keepdims=True)
    mean_along = jnp.mean(scaled * unit, -1, keepdims=True)
    lead = tuple(range(grad.ndim - 1))
    return (
        (scaled - mean_scaled - unit * mean_along) * spread,
        jnp.sum(grad * unit, lead),
        jnp.sum(grad, lead),
    )


def gelu_and_slope(value):
    square = value * value
    bent = jnp.tanh(value * (ROOT + (ROOT * CUBE) * square))
    half = 0.5 + 0.5 * bent
    slope = half + value * (0.5 - 0.5 * bent * bent) * (ROOT + (3.0 * ROOT * CUBE) * square)
    return value * half, slope


def tiles_of(count):
    return [pl.ds(at, TILE) for at in range(0, count, TILE)]


def feed_forward_kernel(
    middle_ref, mixed_ref, join_ref, gain_ref, shift_ref, up_ref, bias_ref, down_ref, grad_ref,
    out_ref, second_ref, mixed_grad_ref, join_grad_ref, gain_grad_ref, shift_grad_ref,
    bias_grad_ref, chunk_ref,
    normed_s, grad_t_s, back_s, hidden_s, pre_grad_s, low_s, up_s, down_s, sems,
):
    step = pl.program_id(0)
    steps = pl.num_programs(0)
    rows = middle_ref.shape[0]
    shares, deep = chunk_ref.shape[0], chunk_ref.shape[1] // 2
    group, narrow = D // deep, D // shares

    @pl.when(step == 0)
    def _():
        for at in tiles_of(rows):
            total = middle_ref[at, :] + dot_nn(mixed_ref[at, :], join_ref[...])
            out_ref[at, :] = total
            second_ref[at, :] = total
            unit, _ = normalized(total)
            normed_s[at, :] = (unit * gain_ref[...] + shift_ref[...]).astype(bf16)
            back_s[at, :] = jnp.zeros((TILE, D), f32)
            grad_t_s[:, at] = grad_ref[at, :].T

    bias_grad = jnp.zeros((1, D), f32)
    for at in tiles_of(rows):
        hidden, slope = gelu_and_slope(dot_nn(normed_s[at, :], up_ref[...]) + bias_ref[...])
        hidden = hidden.astype(bf16)
        hidden_s[at, :] = hidden
        pre_grad = (dot_nt(grad_ref[at, :], down_ref[...]) * slope).astype(bf16)
        pre_grad_s[at, :] = pre_grad
        bias_grad += jnp.sum(pre_grad.astype(f32), 0, keepdims=True)
        out_ref[at, :] += dot_nn(hidden, down_ref[...])
        back_s[at, :] += dot_nt(pre_grad, up_ref[...])
    bias_grad_ref[...] = bias_grad
    up_s[step] = dot_tn(pre_grad_s[...], normed_s[...]).astype(bf16).reshape(group, deep, D)
    down_s[step] = dot_nn(grad_t_s[...], hidden_s[...]).astype(bf16).reshape(shares, narrow, D)

    def copies(at):
        return (
            pltpu.make_async_copy(
                up_s.at[at], chunk_ref.at[pl.ds(at * group, group), pl.ds(0, deep)], sems.at[0, at]
            ),
            pltpu.make_async_copy(
                down_s.at[at],
                chunk_ref.at[:, pl.ds(pl.multiple_of(deep + at * narrow, 16), narrow)],
                sems.at[1, at],
            ),
        )

    for copy in copies(step):
        copy.start()

    @pl.when(step == steps - 1)
    def _():
        gain_grad = jnp.zeros((1, D), f32)
        shift_grad = jnp.zeros((1, D), f32)
        for at in tiles_of(rows):
            unit, spread = normalized(second_ref[at, :])
            part, one, two = norm_back(unit, spread, gain_ref[...], back_s[at, :])
            gain_grad += one[None]
            shift_grad += two[None]
            total = grad_ref[at, :].astype(f32) + part
            second_ref[at, :] = total
            low = total.astype(bf16)
            low_s[at, :] = low
            mixed_grad_ref[at, :] = dot_nt(low, join_ref[...]).astype(bf16)
        gain_grad_ref[...] = gain_grad
        shift_grad_ref[...] = shift_grad
        join_grad_ref[...] = dot_tn(low_s[...], mixed_ref[...]).astype(bf16)
        for at in range(FF // D):
            for copy in copies(at):
                copy.wait()


FF = 3072


def still(shape):
    return pl.BlockSpec(shape, lambda *_: (0,) * len(shape), pipeline_mode=pl.Buffered(1))


def feed_forward(middle, mixed, join, gain, shift, up, bias, down, grad, shares):
    rows = middle.shape[0]
    steps = FF // D
    deep = FF // shares
    tall = still((rows, D))
    row = still((1, D))
    return pl.pallas_call(
        feed_forward_kernel,
        out_shape=(
            jax.ShapeDtypeStruct((rows, D), f32),
            jax.ShapeDtypeStruct((rows, D), f32),
            jax.ShapeDtypeStruct((rows, D), bf16),
            jax.ShapeDtypeStruct((D, D), bf16),
            jax.ShapeDtypeStruct((1, D), f32),
            jax.ShapeDtypeStruct((1, D), f32),
            jax.ShapeDtypeStruct((1, FF), f32),
            jax.ShapeDtypeStruct((shares, 2 * deep, D), bf16),
        ),
        grid_spec=pltpu.PrefetchScalarGridSpec(
            num_scalar_prefetch=0,
            grid=(steps,),
            in_specs=[
                tall, tall, still((D, D)), row, row,
                pl.BlockSpec((D, D), lambda j: (0, j)),
                pl.BlockSpec((1, D), lambda j: (0, j)),
                pl.BlockSpec((D, D), lambda j: (j, 0)),
                tall,
            ],
            out_specs=[
                tall, tall, tall, still((D, D)), row, row,
                pl.BlockSpec((1, D), lambda j: (0, j)),
                pl.BlockSpec(memory_space=pl.ANY),
            ],
            scratch_shapes=[
                pltpu.VMEM((rows, D), bf16),
                pltpu.VMEM((D, rows), bf16),
                pltpu.VMEM((rows, D), f32),
                pltpu.VMEM((rows, D), bf16),
                pltpu.VMEM((rows, D), bf16),
                pltpu.VMEM((rows, D), bf16),
                pltpu.VMEM((steps, D // deep, deep, D), bf16),
                pltpu.VMEM((steps, shares, D // shares, D), bf16),
                pltpu.SemaphoreType.DMA((2, steps)),
            ],
        ),
        compiler_params=pltpu.CompilerParams(vmem_limit_bytes=52 * 2**20),
        cost_estimate=pl.CostEstimate(
            flops=34_000_000_000, bytes_accessed=40_000_000, transcendentals=3_200_000
        ),
        name="feed_forward",
    )(middle, mixed, join, gain[None], shift[None], up, bias[None], down, grad)


def project_back_kernel(
    query_ref, key_ref, value_ref, project_ref, middle_ref, second_ref, gain_ref, shift_ref,
    join_ref, mixed_ref,
    middle_grad_ref, mixed_grad_ref, project_grad_ref, join_grad_ref, gain_grad_ref, shift_grad_ref,
    normed_s, low_s,
):
    rows = middle_ref.shape[0]
    gain_grad = jnp.zeros((1, D), f32)
    shift_grad = jnp.zeros((1, D), f32)
    for at in tiles_of(rows):
        back = dot_nt(query_ref[at, :], project_ref[:, 0:D])
        back += dot_nt(key_ref[at, :], project_ref[:, D : 2 * D])
        back += dot_nt(value_ref[at, :], project_ref[:, 2 * D : 3 * D])
        unit, spread = normalized(middle_ref[at, :])
        normed_s[at, :] = (unit * gain_ref[...] + shift_ref[...]).astype(bf16)
        part, one, two = norm_back(unit, spread, gain_ref[...], back)
        gain_grad += one[None]
        shift_grad += two[None]
        total = second_ref[at, :] + part
        middle_grad_ref[at, :] = total
        low = total.astype(bf16)
        low_s[at, :] = low
        mixed_grad_ref[at, :] = dot_nt(low, join_ref[...]).astype(bf16)
    gain_grad_ref[...] = gain_grad
    shift_grad_ref[...] = shift_grad
    project_grad_ref[0:D] = dot_tn(query_ref[...], normed_s[...]).astype(bf16)
    project_grad_ref[D : 2 * D] = dot_tn(key_ref[...], normed_s[...]).astype(bf16)
    project_grad_ref[2 * D : 3 * D] = dot_tn(value_ref[...], normed_s[...]).astype(bf16)
    join_grad_ref[...] = dot_tn(low_s[...], mixed_ref[...]).astype(bf16)


def project_back(query, key, value, project, middle, second, gain, shift, join, mixed):
    rows = middle.shape[0]
    return pl.pallas_call(
        project_back_kernel,
        out_shape=(
            jax.ShapeDtypeStruct((rows, D), f32),
            jax.ShapeDtypeStruct((rows, D), bf16),
            jax.ShapeDtypeStruct((3 * D, D), bf16),
            jax.ShapeDtypeStruct((D, D), bf16),
            jax.ShapeDtypeStruct((1, D), f32),
            jax.ShapeDtypeStruct((1, D), f32),
        ),
        in_specs=[pl.BlockSpec(memory_space=pltpu.VMEM)] * 10,
        out_specs=[pl.BlockSpec(memory_space=pltpu.VMEM)] * 6,
        scratch_shapes=[pltpu.VMEM((rows, D), bf16), pltpu.VMEM((rows, D), bf16)],
        compiler_params=pltpu.CompilerParams(vmem_limit_bytes=52 * 2**20),
        cost_estimate=pl.CostEstimate(
            flops=10_000_000_000, bytes_accessed=30_000_000, transcendentals=2_000
        ),
        name="project_back",
    )(query, key, value, project, middle, second, gain[None], shift[None], join, mixed)


def unpack_kernel(
    row, cross_at, filter_at, share_ref, summed_ref,
    up_ref, down_ref, project_ref, join_ref, cross_join_ref, query_ref, key_ref, value_ref, filter_ref,
):
    deep, model, own = FF // row, D // row, C // row
    up_ref[...] = summed_ref[0:deep, :].astype(f32).T
    for part in range(FF // D):
        at = deep + part * model
        down_ref[:, part * D : (part + 1) * D] = summed_ref[at : at + model, :].astype(f32)
    project_ref[...] = share_ref[0 : 3 * model, :].astype(f32)
    join_ref[...] = share_ref[3 * model : 4 * model, :].astype(f32)
    cross_join_ref[...] = share_ref[4 * model : 5 * model, :].astype(f32)
    query_ref[...] = share_ref[cross_at : cross_at + model, :].astype(f32)
    key_ref[...] = share_ref[cross_at + model : cross_at + 2 * model, 0:C].astype(f32)
    value_ref[...] = share_ref[cross_at + model : cross_at + 2 * model, C : 2 * C].astype(f32)
    for tap in range(9):
        at = filter_at + tap // 3 * own
        lanes = slice(tap % 3 * C, (tap % 3 + 1) * C)
        filter_ref[tap] = share_ref[at : at + own, lanes].astype(f32)


def unpack(share, summed, row, cross_at, filter_at):
    deep, model, own = FF // row, D // row, C // row
    shapes = [
        (D, deep), (model, FF), (3 * model, D), (model, D), (model, D), (model, D), (model, C),
        (model, C), (9, own, C),
    ]
    vmem = pl.BlockSpec(memory_space=pltpu.VMEM)
    return pl.pallas_call(
        functools.partial(unpack_kernel, row, cross_at, filter_at),
        out_shape=tuple(jax.ShapeDtypeStruct(shape, f32) for shape in shapes),
        in_specs=[vmem] * 2,
        out_specs=[vmem] * len(shapes),
        name="unpack",
    )(share, summed)


MESH = pl.DeviceIdType.MESH


def bits_of(count):
    return count.bit_length() - 1


def stream_steps(order, dp_bits, q_bits):
    dp_up = [("dp", b) for b in range(dp_bits)]
    dp_down = dp_up[::-1]
    q_steps = [("q", b) for b in range(q_bits)]
    return {"up": dp_up + q_steps, "down": dp_down + q_steps, "q_up": q_steps + dp_up}[order]


def cut_streams(rows, dp, orders):
    unit = 16 * dp
    units = rows // unit
    plan, at = [], 0
    for number, order in enumerate(orders):
        size = units // len(orders) + (number < units % len(orders))
        if size:
            plan.append((at * unit, size * unit, order))
            at += size
    return plan


def stream_scratch(plan, dp, row, partial):
    dp_bits, q_bits = bits_of(dp), bits_of(row // 2) if partial else 0
    shapes = []
    for _, rows, order in plan:
        lead = q_bits
        shapes.append(pltpu.VMEM((2,) * lead + (rows, D), bf16))
        if partial:
            shapes.append(pltpu.VMEM((2,) * lead + (rows, D), bf16))
        for kind, _ in stream_steps(order, dp_bits, q_bits):
            if kind == "dp":
                rows //= 2
            else:
                lead -= 1
            shapes.append(pltpu.VMEM((2,) * lead + (rows, D), bf16))
    return shapes


class Exchange:
    def __init__(self, dp, row, send_sem, recv_sem, local_sem):
        self.dp, self.row = dp, row
        self.dp_bits, self.q_bits = bits_of(dp), bits_of(row // 2)
        self.me_dp, self.me_row = lax.axis_index("dp"), lax.axis_index("row")
        self.core, self.me_q = lax.rem(self.me_row, 2), self.me_row // 2
        self.send_sem, self.recv_sem, self.local_sem = send_sem, recv_sem, local_sem
        self.remote, self.local, self.started = 0, 0, []

    def bit(self, step):
        kind, b = step
        return lax.rem((self.me_dp if kind == "dp" else self.me_q) // (2**b), 2)

    def partner(self, step):
        kind, b = step
        if kind == "core":
            return self.me_dp, self.me_row + 1 - 2 * self.core
        ahead = (2**b) * (1 - 2 * self.bit(step))
        if kind == "dp":
            return self.me_dp + ahead, self.me_row
        return self.me_dp, self.me_row + 2 * ahead

    def greet(self, devices):
        barrier = pltpu.get_barrier_semaphore()
        for device in devices:
            pl.semaphore_signal(barrier, inc=1, device_id=device, device_id_type=MESH)
        pl.semaphore_wait(barrier, len(devices))

    def push(self, src, dst, device):
        copy = pltpu.make_async_remote_copy(
            src_ref=src, dst_ref=dst, send_sem=self.send_sem.at[self.remote],
            recv_sem=self.recv_sem.at[self.remote], device_id=device, device_id_type=MESH,
        )
        self.remote += 1
        copy.start()
        self.started.append(copy)
        return copy

    def fetch(self, src, dst):
        copy = pltpu.make_async_copy(src, dst, self.local_sem.at[self.local])
        self.local += 1
        copy.start()
        return copy

    def end(self):
        for copy in self.started:
            copy.wait_send()


class Stream:
    def __init__(self, ex, scratch, rows, order, out_ref, out_at, partial):
        self.ex, self.rows, self.off = ex, rows, 0
        self.out_ref, self.out_at = out_ref, out_at
        q_bits = ex.q_bits if partial else 0
        self.q_bits = q_bits
        self.steps = stream_steps(order, ex.dp_bits, q_bits)
        self.todo = list(self.steps)
        self.back = [step for step in self.steps if step[0] == "dp"][::-1]
        self.acc = scratch.pop(0)
        self.landings = [scratch.pop(0) for _ in range(len(self.steps) + partial)]
        self.picked = [None] * q_bits
        self.copies, self.locals, self.landing = [], [], None
        self.gathering, self.done = False, False

    def start_partial(self, segments):
        ex, at = self.ex, 0
        every = (slice(None),) * self.q_bits
        self.landing = self.landings.pop(0)
        for piece, first, rows in segments:
            here = every + (pl.ds(at, rows),)
            there = (pl.ds(first, rows),)
            self.copies.append(
                ex.push(
                    piece.at[every + (1 - ex.core,) + there], self.landing.at[here],
                    ex.partner(("core", 0)),
                )
            )
            self.locals.append(ex.fetch(piece.at[every + (ex.core,) + there], self.acc.at[here]))
            at += rows

    def start_summed(self, source, first):
        self.ex.fetch(source.at[pl.ds(first, self.rows)], self.acc).wait()
        self.send_next()

    def index(self, off, rows):
        picks = tuple(slice(None) if p is None else p for p in self.picked)
        return picks + (pl.ds(pl.multiple_of(off, 16), rows),)

    def send_next(self):
        step = self.todo.pop(0)
        mine = self.ex.bit(step)
        landing = self.landings.pop(0)
        if step[0] == "dp":
            half = self.rows // 2
            src = self.acc.at[self.index(self.off + (1 - mine) * half, half)]
            self.off, self.rows = self.off + mine * half, half
        else:
            place = self.q_bits - 1 - step[1]
            self.picked[place] = 1 - mine
            src = self.acc.at[self.index(self.off, self.rows)]
            self.picked[place] = mine
        self.copies = [self.ex.push(src, landing, self.ex.partner(step))]
        self.landing = landing

    def add_landing(self):
        picks = self.index(0, 16)[:-1]
        lead = (slice(None),) * (len(self.landing.shape) - 2)

        def body(i, carry):
            own = picks + (pl.ds(pl.multiple_of(self.off + i * 16, 16), 16),)
            other = lead + (pl.ds(pl.multiple_of(i * 16, 16), 16),)
            self.acc[own] = (self.acc[own].astype(f32) + self.landing[other].astype(f32)).astype(bf16)
            return carry

        lax.fori_loop(0, self.rows // 16, body, 0)

    def gather_next(self):
        at = pl.ds(pl.multiple_of(self.out_at + self.off, 16), self.rows)
        step = self.back[0]
        self.copies = [self.ex.push(self.out_ref.at[at], self.out_ref.at[at], self.ex.partner(step))]

    def advance(self):
        for copy in self.locals:
            copy.wait()
        self.locals = []
        for copy in self.copies:
            copy.wait_recv()
        if self.gathering:
            step = self.back.pop(0)
            self.off = self.off - self.ex.bit(step) * self.rows
            self.rows *= 2
            if self.back:
                self.gather_next()
            else:
                self.done = True
            return
        self.add_landing()
        if self.todo:
            self.send_next()
            return
        at = pl.ds(pl.multiple_of(self.out_at + self.off, 16), self.rows)
        self.out_ref[at, :] = self.acc[self.index(self.off, self.rows)]
        self.gathering = True
        self.gather_next()


def drain(streams):
    while any(not stream.done for stream in streams):
        for stream in streams:
            if not stream.done:
                stream.advance()


def sum_shares_kernel(dp, row, plan, *refs):
    summed_ref, out_ref = refs[:2]
    scratch, (send_sem, recv_sem, local_sem) = list(refs[2:-3]), refs[-3:]
    ex = Exchange(dp, row, send_sem, recv_sem, local_sem)
    ex.greet([ex.partner(("dp", b)) for b in range(ex.dp_bits)])
    streams = []
    for first, rows, order in plan:
        stream = Stream(ex, scratch, rows, order, out_ref, first, 0)
        stream.start_summed(summed_ref, first)
        streams.append(stream)
    drain(streams)
    ex.end()


def sum_shares(summed, dp, row, orders):
    plan = cut_streams(summed.shape[0], dp, orders)
    copies = 2 * bits_of(dp) * len(plan)
    return pl.pallas_call(
        functools.partial(sum_shares_kernel, dp, row, plan),
        out_shape=jax.ShapeDtypeStruct(summed.shape, bf16),
        in_specs=[pl.BlockSpec(memory_space=pl.ANY)],
        out_specs=pl.BlockSpec(memory_space=pltpu.VMEM),
        scratch_shapes=stream_scratch(plan, dp, row, 0) + [
            pltpu.SemaphoreType.DMA((copies,)),
            pltpu.SemaphoreType.DMA((copies,)),
            pltpu.SemaphoreType.DMA((len(plan),)),
        ],
        compiler_params=pltpu.CompilerParams(
            collective_id=3, has_side_effects=True, vmem_limit_bytes=VMEM_ASK
        ),
        name="sum_shares",
    )(summed)


def row_of(lead, me_row):
    return lead + (me_row,)


def greet_row(row):
    me_dp, me_row = lax.axis_index("dp"), lax.axis_index("row")
    barrier = pltpu.get_barrier_semaphore()
    for ahead in range(1, row):
        pl.semaphore_signal(
            barrier, inc=1, device_id=(me_dp, lax.rem(me_row + ahead, row)), device_id_type=MESH
        )
    pl.semaphore_wait(barrier, row - 1)


def edge_copies(cells, above, below, send_sem, recv_sem, row):
    me_dp, me_row = lax.axis_index("dp"), lax.axis_index("row")
    here = cells.shape[1]
    onward = pltpu.make_async_remote_copy(
        src_ref=cells.at[:, here - 1], dst_ref=above, send_sem=send_sem.at[0],
        recv_sem=recv_sem.at[0], device_id=(me_dp, lax.rem(me_row + 1, row)), device_id_type=MESH,
    )
    back = pltpu.make_async_remote_copy(
        src_ref=cells.at[:, 0], dst_ref=below, send_sem=send_sem.at[1],
        recv_sem=recv_sem.at[1], device_id=(me_dp, lax.rem(me_row + row - 1, row)),
        device_id_type=MESH,
    )
    return onward, back


def start_edges(copies):
    for copy in copies:
        copy.start()


def end_edges(copies):
    for copy in copies:
        copy.wait_send()
        copy.wait_recv()


def put_wide(wide, frame, first, cells):
    column = lax.broadcasted_iota(jnp.int32, cells.shape, 0) % IMG
    cells = cells.astype(f32)
    count = cells.shape[0]
    left = jnp.where(column == 0, 0.0, pltpu.roll(cells, 1, 0))
    right = jnp.where(column == IMG - 1, 0.0, pltpu.roll(cells, count - 1, 0))
    at = pl.ds(first, count)
    wide[frame, at, 0:C] = left.astype(bf16)
    wide[frame, at, C : 2 * C] = cells.astype(bf16)
    wide[frame, at, 2 * C : 3 * C] = right.astype(bf16)


def put_edges(wide, above, below, here, row):
    me_row = lax.axis_index("row")
    keep_above = jnp.where(me_row > 0, 1.0, 0.0)
    keep_below = jnp.where(me_row < row - 1, 1.0, 0.0)
    for frame in range(wide.shape[0]):
        put_wide(wide, frame, 0, above[frame].astype(f32) * keep_above)
        put_wide(wide, frame, (here + 1) * IMG, below[frame].astype(f32) * keep_below)


def conv_forward_kernel(
    row, frames_ref, taps_ref, bias_ref, gain_ref, shift_ref,
    pre_ref, wide_ref, every_ref,
    above_s, below_s, pool_s, edge_send, edge_recv, send_sem, recv_sem,
):
    me_dp, me_row = lax.axis_index("dp"), lax.axis_index("row")
    core, me_q, places = lax.rem(me_row, 2), me_row // 2, row // 2
    count, here = frames_ref.shape[0], frames_ref.shape[1]
    greet_row(row)
    edges = edge_copies(frames_ref, above_s, below_s, edge_send, edge_recv, row)
    start_edges(edges)
    for frame in range(count):
        put_wide(wide_ref, frame, IMG, frames_ref[frame].reshape(here * IMG, C))
    end_edges(edges)
    put_edges(wide_ref, above_s, below_s, here, row)
    tile = POOL * IMG
    for frame in range(count):
        for part in range(here // POOL):
            first = part * tile
            pre = bias_ref[...] + dot_nn(wide_ref[frame, pl.ds(first, tile), :], taps_ref[0])
            pre += dot_nn(wide_ref[frame, pl.ds(first + IMG, tile), :], taps_ref[1])
            pre += dot_nn(wide_ref[frame, pl.ds(first + 2 * IMG, tile), :], taps_ref[2])
            pre_ref[frame, pl.ds(first, tile), :] = pre
            active, _ = gelu_and_slope(pre)
            unit, _ = normalized(active)
            normed = unit * gain_ref[...] + shift_ref[...]
            lines = normed.reshape(POOL, IMG, C)
            lines = lines[0] + lines[1] + lines[2] + lines[3]
            cells = IMG // POOL
            for side in range(C // PAIR):
                lanes = slice(side * PAIR, (side + 1) * PAIR)
                pool_s[side] = lines[:, lanes]
                total = pool_s[side, pl.ds(0, cells, stride=POOL), :]
                for at in range(1, POOL):
                    total += pool_s[side, pl.ds(at, cells, stride=POOL), :]
                every_ref[frame, me_row, pl.ds(part * cells, cells), lanes] = (
                    total * (1.0 / (POOL * POOL))
                ).astype(bf16)

    def push(source_row, to_row, at):
        copy = pltpu.make_async_remote_copy(
            src_ref=every_ref.at[:, source_row], dst_ref=every_ref.at[:, source_row],
            send_sem=send_sem.at[at], recv_sem=recv_sem.at[at], device_id=(me_dp, to_row),
            device_id_type=MESH,
        )
        copy.start()
        return copy

    other = me_row + 1 - 2 * core
    copies = [push(me_row, other, 0)]
    for ahead in range(1, places):
        copies.append(push(me_row, lax.rem(me_q + ahead, places) * 2 + core, ahead))
    for ahead in range(1, places):
        copies[ahead].wait_recv()
        came = lax.rem(me_q + places - ahead, places) * 2 + core
        copies.append(push(came, other, places - 1 + ahead))
    copies[0].wait_recv()
    for copy in copies[places:]:
        copy.wait_recv()
    for copy in copies:
        copy.wait_send()


def conv_forward(frames, taps, bias, gain, shift, row):
    count, here = frames.shape[0], frames.shape[1]
    keys = (here // POOL) * (IMG // POOL)
    return pl.pallas_call(
        functools.partial(conv_forward_kernel, row),
        out_shape=(
            jax.ShapeDtypeStruct((count, here * IMG, C), f32),
            jax.ShapeDtypeStruct((count, (here + 2) * IMG, 3 * C), bf16),
            jax.ShapeDtypeStruct((count, row, keys, C), bf16),
        ),
        in_specs=[pl.BlockSpec(memory_space=pltpu.VMEM)] * 5,
        out_specs=[pl.BlockSpec(memory_space=pltpu.VMEM)] * 3,
        scratch_shapes=[
            pltpu.VMEM((count, IMG, C), bf16),
            pltpu.VMEM((count, IMG, C), bf16),
            pltpu.VMEM((C // PAIR, IMG, PAIR), f32),
            pltpu.SemaphoreType.DMA((2,)),
            pltpu.SemaphoreType.DMA((2,)),
            pltpu.SemaphoreType.DMA((row,)),
            pltpu.SemaphoreType.DMA((row,)),
        ],
        compiler_params=pltpu.CompilerParams(
            collective_id=1, has_side_effects=True, vmem_limit_bytes=20 * 2**20
        ),
        name="conv_forward",
    )(frames, taps.reshape(3, 3 * C, C), bias[None], gain[None], shift[None])


READY_ORDERS = ("up", "down", "up", "down")
CROSS_ORDERS = ("q_up", "up", "down")
FILTER_ORDERS = ("q_up", "up")


def segments_of(pieces, first, rows):
    parts, at = [], 0
    for piece, start, count in pieces:
        low, high = max(first, at), min(first + rows, at + count)
        if low < high:
            parts.append((piece, start + low - at, high - low))
        at += count
    return parts


def finish_kernel(
    dp, row, plans,
    project_ref, join_ref, cross_join_ref, query_grad_ref, x_ref, query_w_ref, middle_grad_ref,
    keys_grad_ref, values_grad_ref, every_ref, key_w_ref, value_w_ref, pre_ref, wide_ref, taps_ref,
    gain_ref, small_ref,
    tokens_grad_ref, frames_grad_ref, share_ref,
    query_s, both_s, filter_s, x_s, query_w_s, pre_s, wide_in_s, taps_s, keys_grad_s, values_grad_s,
    part_s, landing_s, sum_s, arrive_s, spread_s, grad_s, grad_t_s, wide_s, above_s, below_s,
    edge_send, edge_recv, send_sem, recv_sem, local_sem, *scratch,
):
    scratch = list(scratch)
    ex = Exchange(dp, row, send_sem, recv_sem, local_sem)
    me_dp, me_row, core, me_q, places = ex.me_dp, ex.me_row, ex.core, ex.me_q, row // 2
    count, here = grad_s.shape[0], grad_s.shape[1]
    keys = part_s.shape[3]
    model, own = D // row, C // row
    ex.greet(
        [(me_dp, lax.rem(me_row + ahead, row)) for ahead in range(1, row)]
        + [ex.partner(("dp", b)) for b in range(ex.dp_bits)]
    )
    keys_in = ex.fetch(keys_grad_ref, keys_grad_s)
    values_in = ex.fetch(values_grad_ref, values_grad_s)
    base, groups = 0, []
    for plan in plans:
        groups.append([
            Stream(ex, scratch, rows, order, share_ref, base + first, 1) for first, rows, order in plan
        ])
        base += sum(rows for _, rows, _ in plan)
    ready, crossed, filtered = groups

    def start(group, plan, pieces):
        for stream, (first, rows, _) in zip(group, plan):
            stream.start_partial(segments_of(pieces, first, rows))

    used = 5 * model
    total_rows = sum(rows for _, rows, _ in plans[0])
    start(ready, plans[0], [
        (project_ref, 0, 3 * model), (join_ref, 0, model), (cross_join_ref, 0, model),
        (project_ref, 0, total_rows - used),
    ])
    x_in = ex.fetch(x_ref, x_s)
    query_in = ex.fetch(query_w_ref, query_w_s)
    pre_in = ex.fetch(pre_ref, pre_s)
    wide_in = ex.fetch(wide_ref, wide_in_s)
    taps_in = ex.fetch(taps_ref, taps_s)

    keys_in.wait()
    part = lax.dot_general(
        keys_grad_s[...], key_w_ref[...], (((0,), (1,)), ((), ())), preferred_element_type=f32
    )
    values_in.wait()
    part += lax.dot_general(
        values_grad_s[...], value_w_ref[...], (((0,), (1,)), ((), ())), preferred_element_type=f32
    )
    part_s[...] = part.astype(bf16).reshape(count, places, 2, keys, C)
    pooled_core = ex.push(part_s.at[:, :, 1 - core], landing_s, ex.partner(("core", 0)))

    split = (2,) * ex.q_bits + (2,)
    lines = both_s.shape[-2]
    for at, grad_ref in enumerate((keys_grad_s, values_grad_s)):
        both_s[..., 0:model, at * C : (at + 1) * C] = (
            dot_nn(grad_ref[...], every_ref[...]).astype(bf16).reshape(split + (model, C))
        )
    both_s[..., 0:model, 2 * C : 3 * C] = jnp.zeros(split + (model, C), bf16)
    if lines > model:
        both_s[..., model:lines, :] = jnp.zeros(split + (lines - model, D), bf16)
    x_in.wait()
    query_s[...] = dot_tn(query_grad_ref[...], x_s[...]).astype(bf16).reshape(split + (model, D))
    start(crossed, plans[1], [(query_s, 0, model), (both_s, 0, lines)])

    pooled_core.wait_recv()
    sum_s[...] = (part_s[:, :, core].astype(f32) + landing_s[...].astype(f32)).astype(bf16)
    pooled_in = []
    for ahead in range(1, places):
        to = lax.rem(me_q + ahead, places)
        pooled_in.append(ex.push(sum_s.at[:, to], arrive_s.at[ahead - 1], (me_dp, to * 2 + core)))
    for stream in ready:
        stream.advance()
    query_in.wait()
    for at in tiles_of(x_s.shape[0]):
        tokens_grad_ref[at, :] = middle_grad_ref[at, :] + dot_nt(query_grad_ref[at, :], query_w_s[...])
    for copy in pooled_in:
        copy.wait_recv()
    pooled = sum_s[:, me_q].astype(f32)
    for ahead in range(1, places):
        pooled += arrive_s[ahead - 1].astype(f32)
    pooled = pooled * (1.0 / (POOL * POOL))
    for stream in crossed:
        stream.advance()

    tile = POOL * IMG
    cells = IMG // POOL
    bias_grad = jnp.zeros((1, C), f32)
    gain_grad = jnp.zeros((1, C), f32)
    shift_grad = jnp.zeros((1, C), f32)
    pre_in.wait()
    for frame in range(count):
        for part in range(here // POOL):
            for side in range(C // PAIR):
                own_cells = pooled[
                    frame, part * cells : (part + 1) * cells, side * PAIR : (side + 1) * PAIR
                ]
                for at in range(POOL):
                    spread_s[side, pl.ds(at, cells, stride=POOL), :] = own_cells
            line = jnp.concatenate([spread_s[side] for side in range(C // PAIR)], 1)
            back = jnp.broadcast_to(line[None], (POOL, IMG, C)).reshape(tile, C)
            active, slope = gelu_and_slope(pre_s[frame, pl.ds(part * tile, tile), :])
            unit, spread = normalized(active)
            grad, one, two = norm_back(unit, spread, gain_ref[...], back)
            gain_grad += one[None]
            shift_grad += two[None]
            grad = (slope * grad).astype(bf16)
            bias_grad += jnp.sum(grad.astype(f32), 0, keepdims=True)
            grad_s[frame, pl.ds(part * POOL, POOL)] = grad.reshape(POOL, IMG, C)
    edges = edge_copies(grad_s, above_s, below_s, edge_send, edge_recv, row)
    start_edges(edges)
    for frame in range(count):
        cells_here = grad_s[frame].reshape(here * IMG, C)
        put_wide(wide_s, frame, IMG, cells_here)
        grad_t_s[frame] = cells_here.T
    for stream in ready[:3]:
        stream.advance()
    wide_in.wait()
    for dy in range(3):
        total = None
        for frame in range(count):
            piece = dot_nn(grad_t_s[frame], wide_in_s[frame, pl.ds(dy * IMG, here * IMG), :])
            total = piece if total is None else total + piece
        filter_s[..., dy * own : (dy + 1) * own, :] = total.astype(bf16).reshape(split + (own, D))
    lines = filter_s.shape[-2] - 3 * own
    line_at = lax.broadcasted_iota(jnp.int32, (lines, D), 0)
    extra = jnp.zeros((lines, D), f32)
    for at, item in enumerate((bias_grad, gain_grad, shift_grad)):
        item = jnp.concatenate([item, jnp.zeros((1, D - C), f32)], 1)
        extra = jnp.where(line_at == 8 + at, item, extra)
    for place in range(places):
        for side in range(2):
            index = tuple((place >> b) & 1 for b in reversed(range(ex.q_bits))) + (side,)
            own_small = small_ref[place * 2 + side].astype(f32)
            filter_s[index + (slice(3 * own, 3 * own + lines),)] = (own_small + extra).astype(bf16)
    start(filtered, plans[2], [(filter_s, 0, 3 * own + lines)])
    for stream in ready[3:] + crossed:
        stream.advance()
    end_edges(edges)
    put_edges(wide_s, above_s, below_s, here, row)
    taps_in.wait()
    for frame in range(count):
        for part in range(here // POOL):
            total = None
            for tap in range(9):
                dy, dx = tap // 3, tap % 3
                window = wide_s[frame, pl.ds(part * tile + dy * IMG, tile), dx * C : (dx + 1) * C]
                piece = dot_nt(window, taps_s[8 - tap])
                total = piece if total is None else total + piece
            frames_grad_ref[frame, pl.ds(part * tile, tile), :] = total
        if frame == 0:
            for stream in filtered:
                stream.advance()
        if frame == 1:
            for stream in ready:
                stream.advance()
    drain(filtered + ready + crossed)
    ex.end()


def finish(project_grad, join_grad, cross_join_grad, query_grad, x, query_w, middle_grad,
           keys_grad_t, values_grad_t, everyone, key_w, value_w, pre, wide, taps, gain, small, dp, row):
    unit = 16 * dp
    model, own = D // row, C // row
    count, here = pre.shape[0], pre.shape[1] // IMG
    keys = (here // POOL) * (IMG // POOL)
    whole_units = lambda rows: -(-rows // unit) * unit
    rows = [whole_units(5 * model), whole_units(2 * model), 3 * own + small.shape[1]]
    plans = [
        cut_streams(count_rows, dp, orders)
        for count_rows, orders in zip(rows, (READY_ORDERS, CROSS_ORDERS, FILTER_ORDERS))
    ]
    split = (2,) * bits_of(row // 2) + (2,)
    view = lambda piece: piece.reshape(split + (piece.shape[0] // row, D))
    streams = [stream for plan in plans for stream in plan]
    per_stream = 2 * bits_of(dp) + bits_of(row // 2)
    remote = per_stream * len(streams) + 8 * len(streams) + row
    local = 8 * len(streams) + 8
    vmem = pl.BlockSpec(memory_space=pltpu.VMEM)
    away = pl.BlockSpec(memory_space=pl.ANY)
    return pl.pallas_call(
        functools.partial(finish_kernel, dp, row, plans),
        out_shape=(
            jax.ShapeDtypeStruct(x.shape, f32),
            jax.ShapeDtypeStruct(pre.shape, f32),
            jax.ShapeDtypeStruct((sum(rows), D), bf16),
        ),
        in_specs=[
            away, away, away, vmem, away, away, vmem, away, away, vmem, vmem, vmem, away, away, away,
            vmem, vmem,
        ],
        out_specs=[vmem] * 3,
        scratch_shapes=[
            pltpu.VMEM(split + (model, D), bf16),
            pltpu.VMEM(split + (rows[1] - model, D), bf16),
            pltpu.VMEM(split + (rows[2], D), bf16),
            pltpu.VMEM(x.shape, bf16),
            pltpu.VMEM(query_w.shape, bf16),
            pltpu.VMEM(pre.shape, f32),
            pltpu.VMEM(wide.shape, bf16),
            pltpu.VMEM(taps.shape, bf16),
            pltpu.VMEM(keys_grad_t.shape, bf16),
            pltpu.VMEM(values_grad_t.shape, bf16),
            pltpu.VMEM((count, row // 2, 2, keys, C), bf16),
            pltpu.VMEM((count, row // 2, keys, C), bf16),
            pltpu.VMEM((count, row // 2, keys, C), bf16),
            pltpu.VMEM((row // 2 - 1, count, keys, C), bf16),
            pltpu.VMEM((C // PAIR, IMG, PAIR), f32),
            pltpu.VMEM((count, here, IMG, C), bf16),
            pltpu.VMEM((count, C, here * IMG), bf16),
            pltpu.VMEM((count, (here + 2) * IMG, 3 * C), bf16),
            pltpu.VMEM((count, IMG, C), bf16),
            pltpu.VMEM((count, IMG, C), bf16),
            pltpu.SemaphoreType.DMA((2,)),
            pltpu.SemaphoreType.DMA((2,)),
            pltpu.SemaphoreType.DMA((remote,)),
            pltpu.SemaphoreType.DMA((remote,)),
            pltpu.SemaphoreType.DMA((local,)),
        ] + [shape for plan in plans for shape in stream_scratch(plan, dp, row, 1)],
        compiler_params=pltpu.CompilerParams(
            collective_id=2, has_side_effects=True, vmem_limit_bytes=54 * 2**20
        ),
        name="finish",
    )(
        view(project_grad), view(join_grad), view(cross_join_grad), query_grad, x, query_w,
        middle_grad, keys_grad_t, values_grad_t, everyone, key_w, value_w, pre, wide, taps,
        gain[None], small,
    )


def fast_dot(left, right):
    return jnp.dot(left, right, preferred_element_type=f32)


def shared_rows(matrix, count):
    return matrix.reshape(count, matrix.shape[0] // count, matrix.shape[1])


def on_device(
    frames, tokens, segment_ids, clip_frame, filter_weight, filter_bias, context_gain,
    context_shift, cross_query, cross_key, cross_value, cross_output, first_gain, first_shift,
    self_project, self_output, second_gain, second_shift, up_weight, up_bias, down_weight, cotangent,
):
    shares = lax.axis_size("row")
    x = tokens[0]
    segments = segment_ids[0]
    clip_frames = clip_frame[0]
    out_grad = cotangent[0]
    tags = segment_tags(segments)
    key_tag = key_tags(segments)
    first_blocks = first_block_table(segments)

    pre_act, wide, everyone = conv_forward(
        frames, filter_weight, filter_bias, context_gain, context_shift, shares
    )
    everyone = everyone.reshape(-1, C)
    cross_q = fast_dot(x, cross_query).astype(bf16)
    cross_mixed, cross_extra = cross_forward(
        segments, clip_frames, cross_q, everyone, cross_key, cross_value
    )
    middle = x.astype(f32) + fast_dot(cross_mixed, cross_output)
    first_unit, first_spread = normalized(middle)
    first_normed = (first_unit * first_gain + first_shift).astype(bf16)
    packed = fast_dot(first_normed, self_project).astype(bf16)
    self_mixed, self_extra = self_forward(first_blocks, packed, tags, key_tag)
    (
        output, second_grad, self_mixed_grad, join_grad, second_gain_grad,
        second_shift_grad, up_bias_grad, chunk_a,
    ) = feed_forward(
        middle, self_mixed, self_output, second_gain, second_shift, up_weight, up_bias, down_weight,
        out_grad, shares,
    )
    share_a = lax.psum_scatter(chunk_a, "row", scatter_dimension=0, tiled=False)
    query_grad, key_grad, value_grad = self_backward(
        first_blocks, packed, key_tag, self_extra, self_mixed, self_mixed_grad
    )
    (
        middle_grad, cross_mixed_grad, project_grad, cross_join_grad, first_gain_grad,
        first_shift_grad,
    ) = project_back(
        query_grad, key_grad, value_grad, self_project, middle, second_grad, first_gain, first_shift,
        cross_output, cross_mixed,
    )
    cross_q_grad, keys_grad_t, values_grad_t = cross_backward(
        segments, clip_frames, cross_q, everyone, cross_key, cross_value, cross_extra, cross_mixed,
        cross_mixed_grad,
    )
    dp = lax.axis_size("dp")
    small = jnp.concatenate(
        [
            item.astype(bf16).reshape(shares, -1)
            for item in (
                first_gain_grad, first_shift_grad, second_gain_grad, second_shift_grad, up_bias_grad,
            )
        ],
        1,
    )
    lines = 16 + -(3 * C // shares + 16) % (16 * dp)
    small = jnp.pad(small, ((0, 0), (0, lines * D - small.shape[1]))).reshape(shares, lines, D)
    tokens_grad, frames_grad, reduced = finish(
        project_grad, join_grad, cross_join_grad, cross_q_grad, x, cross_query, middle_grad,
        keys_grad_t, values_grad_t, everyone, cross_key, cross_value, pre_act, wide, filter_weight,
        context_gain, small, dp, shares,
    )
    share_a = sum_shares(share_a, dp, shares, ("up", "down"))
    own_part = C // shares
    filter_at = reduced.shape[0] - (3 * own_part + lines)
    cross_at = filter_at - -(-2 * D // shares // (16 * dp)) * 16 * dp
    (
        up_grad, down_grad, project_grad, self_output_grad, cross_output_grad, cross_query_grad,
        cross_key_grad, cross_value_grad, filter_grad,
    ) = unpack(reduced, share_a, shares, cross_at, filter_at)
    late = reduced[filter_at + 3 * own_part :].astype(f32)
    flat = late[:2].reshape(-1)
    sizes = [D // shares] * 4 + [3072 // shares]
    ends = [sum(sizes[: i + 1]) for i in range(len(sizes))]
    vectors = [flat[e - s : e] for e, s in zip(ends, sizes)]
    mine = lax.dynamic_slice_in_dim(late[8:11, :C], lax.axis_index("row") * own_part, own_part, 1)
    vectors = vectors + [mine[0], mine[1], mine[2]]
    return (
        middle[None],
        output[None],
        tokens_grad[None],
        frames_grad.reshape(frames.shape),
        jnp.transpose(filter_grad, (0, 2, 1)),
        vectors[5],
        vectors[6],
        vectors[7],
        cross_query_grad.T,
        cross_key_grad.T,
        cross_value_grad.T,
        cross_output_grad.T,
        vectors[0],
        vectors[1],
        project_grad.T,
        self_output_grad.T,
        vectors[2],
        vectors[3],
        up_grad,
        vectors[4],
        down_grad.T,
    )


def solution(mesh):
    whole = P()
    by_row = P(("dp", "row"), None, None)
    in_specs = (
        P("dp", "row", None, None),
        by_row,
        P(("dp", "row"), None),
        P(("dp", "row"), None),
    ) + (whole,) * 17 + (by_row,)
    columns = P(None, "row")
    vector = P("row")
    out_specs = (
        by_row, by_row, by_row, P("dp", "row", None, None), P(None, None, "row"), vector, vector,
        vector, columns, columns, columns, columns, vector, vector, columns, columns, vector, vector,
        columns, vector, columns,
    )
    return jax.shard_map(
        on_device, mesh=mesh, in_specs=in_specs, out_specs=out_specs, check_vma=False
    )
```
